32 devices in a mesh: dp: 8 (over z, y), cp: 4 (over x, core).
Axes of the slice: x: 2, y: 2, z: 4, core: 2. Of those that a mesh axis runs over, the one named last changes fastest.
Arguments:
- inputs: bfloat16 [16, 1024, 1024], P('dp', 'cp'), may hold values from -6 to 6
- cotangent: bfloat16 [16, 1024, 1024], P('dp', 'cp'), may hold values from -6 to 6
- lengths: int32 [16], P('dp'), may hold values from 256 to 1024, as said below
- bucket_ids: int32 [2047], replicated, may hold values from 0 to 31
- attn_gain_one: bfloat16 [1024], P(('dp', 'cp')), may hold values from 0.5 to 1.5
- query_one: bfloat16 [1024, 1024], P(('dp', 'cp')), may hold values from -0.0234375 to 0.0234375
- key_one: bfloat16 [1024, 1024], P(('dp', 'cp')), may hold values from -0.1875 to 0.1875
- value_one: bfloat16 [1024, 1024], P(('dp', 'cp')), may hold values from -0.1875 to 0.1875
- output_one: bfloat16 [1024, 1024], P(('dp', 'cp')), may hold values from -1 to 1
- mlp_gain_one: bfloat16 [1024], P(('dp', 'cp')), may hold values from 0.5 to 1.5
- inner_one: bfloat16 [1024, 4096], P(('dp', 'cp')), may hold values from -0.1875 to 0.1875
- outer_one: bfloat16 [4096, 1024], P(('dp', 'cp')), may hold values from -0.09375 to 0.09375
- bias_table: bfloat16 [512], P(('dp', 'cp')), may hold values from -4 to 4
- attn_gain_two: bfloat16 [1024], P(('dp', 'cp')), may hold values from 0.5 to 1.5
- query_two: bfloat16 [1024, 1024], P(('dp', 'cp')), may hold values from -0.0234375 to 0.0234375
- key_two: bfloat16 [1024, 1024], P(('dp', 'cp')), may hold values from -0.1875 to 0.1875
- value_two: bfloat16 [1024, 1024], P(('dp', 'cp')), may hold values from -0.1875 to 0.1875
- output_two: bfloat16 [1024, 1024], P(('dp', 'cp')), may hold values from -1 to 1
- mlp_gain_two: bfloat16 [1024], P(('dp', 'cp')), may hold values from 0.5 to 1.5
- inner_two: bfloat16 [1024, 4096], P(('dp', 'cp')), may hold values from -0.1875 to 0.1875
- outer_two: bfloat16 [4096, 1024], P(('dp', 'cp')), may hold values from -0.09375 to 0.09375
Outputs:
- output: bfloat16 [16, 1024, 1024], P('dp', 'cp')
- input_grad: bfloat16 [16, 1024, 1024], P('dp', 'cp')
- grad_attn_gain_one: float32 [1024], P(('dp', 'cp'))
- grad_query_one: float32 [1024, 1024], P(('dp', 'cp'))
- grad_key_one: float32 [1024, 1024], P(('dp', 'cp'))
- grad_value_one: float32 [1024, 1024], P(('dp', 'cp'))
- grad_output_one: float32 [1024, 1024], P(('dp', 'cp'))
- grad_mlp_gain_one: float32 [1024], P(('dp', 'cp'))
- grad_inner_one: float32 [1024, 4096], P(('dp', 'cp'))
- grad_outer_one: float32 [4096, 1024], P(('dp', 'cp'))
- grad_bias_table: float32 [512], P(('dp', 'cp'))
- grad_attn_gain_two: float32 [1024], P(('dp', 'cp'))
- grad_query_two: float32 [1024, 1024], P(('dp', 'cp'))
- grad_key_two: float32 [1024, 1024], P(('dp', 'cp'))
- grad_value_two: float32 [1024, 1024], P(('dp', 'cp'))
- grad_output_two: float32 [1024, 1024], P(('dp', 'cp'))
- grad_mlp_gain_two: float32 [1024], P(('dp', 'cp'))
- grad_inner_two: float32 [1024, 4096], P(('dp', 'cp'))
- grad_outer_two: float32 [4096, 1024], P(('dp', 'cp'))
The draws below stay inside these ranges and needn't reach their ends.
Inputs may be any that keep to these rules, and one draw needn't show every extreme that they name: `lengths`: positions at or past a sequence's length are padding; some sequence has length 1024 and some has length 256 in every draw.
All inputs are finite; a program needn't handle non-finite values.
Results may differ from the reference program's by a relative error of at most 0.023.
Values may be sent and summed in bfloat16 or wider, within the bound.
No kernel may reach another device: no remote copies, remote signals or barrier semaphores. Data moves between devices by JAX's collectives and lax.ppermute only.
A program may use at most 384 MiB of HBM per device.

```python
import jax
import jax.numpy as jnp
from jax import lax

D = 1024
HEAD_COUNT = 16
DK = 64
FF = 4096
BUCKET_COUNT = 32
L = 1024
SEQS = 16


def draw_lengths(key, part):
    key_base, key_long = jax.random.split(jax.random.fold_in(key, 7), 2)
    lengths_drawn = jax.random.randint(key_base, (SEQS,), L // 4, L + 1, dtype=jnp.int32)
    longest = jax.random.randint(key_long, (), 0, SEQS, dtype=jnp.int32)
    places = jnp.arange(SEQS, dtype=jnp.int32)
    lengths_drawn = jnp.where(places == longest, L, lengths_drawn)
    shortest = (longest + 1) % SEQS
    return jnp.where(places == shortest, L // 4, lengths_drawn).astype(jnp.int32)


def place_ends(entries, own_key, smallest, top_value):
    extent = entries.shape
    spot = [jax.random.randint(jax.random.fold_in(own_key, axis), (), 0, extent[axis]) for axis in range(len(extent))]
    entries = entries.at[tuple(spot)].set(smallest)
    longest = extent.index(max(extent))
    spot[longest] = (spot[longest] + 1) % extent[longest]
    return entries.at[tuple(spot)].set(top_value)


def with_spikes(entries, key, source, target, blocks, factor):
    owner, partner = [(jnp.arange(entries.shape[axis_at]) // (entries.shape[axis_at] // blocks)).reshape([-1 if axis == axis_at else 1 for axis in range(entries.ndim)]) for axis_at in (source, target)]
    chosen = jax.random.permutation(key, blocks)[partner]
    strong = (owner == chosen) | (owner == (partner + blocks // 2) % blocks)
    return jnp.where(strong, factor * entries, entries)


def steps_of(key, dims, shards, low, top_value):
    factor_of, own = 1.0, jax.random.fold_in(key, 6)
    for position, parts in shards:
        heights = jnp.exp(jax.random.uniform(jax.random.fold_in(own, position), (parts,), jnp.float32, low / len(shards), top_value / len(shards)))
        factor_of = factor_of * jnp.repeat(heights, dims[position] // parts).reshape([-1 if axis == position else 1 for axis in range(len(dims))])
    return factor_of


def noise(rng, extent, deviation, most, pieces=(), kind=jnp.bfloat16):
    drawn = deviation * jax.random.normal(rng, extent, jnp.float32)
    if pieces:
        drawn = drawn * steps_of(rng, extent, pieces, -0.22, 0.18)
    return jnp.clip(drawn, -most, most).astype(kind)


def gaussian_with(own_key, dims, spread, limit, shards, heavy, kind=jnp.bfloat16):
    values = spread * jax.random.normal(own_key, dims, jnp.float32)
    if shards:
        values = values * steps_of(own_key, dims, shards, -0.22, 0.18)
    return jnp.clip(with_spikes(values, jax.random.fold_in(own_key, 3), *heavy), -limit, limit).astype(kind)


def setup_inputs(seed: int = 0) -> dict:
    splits = jax.random.split(jax.random.key(seed), 22)
    inputs = gaussian_with(splits[0], (SEQS, L, D), 1.0, 6.0, ((0, 8), (1, 4)), (0, 2, 8, 2.0))
    cotangent = noise(splits[1], (SEQS, L, D), 1.0, 6.0, ((0, 8), (1, 4)))
    lengths = draw_lengths(jax.random.fold_in(splits[21], 71), 0)
    bucket_ids = place_ends(jax.random.randint(splits[3], (2 * L - 1,), 0, BUCKET_COUNT), jax.random.fold_in(splits[3], 1), 0, BUCKET_COUNT - 1).astype(jnp.int32)
    attn_gain_one = jnp.clip(1.0 + 0.1 * jax.random.normal(splits[4], (D,), jnp.float32), 0.5, 1.5).astype(jnp.bfloat16)
    query_one = noise(splits[5], (D, D), (D * DK) ** -0.5, 0.0234375, ((0, 32),))
    key_one = noise(splits[6], (D, D), D ** -0.5, 0.1875, ((0, 32),))
    value_one = noise(splits[7], (D, D), D ** -0.5, 0.1875, ((0, 32),))
    output_one = noise(splits[8], (D, D), (D // 32) ** -0.5, 1.0, ((0, 32),))
    mlp_gain_one = jnp.clip(1.0 + 0.1 * jax.random.normal(splits[9], (D,), jnp.float32), 0.5, 1.5).astype(jnp.bfloat16)
    inner_one = noise(splits[10], (D, FF), D ** -0.5, 0.1875, ((0, 32),))
    outer_one = noise(splits[11], (FF, D), FF ** -0.5, 0.09375, ((0, 32),))
    bias_table = noise(splits[12], (HEAD_COUNT * BUCKET_COUNT,), 1.0, 4.0, ((0, 32),))
    attn_gain_two = jnp.clip(1.0 + 0.1 * jax.random.normal(splits[13], (D,), jnp.float32), 0.5, 1.5).astype(jnp.bfloat16)
    query_two = noise(splits[14], (D, D), (D * DK) ** -0.5, 0.0234375, ((0, 32),))
    key_two = noise(splits[15], (D, D), D ** -0.5, 0.1875, ((0, 32),))
    value_two = noise(splits[16], (D, D), D ** -0.5, 0.1875, ((0, 32),))
    output_two = noise(splits[17], (D, D), (D // 32) ** -0.5, 1.0, ((0, 32),))
    mlp_gain_two = jnp.clip(1.0 + 0.1 * jax.random.normal(splits[18], (D,), jnp.float32), 0.5, 1.5).astype(jnp.bfloat16)
    inner_two = noise(splits[19], (D, FF), D ** -0.5, 0.1875, ((0, 32),))
    outer_two = noise(splits[20], (FF, D), FF ** -0.5, 0.09375, ((0, 32),))
    return dict(inputs=inputs, cotangent=cotangent, lengths=lengths, bucket_ids=bucket_ids, attn_gain_one=attn_gain_one, query_one=query_one, key_one=key_one, value_one=value_one, output_one=output_one, mlp_gain_one=mlp_gain_one, inner_one=inner_one, outer_one=outer_one, bias_table=bias_table, attn_gain_two=attn_gain_two, query_two=query_two, key_two=key_two, value_two=value_two, output_two=output_two, mlp_gain_two=mlp_gain_two, inner_two=inner_two, outer_two=outer_two)


@jax.custom_vjp
def low(v):
    return lax.optimization_barrier(v.astype(jnp.bfloat16)).astype(jnp.float32)

@jax.custom_vjp
def low_back(v):
    return v

def low_keep(v):
    return (low(v), None)

def low_pass(kept, grad):
    return (grad,)

def back_keep(v):
    return (v, None)

def back_low(kept, grad):
    return (low(grad),)
low.defvjp(low_keep, low_pass)
low_back.defvjp(back_keep, back_low)
EPS = 1e-06
HIGH_PRECISION = lax.Precision.HIGHEST
NEGATIVE = -1e+30

def rms_norm(values, norm_gain):
    return values * lax.rsqrt(lax.optimization_barrier(jnp.mean(values * values, axis=-1, keepdims=True)) + EPS) * norm_gain

def project(left, right):
    return jnp.matmul(left, right, precision=HIGH_PRECISION)

def encoder_layer(hidden_in, key_valid, relative_bias, params):
    attn_gain, w_query, w_key, w_value, w_output, mlp_gain, w_inner, w_outer = params
    seq_count = hidden_in.shape[0]
    normed = low(rms_norm(hidden_in, attn_gain))
    queries = low(low_back(project(normed, w_query))).reshape(seq_count, L, HEAD_COUNT, DK)
    key_heads = low(low_back(project(normed, w_key))).reshape(seq_count, L, HEAD_COUNT, DK)
    value_heads = low(low_back(project(normed, w_value))).reshape(seq_count, L, HEAD_COUNT, DK)
    scores = jnp.einsum('bqhd,bkhd->bhqk', queries, key_heads, precision=HIGH_PRECISION) + relative_bias[None]
    scores = low_back(scores)
    scores = jnp.where(key_valid[:, None, None, :], scores, NEGATIVE)
    top_score = lax.optimization_barrier(jnp.max(scores, axis=-1, keepdims=True))
    exp_scores = jnp.exp(scores - top_score)
    probabilities = low(exp_scores / lax.optimization_barrier(jnp.sum(exp_scores, axis=-1, keepdims=True)))
    context = jnp.einsum('bhqk,bkhd->bqhd', probabilities, value_heads, precision=HIGH_PRECISION).reshape(seq_count, L, D)
    context = low(low_back(context))
    attended = hidden_in + low_back(project(context, w_output))
    normed_mlp = low(rms_norm(attended, mlp_gain))
    hidden = low(jax.nn.gelu(low_back(project(normed_mlp, w_inner)), approximate=True))
    return attended + low_back(project(hidden, w_outer))

def reference(inputs, cotangent, lengths, bucket_ids, attn_gain_one, query_one, key_one, value_one, output_one, mlp_gain_one, inner_one, outer_one, bias_table, attn_gain_two, query_two, key_two, value_two, output_two, mlp_gain_two, inner_two, outer_two):
    weights = tuple((weight_arg.astype(jnp.float32) for weight_arg in (attn_gain_one, query_one, key_one, value_one, output_one, mlp_gain_one, inner_one, outer_one, bias_table, attn_gain_two, query_two, key_two, value_two, output_two, mlp_gain_two, inner_two, outer_two)))
    positions = jnp.arange(L, dtype=jnp.int32)
    offsets = (positions[None, :] - positions[:, None] + (L - 1)).astype(jnp.int32)
    bucket_grid = bucket_ids[offsets]
    group_size = 2
    groups = SEQS // group_size
    inputs_grouped = inputs.astype(jnp.float32).reshape(groups, group_size, L, D)
    cot_grouped = cotangent.astype(jnp.float32).reshape(groups, group_size, L, D)
    lengths_grouped = lengths.reshape(groups, group_size)

    def one_group(grad_totals, group_batch):
        inputs_part, cot_part, lengths_part = group_batch
        key_valid = positions[None, :] < lengths_part[:, None]
        row_valid = key_valid.astype(jnp.float32)[:, :, None]

        def forward(inputs_now, params):
            bucket_table = params[8].reshape(HEAD_COUNT, BUCKET_COUNT)
            relative_bias = bucket_table[:, bucket_grid]
            middle = encoder_layer(inputs_now, key_valid, relative_bias, params[0:8])
            final_state = encoder_layer(middle, key_valid, relative_bias, params[9:17])
            return final_state * row_valid
        result, pullback = jax.vjp(forward, inputs_part, weights)
        grad_inputs, grad_params = pullback(cot_part)
        grad_totals = tuple((grad_total + grad_part for grad_total, grad_part in zip(grad_totals, grad_params)))
        return (grad_totals, (result.astype(jnp.bfloat16), grad_inputs.astype(jnp.bfloat16)))
    zeros_init = tuple((jnp.zeros_like(weight_arg) for weight_arg in weights))
    grad_totals, (outputs, input_grads) = lax.scan(one_group, zeros_init, (inputs_grouped, cot_grouped, lengths_grouped))
    return (outputs.reshape(SEQS, L, D), input_grads.reshape(SEQS, L, D), grad_totals[0], grad_totals[1], grad_totals[2], grad_totals[3], grad_totals[4], grad_totals[5], grad_totals[6], grad_totals[7], grad_totals[8], grad_totals[9], grad_totals[10], grad_totals[11], grad_totals[12], grad_totals[13], grad_totals[14], grad_totals[15], grad_totals[16])
```

```python
import functools

import jax
import jax.numpy as jnp
import numpy as np
from jax import lax
from jax.experimental import pallas as pl
from jax.experimental.pallas import tpu as pltpu
from jax.sharding import Mesh
from jax.sharding import PartitionSpec as P

DK = 64
TILE = 128
EPS = 1e-06
NEGATIVE = -1e30
HIGH_PRECISION = lax.Precision.HIGHEST


def toeplitz_kernel(span, u_ref, t_ref):
    for e in range(span):
        base = TILE * (span - 1 - e)
        w = jnp.broadcast_to(u_ref[0, :, base:base + 2 * TILE], (TILE, 2 * TILE))
        t_ref[0, e] = pltpu.roll(w, TILE, 1, stride=1, stride_axis=0)[:, :TILE].astype(t_ref.dtype)

def toeplitz_tiles(u):
    heads, width = u.shape
    span = width // TILE - 1
    return pl.pallas_call(
        functools.partial(toeplitz_kernel, span),
        grid=(heads,),
        in_specs=[pl.BlockSpec((1, 1, width), lambda h: (h, 0, 0))],
        out_specs=pl.BlockSpec((1, span, TILE, TILE), lambda h: (h, 0, 0, 0)),
        out_shape=jax.ShapeDtypeStruct((heads, span, TILE, TILE), jnp.bfloat16),
        cost_estimate=pl.CostEstimate(flops=heads * span * TILE * TILE * 4, bytes_accessed=heads * span * TILE * TILE * 2, transcendentals=0),
        name="toeplitz",
    )(u.reshape(heads, 1, width))

def head_lanes(h, x):
    lane = lax.broadcasted_iota(jnp.int32, x.shape, 1)
    return jnp.where((lane // DK) == h, x, jnp.zeros_like(x))

def dot_nt(a, b):
    return lax.dot_general(a, b, (((1,), (1,)), ((), ())), preferred_element_type=jnp.float32)

def dot_tn(a, b):
    return lax.dot_general(a, b, (((0,), (0,)), ((), ())), preferred_element_type=jnp.float32)

def dot_nn(a, b):
    return lax.dot_general(a, b, (((1,), (0,)), ((), ())), preferred_element_type=jnp.float32)

def key_chunks(parts, rows, chunk):
    return [(i, s) for i in range(parts) for s in range(0, rows, chunk)]

def chunk_scores(pos_ref, k_chunk, q_head, bias_ref, h, c, chunk, blk, q_rows):
    n = chunk // blk
    sub = blk // TILE
    nq = q_rows // blk
    s = dot_nt(k_chunk, q_head)
    half = bias_ref.shape[1] // 2
    rows = []
    for kb in range(n):
        kpos = pos_ref[1 + nq + c * n + kb]
        for kk in range(sub):
            cols = []
            for qb in range(nq):
                e0 = (kpos - pos_ref[1 + qb]) + half + kk
                for qq in range(sub):
                    cols.append(bias_ref[h, e0 - qq])
            rows.append(jnp.concatenate(cols, axis=1))
    bias = jnp.concatenate(rows, axis=0).astype(jnp.float32)
    s = s + bias
    valid = []
    for kb in range(n):
        limit = pos_ref[0] - pos_ref[1 + nq + c * n + kb] * TILE
        valid.append(lax.broadcasted_iota(jnp.int32, (blk, 1), 0) < limit)
    ok = valid[0] if n == 1 else jnp.concatenate([v.astype(jnp.int32) for v in valid], axis=0) > 0
    return s, ok

def attn_fwd_kernel(parts, chunk, blk, pos_ref, q_ref, *refs):
    k_refs, v_refs = refs[:parts], refs[parts:2 * parts]
    bias_ref, o_ref, lse_ref, s_ref = refs[2 * parts:]
    q_rows = q_ref.shape[0]
    rows = k_refs[0].shape[0]
    chunks = key_chunks(parts, rows, chunk)
    outs = []
    for h in range(2):
        qh = head_lanes(h, q_ref[...])
        top = None
        for c, (i, s0) in enumerate(chunks):
            s, ok = chunk_scores(pos_ref, k_refs[i][s0:s0 + chunk, :], qh, bias_ref, h, c, chunk, blk, q_rows)
            s = jnp.where(ok, s, NEGATIVE)
            s_ref[c * chunk:(c + 1) * chunk, :] = s
            m = jnp.max(s, axis=0, keepdims=True)
            top = m if top is None else jnp.maximum(top, m)
        total = jnp.zeros((1, q_rows), jnp.float32)
        acc = jnp.zeros((2 * DK, q_rows), jnp.float32)
        for c, (i, s0) in enumerate(chunks):
            p = jnp.exp(s_ref[c * chunk:(c + 1) * chunk, :] - top)
            total = total + jnp.sum(p, axis=0, keepdims=True)
            acc = acc + dot_tn(v_refs[i][s0:s0 + chunk, :], p.astype(jnp.bfloat16))
        outs.append((acc / total)[h * DK:(h + 1) * DK])
        lse_ref[0, h:h + 1, :] = top + jnp.log(total)
    o_ref[...] = jnp.concatenate(outs, axis=0).T.astype(o_ref.dtype)

def attn_fwd(pos, q, ks, vs, bias, blk):
    q_rows, width = q.shape
    parts, rows = len(ks), ks[0].shape[0]
    keys = parts * rows
    heads = width // DK
    span = bias.shape[1]
    chunk = min(256, rows)
    spec_q = pl.BlockSpec((q_rows, 2 * DK), lambda p, s: (0, p))
    spec_k = pl.BlockSpec((rows, 2 * DK), lambda p, s: (0, p))
    o, lse = pl.pallas_call(
        functools.partial(attn_fwd_kernel, parts, chunk, blk),
        grid_spec=pltpu.PrefetchScalarGridSpec(
            num_scalar_prefetch=1,
            grid=(heads // 2,),
            in_specs=[spec_q] + [spec_k] * (2 * parts) + [pl.BlockSpec((2, span, TILE, TILE), lambda p, s: (p, 0, 0, 0))],
            out_specs=[spec_q, pl.BlockSpec((1, 2, q_rows), lambda p, s: (p, 0, 0))],
            scratch_shapes=[pltpu.VMEM((keys, q_rows), jnp.float32)],
        ),
        out_shape=[jax.ShapeDtypeStruct((q_rows, width), jnp.bfloat16), jax.ShapeDtypeStruct((heads // 2, 2, q_rows), jnp.float32)],
        compiler_params=pltpu.CompilerParams(vmem_limit_bytes=48 << 20),
        cost_estimate=pl.CostEstimate(flops=16 * q_rows * keys * width, bytes_accessed=4 * keys * width + 4 * q_rows * width + heads * span * TILE * TILE * 2, transcendentals=heads * q_rows * keys),
        name="attn_fwd",
    )(pos, q, *ks, *vs, bias)
    return o, lse

def skew_rows(x):
    width = 2 * x.shape[1]
    x = jnp.concatenate([jnp.zeros_like(x), x], axis=1)
    rows = x.shape[0]
    while rows > 8:
        rows //= 2
        x = x[:rows] + pltpu.roll(x[rows:], width - rows, 1)
    row = lax.broadcasted_iota(jnp.int32, x.shape, 0)
    for bit in (1, 2, 4):
        x = jnp.where((row & bit) != 0, pltpu.roll(x, width - bit, 1), x)
    return x

def attn_bwd_kernel(parts, chunk, blk, pos_ref, q_ref, do_ref, o_ref, lse_ref, *refs):
    k_refs, v_refs = refs[:parts], refs[parts:2 * parts]
    bias_ref, dq_ref = refs[2 * parts:2 * parts + 2]
    dk_refs, dv_refs = refs[2 * parts + 2:3 * parts + 2], refs[3 * parts + 2:4 * parts + 2]
    d_ref, e_ref = refs[4 * parts + 2:]
    q_rows = q_ref.shape[0]
    rows = k_refs[0].shape[0]
    chunks = key_chunks(parts, rows, chunk)
    span = bias_ref.shape[1]
    half = span // 2
    n, sub, nq = chunk // blk, blk // TILE, q_rows // blk
    prod = (do_ref[...].astype(jnp.float32) * o_ref[...].astype(jnp.float32)).T
    outs = []
    for h in range(2):
        qh = head_lanes(h, q_ref[...])
        doh = head_lanes(h, do_ref[...])
        inner = jnp.sum(prod[h * DK:(h + 1) * DK], axis=0, keepdims=True)
        lse = lse_ref[0, h:h + 1, :]
        acc = jnp.zeros((2 * DK, q_rows), jnp.float32)
        e_ref[...] = jnp.zeros_like(e_ref)
        for c, (i, s0) in enumerate(chunks):
            k_chunk = k_refs[i][s0:s0 + chunk, :]
            s, ok = chunk_scores(pos_ref, k_chunk, qh, bias_ref, h, c, chunk, blk, q_rows)
            p = jnp.where(ok, jnp.exp(s - lse), 0.0)
            dp = dot_nt(v_refs[i][s0:s0 + chunk, :], doh)
            ds = p * (dp - inner)
            dsb = ds.astype(jnp.bfloat16)
            dv = dot_nn(p.astype(jnp.bfloat16), doh)
            dk = dot_nn(dsb, qh)
            at = pl.ds(s0, chunk)
            if h == 0:
                dk_refs[i][at, :] = dk.astype(jnp.bfloat16)
                dv_refs[i][at, :] = dv.astype(jnp.bfloat16)
            else:
                dk_refs[i][at, :] = (dk_refs[i][at, :].astype(jnp.float32) + dk).astype(jnp.bfloat16)
                dv_refs[i][at, :] = (dv_refs[i][at, :].astype(jnp.float32) + dv).astype(jnp.bfloat16)
            acc = acc + dot_tn(k_chunk, dsb)
            for kb in range(n):
                kpos = pos_ref[1 + nq + c * n + kb]
                for qb in range(nq):
                    e0 = (kpos - pos_ref[1 + qb]) + half
                    for d in range(1 - sub, sub):
                        tot = None
                        for kk in range(sub):
                            qq = kk - d
                            if 0 <= qq < sub:
                                r0, c0 = kb * blk + kk * TILE, qb * blk + qq * TILE
                                t = ds[r0:r0 + TILE, c0:c0 + TILE]
                                tot = t if tot is None else tot + t
                        e_ref[e0 + d] += tot
        outs.append(acc[h * DK:(h + 1) * DK])
        pieces = [jnp.zeros((1, TILE), jnp.float32) for _ in range(span + 1)]
        for e in range(span):
            r = jnp.sum(skew_rows(e_ref[e]), axis=0, keepdims=True)
            b = span - 1 - e
            pieces[b] = pieces[b] + r[:, :TILE]
            pieces[b + 1] = pieces[b + 1] + r[:, TILE:]
        d_ref[0, h:h + 1, :] = jnp.concatenate(pieces, axis=1)
    dq_ref[...] = jnp.concatenate(outs, axis=0).T.astype(dq_ref.dtype)

def attn_bwd(pos, q, do, o, lse, ks, vs, bias, blk):
    q_rows, width = q.shape
    parts, rows = len(ks), ks[0].shape[0]
    keys = parts * rows
    heads = width // DK
    span = bias.shape[1]
    chunk = min(256, rows)
    spec_q = pl.BlockSpec((q_rows, 2 * DK), lambda p, s: (0, p))
    spec_k = pl.BlockSpec((rows, 2 * DK), lambda p, s: (0, p))
    spec_l = pl.BlockSpec((1, 2, q_rows), lambda p, s: (p, 0, 0))
    out = pl.pallas_call(
        functools.partial(attn_bwd_kernel, parts, chunk, blk),
        grid_spec=pltpu.PrefetchScalarGridSpec(
            num_scalar_prefetch=1,
            grid=(heads // 2,),
            in_specs=[spec_q, spec_q, spec_q, spec_l] + [spec_k] * (2 * parts) + [pl.BlockSpec((2, span, TILE, TILE), lambda p, s: (p, 0, 0, 0))],
            out_specs=[spec_q] + [spec_k] * (2 * parts) + [pl.BlockSpec((1, 2, (span + 1) * TILE), lambda p, s: (p, 0, 0))],
            scratch_shapes=[pltpu.VMEM((span, TILE, TILE), jnp.float32)],
        ),
        out_shape=[jax.ShapeDtypeStruct((q_rows, width), jnp.bfloat16)]
        + [jax.ShapeDtypeStruct((rows, width), jnp.bfloat16)] * (2 * parts)
        + [jax.ShapeDtypeStruct((heads // 2, 2, (span + 1) * TILE), jnp.float32)],
        compiler_params=pltpu.CompilerParams(vmem_limit_bytes=48 << 20),
        cost_estimate=pl.CostEstimate(flops=40 * q_rows * keys * width, bytes_accessed=8 * keys * width + 8 * q_rows * width + heads * span * TILE * TILE * 2, transcendentals=heads * q_rows * keys),
        name="attn_bwd",
    )(pos, q, do, o, lse, *ks, *vs, bias)
    dq, dks, dvs, d = out[0], out[1:1 + parts], out[1 + parts:1 + 2 * parts], out[-1]
    return dq, dks, dvs, d.reshape(heads, (span + 1) * TILE)


def matmul_rows(left, right):
    return jnp.dot(left, right, preferred_element_type=jnp.float32)


def matmul_left(left, right):
    return lax.dot_general(left, right, (((0,), (0,)), ((), ())), preferred_element_type=jnp.float32)


def matmul_back(left, right):
    return lax.dot_general(left, right, (((1,), (1,)), ((), ())), preferred_element_type=jnp.float32)


def inv_rms(values):
    return lax.rsqrt(jnp.mean(values * values, axis=-1, keepdims=True) + EPS)


def norm_pull(grad, values, gain):
    scale = inv_rms(values)
    weighted = gain * grad
    mean = jnp.mean(weighted * values, axis=-1, keepdims=True)
    grad_in = scale * weighted - values * (scale * scale * scale) * mean
    grad_gain = jnp.sum(grad * values * scale, axis=0)
    return grad_in, grad_gain


def gelu_pair(pre):
    c = np.float32(np.sqrt(2.0 / np.pi))
    sq = pre * pre
    t = jnp.tanh(c * (pre + 0.044715 * (sq * pre)))
    half = 0.5 * (1.0 + t)
    slope = half + (0.5 * c) * pre * (1.0 - t * t) * (1.0 + 0.134145 * sq)
    return (pre * half).astype(jnp.bfloat16), slope.astype(jnp.bfloat16)


SWAP = [(0, 1), (1, 0)]


class Plan:
    def __init__(self, sizes):
        self.nz, self.ny, self.ns, self.m = sizes
        self.nx = self.ns * self.m
        self.z = lax.axis_index("z")
        self.y = lax.axis_index("y")
        self.s = lax.axis_index("s")
        self.q = lax.axis_index("q")
        self.core = lax.axis_index("core")
        self.x = self.s * self.m + self.q
        self.everywhere = ("z", "y", "s", "q", "core")
        self.axes = {"x": (("s", "q") if self.m > 1 else "s", self.nx, self.x), "y": ("y", self.ny, self.y)}

    def block_of(self, order, n):
        n_z = n % self.nz
        n = n // self.nz
        place = {}
        for name in reversed(order):
            _, size, mine = self.axes[name]
            part = n % size
            n = n // size
            place[name] = part ^ mine if size == 2 else part
        core = n ^ self.core
        return ((n_z * self.ny + place["y"]) * self.nx + place["x"]) * 2 + core

    def permutation(self, order, width):
        depth = width // (self.nz * self.ny * self.nx * 2)
        n = lax.broadcasted_iota(jnp.int32, (width, width), 1)
        i = lax.broadcasted_iota(jnp.int32, (width, width), 0)
        source = self.block_of(order, n // depth) * depth + n % depth
        return (i == source).astype(jnp.bfloat16)

    def take_blocks(self, rows, table):
        return jnp.take(rows.reshape(table.shape[0], -1, rows.shape[1]), table, axis=0).reshape(rows.shape)

    def exchange(self, piece, name):
        return lax.ppermute(piece, name, SWAP)

    def scatter_sum(self, product, order, rows):
        half = rows // 2
        other = self.exchange(product(half, rows), "core")
        name_a, size_a, _ = self.axes[order[0]]
        name_b, size_b, _ = self.axes[order[1]]
        low = jnp.bfloat16
        f32 = jnp.float32
        if size_a == 2 and size_b == 2:
            quarter = half // 2
            far = (product(quarter, half).astype(f32) + other[quarter:].astype(f32)).astype(low)
            far = self.exchange(far, name_a)
            near = (product(0, quarter).astype(f32) + other[:quarter].astype(f32)).astype(low)
            eighth = quarter // 2
            side = (near[eighth:].astype(f32) + far[eighth:].astype(f32)).astype(low)
            side = self.exchange(side, name_b)
            total = near[:eighth].astype(f32) + far[:eighth].astype(f32) + side.astype(f32)
            return total.astype(low).reshape(self.nz, eighth // self.nz, -1)
        whole = (product(0, half).astype(f32) + other.astype(f32)).astype(low)
        whole = whole.reshape(size_a, half // size_a, -1)
        whole = lax.psum_scatter(whole, name_a, scatter_dimension=0, tiled=False)
        whole = whole.reshape(size_b, half // (size_a * size_b), -1)
        whole = lax.psum_scatter(whole, name_b, scatter_dimension=0, tiled=False)
        return whole.reshape(self.nz, half // (size_a * size_b * self.nz), -1)

    def sum_z(self, piece):
        if self.nz == 1:
            return piece[0].astype(jnp.float32)
        return lax.psum_scatter(piece, "z", scatter_dimension=0, tiled=False).astype(jnp.float32)

    def to_sequences(self, local):
        own = lax.dynamic_index_in_dim(local, self.s, 0, keepdims=False)
        other = lax.dynamic_index_in_dim(local, 1 - self.s, 0, keepdims=False)
        return jnp.concatenate([own, self.exchange(other, "s")], axis=0)

    def from_sequences(self, rows):
        blk = rows.shape[0] // 2
        own, other = rows[:blk], self.exchange(rows[blk:], "s")
        first = self.s == 0
        return jnp.stack([jnp.where(first, own, other), jnp.where(first, other, own)], axis=0)

    def gather_keys(self, rows):
        if self.m == 1:
            return [rows, self.exchange(rows, "core")]
        return [lax.all_gather(rows, ("q", "core"), axis=0, tiled=True)]

    def reduce_keys(self, parts):
        if self.m == 1:
            return parts[0].astype(jnp.float32) + self.exchange(parts[1], "core").astype(jnp.float32)
        return lax.psum_scatter(parts[0], ("q", "core"), scatter_dimension=0, tiled=True).astype(jnp.float32)

    def positions(self, length, blk):
        unit = blk // TILE
        mine = [(((self.s ^ j) * self.m + self.q) * 2 + self.core) * unit for j in range(2)]
        if self.m == 1:
            keys = [(((self.s ^ j) * self.m + self.q) * 2 + (self.core ^ c)) * unit for c in range(2) for j in range(2)]
        else:
            keys = [(((self.s ^ j) * self.m + q) * 2 + c) * unit for q in range(self.m) for c in range(2) for j in range(2)]
        return jnp.stack([length] + mine + keys).astype(jnp.int32)


def outer_grad_kernel(count, table_ref, *refs):
    left = jnp.concatenate([r[...] for r in refs[:count]], axis=1)
    refs[-1][...] = dot_tn(left, refs[count][...]).astype(refs[-1].dtype)


def outer_grad(hidden, grad_low, table, start, stop):
    rows, width = grad_low.shape
    count = 4 if (stop - start) % 4 == 0 else 1
    steps = (stop - start) // count
    specs = [pl.BlockSpec((rows, TILE), functools.partial(lambda j, i, t: (0, t[start + i * count + j]), j)) for j in range(count)]
    return pl.pallas_call(
        functools.partial(outer_grad_kernel, count),
        grid_spec=pltpu.PrefetchScalarGridSpec(
            num_scalar_prefetch=1,
            grid=(steps,),
            in_specs=specs + [pl.BlockSpec((rows, width), lambda i, t: (0, 0))],
            out_specs=pl.BlockSpec((count * TILE, width), lambda i, t: (i, 0)),
        ),
        out_shape=jax.ShapeDtypeStruct(((stop - start) * TILE, width), jnp.bfloat16),
        compiler_params=pltpu.CompilerParams(vmem_limit_bytes=32 << 20),
        cost_estimate=pl.CostEstimate(flops=2 * rows * width * (stop - start) * TILE, bytes_accessed=2 * (stop - start) * TILE * (rows + width) + 2 * rows * width, transcendentals=0),
        name="outer_grad",
    )(table, *([hidden] * count), grad_low)


def layer_forward(plan, x, weights, pos, bias, blk):
    attn_gain, w_qkv, w_output, mlp_gain, w_inner, w_outer = weights
    width = x.shape[1]
    normed = (x * inv_rms(x) * attn_gain).astype(jnp.bfloat16)
    qkv = matmul_rows(normed, w_qkv).astype(jnp.bfloat16)
    queries = qkv[:, :width]
    kv = plan.gather_keys(qkv[:, width:])
    keys = [p[:, :width] for p in kv]
    values = [p[:, width:] for p in kv]
    context, log_total = attn_fwd(pos, queries, keys, values, bias, blk)
    attended = x + matmul_rows(context, w_output)
    normed_mlp = (attended * inv_rms(attended) * mlp_gain).astype(jnp.bfloat16)
    hidden, slope = gelu_pair(matmul_rows(normed_mlp, w_inner))
    result = attended + matmul_rows(hidden, w_outer)
    return result, (x, normed, queries, keys, values, context, log_total, attended, normed_mlp, hidden, slope)


def layer_backward(plan, grad_out, weights, saved, pos, bias, blk, perms, table, orders):
    attn_gain, w_qkv, w_output, mlp_gain, w_inner, w_outer = weights
    x, normed, queries, keys, values, context, log_total, attended, normed_mlp, hidden, slope = saved
    low = jnp.bfloat16
    width = x.shape[1]
    grad_low = grad_out.astype(low)
    grad_pre = (matmul_back(grad_low, w_outer) * slope.astype(jnp.float32)).astype(low)
    wide = hidden.shape[1]
    if wide // (table[orders[1]].shape[0]) == TILE:
        outer_rows = lambda a, b: outer_grad(hidden, grad_low, table[orders[1]], a // TILE, b // TILE)
    else:
        outer_rows = lambda a, b: plan.take_blocks(matmul_left(hidden, grad_low).astype(low), table[orders[1]])[a:b]
    outer_piece = plan.scatter_sum(outer_rows, orders[1], wide)
    left = matmul_rows(normed_mlp, perms[orders[0]]).astype(low)
    inner_piece = plan.scatter_sum(lambda a, b: matmul_left(left[:, a:b], grad_pre).astype(low), orders[0], width)
    grad_normed_mlp = matmul_back(grad_pre, w_inner)
    grad_branch, grad_mlp_gain = norm_pull(grad_normed_mlp, attended, mlp_gain)
    grad_attended = grad_out + grad_branch
    attn_low = grad_attended.astype(low)
    grad_context = matmul_back(attn_low, w_output).astype(low)
    left_c = matmul_rows(context, perms[orders[2]]).astype(low)
    output_piece = plan.scatter_sum(lambda a, b: matmul_left(left_c[:, a:b], attn_low).astype(low), orders[2], width)
    grad_query, dk, dv, diag = attn_bwd(pos, queries, grad_context, context, log_total, keys, values, bias, blk)
    grad_kv = plan.reduce_keys([jnp.concatenate([a, b], axis=1) for a, b in zip(dk, dv)])
    grad_qkv = jnp.concatenate([grad_query, grad_kv.astype(low)], axis=1)
    left_n = matmul_rows(normed, perms[orders[3]]).astype(low)
    qkv_piece = plan.scatter_sum(lambda a, b: matmul_left(left_n[:, a:b], grad_qkv).astype(low), orders[3], width)
    grad_normed = matmul_back(grad_qkv, w_qkv)
    grad_flat, grad_attn_gain = norm_pull(grad_normed, x, attn_gain)
    attn_sum = plan.sum_z(jnp.concatenate([qkv_piece, output_piece], axis=2))
    grads = (
        grad_attn_gain,
        attn_sum[:, :width],
        attn_sum[:, width:2 * width],
        attn_sum[:, 2 * width:3 * width],
        attn_sum[:, 3 * width:],
        grad_mlp_gain,
        plan.sum_z(inner_piece),
        plan.sum_z(outer_piece),
    )
    return grad_attended + grad_flat, grads, diag


def body(sizes, inputs, cotangent, lengths, bucket_ids, *params):
    plan = Plan(sizes)
    one, bias_table, two = params[:8], params[8], params[9:]
    blk, width = inputs.shape[1], inputs.shape[2]
    f32, low = jnp.float32, jnp.bfloat16
    gains = jnp.stack([one[0], one[5], two[0], two[5]], axis=1)
    rows = gains.shape[0]
    table_column = jnp.pad(bias_table, (0, rows - bias_table.shape[0]))[:, None] if bias_table.shape[0] < rows else bias_table[:rows, None]
    small = jnp.pad(jnp.concatenate([gains, table_column], axis=1), ((0, 0), (0, TILE - 5)))
    everywhere = plan.everywhere

    def gather(piece):
        return lax.all_gather(piece, everywhere, axis=0, tiled=True)

    first = gather(jnp.concatenate([one[1], one[2], one[3], small], axis=1))
    second = gather(jnp.concatenate([one[4], one[6]], axis=1))
    outers = gather(jnp.concatenate([one[7], two[7]], axis=1))
    third = gather(jnp.concatenate([two[1], two[2], two[3], two[4], two[6]], axis=1))
    smalls = first[:, 3 * width:].astype(f32)
    gain = smalls[:, :4].T
    whole_table = smalls[:, 4].reshape(-1, rows)[:, :bias_table.shape[0]].reshape(-1)
    heads = width // DK
    buckets = whole_table.shape[0] // heads
    weights_one = (gain[0:1], first[:, :3 * width], second[:, :width], gain[1:2], second[:, width:], outers[:, :width])
    weights_two = (gain[2:3], third[:, :3 * width], third[:, 3 * width:4 * width], gain[3:4], third[:, 4 * width:], outers[:, width:])

    reversed_ids = jnp.concatenate([jnp.full((1,), -1, jnp.int32), bucket_ids[::-1]])
    indicator = (reversed_ids[None, :] == jnp.arange(buckets, dtype=jnp.int32)[:, None]).astype(low)
    bias = toeplitz_tiles(matmul_rows(whole_table.reshape(heads, buckets).astype(low), indicator))

    length = lax.dynamic_index_in_dim(lengths, plan.s, 0, keepdims=False)
    pos = plan.positions(length, blk)
    row = jnp.arange(blk, dtype=jnp.int32)
    row_pos = jnp.concatenate([row + pos[1] * TILE, row + pos[2] * TILE])
    row_valid = (row_pos < length).astype(f32)[:, None]

    x = plan.to_sequences(inputs).astype(f32)
    grad_out = plan.to_sequences(cotangent).astype(f32) * row_valid

    middle, saved_one = layer_forward(plan, x, weights_one, pos, bias, blk)
    final, saved_two = layer_forward(plan, middle, weights_two, pos, bias, blk)
    output = plan.from_sequences((final * row_valid).astype(low))

    xy, yx = ("x", "y"), ("y", "x")
    perms = {o: plan.permutation(o, width) for o in (xy, yx)}
    depth = one[7].shape[0]
    step = TILE if depth % TILE == 0 else depth
    blocks = jnp.arange(saved_one[9].shape[1] // step, dtype=jnp.int32)
    per = depth // step
    table = {o: plan.block_of(o, blocks // per) * per + blocks % per for o in (xy, yx)}
    grad_middle, grads_two, diag_two = layer_backward(plan, grad_out, weights_two, saved_two, pos, bias, blk, perms, table, (xy, yx, yx, xy))
    grad_state, grads_one, diag_one = layer_backward(plan, grad_middle, weights_one, saved_one, pos, bias, blk, perms, table, (xy, yx, xy, yx))
    input_grad = plan.from_sequences(grad_state.astype(low))

    grad_table = lax.dot_general(diag_one + diag_two, indicator.astype(f32), (((1,), (1,)), ((), ())), precision=HIGH_PRECISION)
    vectors = jnp.concatenate([grads_one[0], grads_one[5], grads_two[0], grads_two[5], grad_table.reshape(-1)])
    vectors = lax.psum(vectors, everywhere)
    device = ((plan.z * plan.ny + plan.y) * plan.nx + plan.x) * 2 + plan.core

    def share(start, count):
        return lax.dynamic_slice_in_dim(vectors, start + device * count, count, 0)

    gain_grads = [share(i * width, rows) for i in range(4)]
    table_grad = share(4 * width, bias_table.shape[0])
    return (
        output,
        input_grad,
        gain_grads[0],
        *grads_one[1:5],
        gain_grads[1],
        *grads_one[6:],
        table_grad,
        gain_grads[2],
        *grads_two[1:5],
        gain_grads[3],
        *grads_two[6:],
    )


def solution(mesh):
    dp, cp = mesh.shape["dp"], mesh.shape["cp"]
    nx = cp // 2
    ny = nx if dp % nx == 0 else 1

    def run(inputs, *rest):
        ns = inputs.shape[0] // dp
        assert ns == 2 and nx % ns == 0
        sizes = (dp // ny, ny, ns, nx // ns)
        finer = Mesh(mesh.devices.reshape(*sizes, 2), ("z", "y", "s", "q", "core"))
        dpn, cpn = ("z", "y"), ("s", "q", "core")
        tokens = P(dpn, cpn, None)
        vector, matrix = P(dpn + cpn), P(dpn + cpn, None)
        layer = (vector, matrix, matrix, matrix, matrix, vector, matrix, matrix)
        return jax.shard_map(
            functools.partial(body, sizes),
            mesh=finer,
            in_specs=(tokens, tokens, P(dpn), P()) + layer + (vector,) + layer,
            out_specs=(tokens, tokens) + layer + (vector,) + layer,
            check_vma=False,
        )(inputs, *rest)

    return run
```

```python
import functools

import jax
import jax.numpy as jnp
import numpy as np
from jax import lax
from jax.experimental import pallas as pl
from jax.experimental.pallas import tpu as pltpu
from jax.sharding import Mesh
from jax.sharding import PartitionSpec as P

DK = 64
TILE = 128
EPS = 1e-06
NEGATIVE = -1e30
HIGH_PRECISION = lax.Precision.HIGHEST


def toeplitz_kernel(span, u_ref, t_ref):
    for e in range(span):
        base = TILE * (span - 1 - e)
        w = jnp.broadcast_to(u_ref[0, :, base:base + 2 * TILE], (TILE, 2 * TILE))
        t_ref[0, e] = pltpu.roll(w, TILE, 1, stride=1, stride_axis=0)[:, :TILE].astype(t_ref.dtype)

def toeplitz_tiles(u):
    heads, width = u.shape
    span = width // TILE - 1
    return pl.pallas_call(
        functools.partial(toeplitz_kernel, span),
        grid=(heads,),
        in_specs=[pl.BlockSpec((1, 1, width), lambda h: (h, 0, 0))],
        out_specs=pl.BlockSpec((1, span, TILE, TILE), lambda h: (h, 0, 0, 0)),
        out_shape=jax.ShapeDtypeStruct((heads, span, TILE, TILE), jnp.bfloat16),
        cost_estimate=pl.CostEstimate(flops=heads * span * TILE * TILE * 4, bytes_accessed=heads * span * TILE * TILE * 2, transcendentals=0),
        name="toeplitz",
    )(u.reshape(heads, 1, width))

def head_lanes(h, x):
    lane = lax.broadcasted_iota(jnp.int32, x.shape, 1)
    return jnp.where((lane // DK) == h, x, jnp.zeros_like(x))

def dot_nt(a, b):
    return lax.dot_general(a, b, (((1,), (1,)), ((), ())), preferred_element_type=jnp.float32)

def dot_tn(a, b):
    return lax.dot_general(a, b, (((0,), (0,)), ((), ())), preferred_element_type=jnp.float32)

def dot_nn(a, b):
    return lax.dot_general(a, b, (((1,), (0,)), ((), ())), preferred_element_type=jnp.float32)

def key_chunks(parts, rows, chunk):
    return [(i, s) for i in range(parts) for s in range(0, rows, chunk)]

def chunk_scores(pos_ref, k_chunk, q_head, bias_ref, h, c, chunk, blk, q_rows):
    n = chunk // blk
    sub = blk // TILE
    nq = q_rows // blk
    s = dot_nt(k_chunk, q_head)
    half = bias_ref.shape[1] // 2
    rows = []
    for kb in range(n):
        kpos = pos_ref[1 + nq + c * n + kb]
        for kk in range(sub):
            cols = []
            for qb in range(nq):
                e0 = (kpos - pos_ref[1 + qb]) + half + kk
                for qq in range(sub):
                    cols.append(bias_ref[h, e0 - qq])
            rows.append(jnp.concatenate(cols, axis=1))
    bias = jnp.concatenate(rows, axis=0).astype(jnp.float32)
    s = s + bias
    valid = []
    for kb in range(n):
        limit = pos_ref[0] - pos_ref[1 + nq + c * n + kb] * TILE
        valid.append(lax.broadcasted_iota(jnp.int32, (blk, 1), 0) < limit)
    ok = valid[0] if n == 1 else jnp.concatenate([v.astype(jnp.int32) for v in valid], axis=0) > 0
    return s, ok

def attn_fwd_kernel(parts, chunk, blk, pos_ref, q_ref, *refs):
    k_refs, v_refs = refs[:parts], refs[parts:2 * parts]
    bias_ref, o_ref, lse_ref, s_ref = refs[2 * parts:]
    q_rows = q_ref.shape[0]
    rows = k_refs[0].shape[0]
    chunks = key_chunks(parts, rows, chunk)
    outs = []
    for h in range(2):
        qh = head_lanes(h, q_ref[...])
        top = None
        for c, (i, s0) in enumerate(chunks):
            s, ok = chunk_scores(pos_ref, k_refs[i][s0:s0 + chunk, :], qh, bias_ref, h, c, chunk, blk, q_rows)
            s = jnp.where(ok, s, NEGATIVE)
            s_ref[c * chunk:(c + 1) * chunk, :] = s
            m = jnp.max(s, axis=0, keepdims=True)
            top = m if top is None else jnp.maximum(top, m)
        total = jnp.zeros((1, q_rows), jnp.float32)
        acc = jnp.zeros((2 * DK, q_rows), jnp.float32)
        for c, (i, s0) in enumerate(chunks):
            p = jnp.exp(s_ref[c * chunk:(c + 1) * chunk, :] - top)
            total = total + jnp.sum(p, axis=0, keepdims=True)
            acc = acc + dot_tn(v_refs[i][s0:s0 + chunk, :], p.astype(jnp.bfloat16))
        outs.append((acc / total)[h * DK:(h + 1) * DK])
        lse_ref[0, h:h + 1, :] = top + jnp.log(total)
    o_ref[...] = jnp.concatenate(outs, axis=0).T.astype(o_ref.dtype)

def attn_fwd(pos, q, ks, vs, bias, blk):
    q_rows, width = q.shape
    parts, rows = len(ks), ks[0].shape[0]
    keys = parts * rows
    heads = width // DK
    span = bias.shape[1]
    chunk = min(256, rows)
    spec_q = pl.BlockSpec((q_rows, 2 * DK), lambda p, s: (0, p))
    spec_k = pl.BlockSpec((rows, 2 * DK), lambda p, s: (0, p))
    o, lse = pl.pallas_call(
        functools.partial(attn_fwd_kernel, parts, chunk, blk),
        grid_spec=pltpu.PrefetchScalarGridSpec(
            num_scalar_prefetch=1,
            grid=(heads // 2,),
            in_specs=[spec_q] + [spec_k] * (2 * parts) + [pl.BlockSpec((2, span, TILE, TILE), lambda p, s: (p, 0, 0, 0))],
            out_specs=[spec_q, pl.BlockSpec((1, 2, q_rows), lambda p, s: (p, 0, 0))],
            scratch_shapes=[pltpu.VMEM((keys, q_rows), jnp.float32)],
        ),
        out_shape=[jax.ShapeDtypeStruct((q_rows, width), jnp.bfloat16), jax.ShapeDtypeStruct((heads // 2, 2, q_rows), jnp.float32)],
        compiler_params=pltpu.CompilerParams(vmem_limit_bytes=48 << 20),
        cost_estimate=pl.CostEstimate(flops=16 * q_rows * keys * width, bytes_accessed=4 * keys * width + 4 * q_rows * width + heads * span * TILE * TILE * 2, transcendentals=heads * q_rows * keys),
        name="attn_fwd",
    )(pos, q, *ks, *vs, bias)
    return o, lse

def skew_rows(x):
    width = 2 * x.shape[1]
    x = jnp.concatenate([jnp.zeros_like(x), x], axis=1)
    rows = x.shape[0]
    while rows > 8:
        rows //= 2
        x = x[:rows] + pltpu.roll(x[rows:], width - rows, 1)
    row = lax.broadcasted_iota(jnp.int32, x.shape, 0)
    for bit in (1, 2, 4):
        x = jnp.where((row & bit) != 0, pltpu.roll(x, width - bit, 1), x)
    return x

def attn_bwd_kernel(parts, chunk, blk, pos_ref, q_ref, do_ref, o_ref, lse_ref, *refs):
    k_refs, v_refs = refs[:parts], refs[parts:2 * parts]
    bias_ref, dq_ref = refs[2 * parts:2 * parts + 2]
    dk_refs, dv_refs = refs[2 * parts + 2:3 * parts + 2], refs[3 * parts + 2:4 * parts + 2]
    d_ref, e_ref = refs[4 * parts + 2:]
    q_rows = q_ref.shape[0]
    rows = k_refs[0].shape[0]
    chunks = key_chunks(parts, rows, chunk)
    span = bias_ref.shape[1]
    half = span // 2
    n, sub, nq = chunk // blk, blk // TILE, q_rows // blk
    prod = (do_ref[...].astype(jnp.float32) * o_ref[...].astype(jnp.float32)).T
    outs = []
    for h in range(2):
        qh = head_lanes(h, q_ref[...])
        doh = head_lanes(h, do_ref[...])
        inner = jnp.sum(prod[h * DK:(h + 1) * DK], axis=0, keepdims=True)
        lse = lse_ref[0, h:h + 1, :]
        acc = jnp.zeros((2 * DK, q_rows), jnp.float32)
        e_ref[...] = jnp.zeros_like(e_ref)
        for c, (i, s0) in enumerate(chunks):
            k_chunk = k_refs[i][s0:s0 + chunk, :]
            s, ok = chunk_scores(pos_ref, k_chunk, qh, bias_ref, h, c, chunk, blk, q_rows)
            p = jnp.where(ok, jnp.exp(s - lse), 0.0)
            dp = dot_nt(v_refs[i][s0:s0 + chunk, :], doh)
            ds = p * (dp - inner)
            dsb = ds.astype(jnp.bfloat16)
            dv = dot_nn(p.astype(jnp.bfloat16), doh)
            dk = dot_nn(dsb, qh)
            at = pl.ds(s0, chunk)
            if h == 0:
                dk_refs[i][at, :] = dk.astype(jnp.bfloat16)
                dv_refs[i][at, :] = dv.astype(jnp.bfloat16)
            else:
                dk_refs[i][at, :] = (dk_refs[i][at, :].astype(jnp.float32) + dk).astype(jnp.bfloat16)
                dv_refs[i][at, :] = (dv_refs[i][at, :].astype(jnp.float32) + dv).astype(jnp.bfloat16)
            acc = acc + dot_tn(k_chunk, dsb)
            for kb in range(n):
                kpos = pos_ref[1 + nq + c * n + kb]
                for qb in range(nq):
                    e0 = (kpos - pos_ref[1 + qb]) + half
                    for d in range(1 - sub, sub):
                        tot = None
                        for kk in range(sub):
                            qq = kk - d
                            if 0 <= qq < sub:
                                r0, c0 = kb * blk + kk * TILE, qb * blk + qq * TILE
                                t = ds[r0:r0 + TILE, c0:c0 + TILE]
                                tot = t if tot is None else tot + t
                        e_ref[e0 + d] += tot
        outs.append(acc[h * DK:(h + 1) * DK])
        pieces = [jnp.zeros((1, TILE), jnp.float32) for _ in range(span + 1)]
        for e in range(span):
            r = jnp.sum(skew_rows(e_ref[e]), axis=0, keepdims=True)
            b = span - 1 - e
            pieces[b] = pieces[b] + r[:, :TILE]
            pieces[b + 1] = pieces[b + 1] + r[:, TILE:]
        d_ref[0, h:h + 1, :] = jnp.concatenate(pieces, axis=1)
    dq_ref[...] = jnp.concatenate(outs, axis=0).T.astype(dq_ref.dtype)

def attn_bwd(pos, q, do, o, lse, ks, vs, bias, blk, share, shares):
    q_rows, width = q.shape
    parts, rows = len(ks), ks[0].shape[0]
    keys = parts * rows
    heads = width // DK // shares
    width = width // shares
    span = bias.shape[1]
    chunk = min(256, rows)
    first = share * (heads // 2)
    spec_q = pl.BlockSpec((q_rows, 2 * DK), lambda p, s: (0, first + p))
    spec_k = pl.BlockSpec((rows, 2 * DK), lambda p, s: (0, first + p))
    spec_l = pl.BlockSpec((1, 2, q_rows), lambda p, s: (first + p, 0, 0))
    spec_b = pl.BlockSpec((2, span, TILE, TILE), lambda p, s: (first + p, 0, 0, 0))
    out_q = pl.BlockSpec((q_rows, 2 * DK), lambda p, s: (0, p))
    out_k = pl.BlockSpec((rows, 2 * DK), lambda p, s: (0, p))
    out = pl.pallas_call(
        functools.partial(attn_bwd_kernel, parts, chunk, blk),
        grid_spec=pltpu.PrefetchScalarGridSpec(
            num_scalar_prefetch=1,
            grid=(heads // 2,),
            in_specs=[spec_q, spec_q, spec_q, spec_l] + [spec_k] * (2 * parts) + [spec_b],
            out_specs=[out_q] + [out_k] * (2 * parts) + [pl.BlockSpec((1, 2, (span + 1) * TILE), lambda p, s: (p, 0, 0))],
            scratch_shapes=[pltpu.VMEM((span, TILE, TILE), jnp.float32)],
        ),
        out_shape=[jax.ShapeDtypeStruct((q_rows, width), jnp.bfloat16)]
        + [jax.ShapeDtypeStruct((rows, width), jnp.bfloat16)] * (2 * parts)
        + [jax.ShapeDtypeStruct((heads // 2, 2, (span + 1) * TILE), jnp.float32)],
        compiler_params=pltpu.CompilerParams(vmem_limit_bytes=48 << 20),
        cost_estimate=pl.CostEstimate(flops=40 * q_rows * keys * width, bytes_accessed=8 * keys * width + 8 * q_rows * width + heads * span * TILE * TILE * 2, transcendentals=heads * q_rows * keys),
        name="attn_bwd",
    )(pos, q, do, o, lse, *ks, *vs, bias)
    dq, dks, dvs, d = out[0], out[1:1 + parts], out[1 + parts:1 + 2 * parts], out[-1]
    return dq, dks, dvs, d.reshape(heads, (span + 1) * TILE)


def matmul_rows(left, right):
    return jnp.dot(left, right, preferred_element_type=jnp.float32)


def matmul_left(left, right):
    return lax.dot_general(left, right, (((0,), (0,)), ((), ())), preferred_element_type=jnp.float32)


def matmul_back(left, right):
    return lax.dot_general(left, right, (((1,), (1,)), ((), ())), preferred_element_type=jnp.float32)


def inv_rms(values):
    return lax.rsqrt(jnp.mean(values * values, axis=-1, keepdims=True) + EPS)


def norm_pull(grad, values, gain):
    scale = inv_rms(values)
    weighted = gain * grad
    mean = jnp.mean(weighted * values, axis=-1, keepdims=True)
    grad_in = scale * weighted - values * (scale * scale * scale) * mean
    grad_gain = jnp.sum(grad * values * scale, axis=0)
    return grad_in, grad_gain


def gelu_pair(pre):
    c = np.float32(np.sqrt(2.0 / np.pi))
    sq = pre * pre
    t = jnp.tanh(c * (pre + 0.044715 * (sq * pre)))
    half = 0.5 * (1.0 + t)
    slope = half + (0.5 * c) * pre * (1.0 - t * t) * (1.0 + 0.134145 * sq)
    return (pre * half).astype(jnp.bfloat16), slope.astype(jnp.bfloat16)


SWAP = [(0, 1), (1, 0)]


class Plan:
    def __init__(self, sizes):
        self.nz, self.ny, self.ns, self.m = sizes
        self.nx = self.ns * self.m
        self.z = lax.axis_index("z")
        self.y = lax.axis_index("y")
        self.s = lax.axis_index("s")
        self.q = lax.axis_index("q")
        self.core = lax.axis_index("core")
        self.x = self.s * self.m + self.q
        self.everywhere = ("z", "y", "s", "q", "core")
        self.axes = {"x": (("s", "q") if self.m > 1 else "s", self.nx, self.x), "y": ("y", self.ny, self.y)}

    def block_of(self, order, n):
        n_z = n % self.nz
        n = n // self.nz
        place = {}
        for name in reversed(order):
            _, size, mine = self.axes[name]
            part = n % size
            n = n // size
            place[name] = part ^ mine if size == 2 else part
        core = n ^ self.core
        return ((n_z * self.ny + place["y"]) * self.nx + place["x"]) * 2 + core

    def permutation(self, order, width):
        depth = width // (self.nz * self.ny * self.nx * 2)
        n = lax.broadcasted_iota(jnp.int32, (width, width), 1)
        i = lax.broadcasted_iota(jnp.int32, (width, width), 0)
        source = self.block_of(order, n // depth) * depth + n % depth
        return (i == source).astype(jnp.bfloat16)

    def take_blocks(self, rows, table):
        return jnp.take(rows.reshape(table.shape[0], -1, rows.shape[1]), table, axis=0).reshape(rows.shape)

    def exchange(self, piece, name):
        return lax.ppermute(piece, name, SWAP)

    def sum_z(self, piece):
        if self.nz == 1:
            return piece[0]
        return lax.psum_scatter(piece, "z", scatter_dimension=0, tiled=False)

    def sum_vector(self, vector):
        for name, size in (("core", 2), ("z", self.nz), ("y", self.ny), ("q", self.m), ("s", self.ns)):
            if size & (size - 1):
                vector = lax.psum(vector, name)
                continue
            step = 1
            while step < size:
                vector = vector + lax.ppermute(vector, name, [(i, i ^ step) for i in range(size)])
                step *= 2
        return vector

    def to_sequences(self, local):
        own = lax.dynamic_index_in_dim(local, self.s, 0, keepdims=False)
        other = lax.dynamic_index_in_dim(local, 1 - self.s, 0, keepdims=False)
        return jnp.concatenate([own, self.exchange(other, "s")], axis=0)

    def from_sequences(self, rows):
        blk = rows.shape[0] // 2
        return self.in_order(rows[:blk], self.exchange(rows[blk:], "s"))

    def in_order(self, own, other):
        first = self.s == 0
        return jnp.stack([jnp.where(first, own, other), jnp.where(first, other, own)], axis=0)

    def gather_keys(self, rows):
        if self.m == 1:
            return [rows, self.exchange(rows, "core")]
        return [lax.all_gather(rows, ("q", "core"), axis=0, tiled=True)]

    def reduce_keys(self, parts):
        if self.m == 1:
            return parts[0].astype(jnp.float32) + self.exchange(parts[1], "core").astype(jnp.float32)
        return lax.psum_scatter(parts[0], ("q", "core"), scatter_dimension=0, tiled=True).astype(jnp.float32)

    def positions(self, length, blk):
        unit = blk // TILE
        mine = [(((self.s ^ j) * self.m + self.q) * 2 + self.core) * unit for j in range(2)]
        if self.m == 1:
            keys = [(((self.s ^ j) * self.m + self.q) * 2 + (self.core ^ c)) * unit for c in range(2) for j in range(2)]
        else:
            keys = [(((self.s ^ j) * self.m + q) * 2 + c) * unit for q in range(self.m) for c in range(2) for j in range(2)]
        return jnp.stack([length] + mine + keys).astype(jnp.int32)


def assemble_kernel(steps, depth, table_ref, *refs):
    i = pl.program_id(0)
    out = refs[-1]
    core, x = table_ref[0], table_ref[1]
    quads = [refs[j:j + 4] for j in range(0, len(refs) - 1, 4)]
    for quad, (start, count) in zip(quads, steps):

        @pl.when(jnp.logical_and(i >= start, i < start + count))
        def _(quad=quad):
            for j, r in enumerate(quad):
                place = (x ^ (j // 2)) * 2 + (core ^ (j % 2))
                out[pl.ds(pl.multiple_of(place * depth, depth), depth), :] = r[...]


def assemble(table, quads, depth):
    width = quads[0][0].shape[1]
    steps, at = [], 0
    for q in quads:
        steps.append((at, q[0].shape[0] // depth))
        at += q[0].shape[0] // depth

    def source_map(start, count):
        return lambda i, t: (jnp.clip(i - start, 0, count - 1), 0)

    return pl.pallas_call(
        functools.partial(assemble_kernel, steps, depth),
        grid_spec=pltpu.PrefetchScalarGridSpec(
            num_scalar_prefetch=1,
            grid=(at,),
            in_specs=[pl.BlockSpec((depth, width), source_map(*s)) for s in steps for _ in range(4)],
            out_specs=pl.BlockSpec((4 * depth, width), lambda i, t: (t[2 + i], 0)),
        ),
        out_shape=jax.ShapeDtypeStruct((at * 4 * depth, width), quads[0][0].dtype),
        compiler_params=pltpu.CompilerParams(vmem_limit_bytes=48 << 20),
        cost_estimate=pl.CostEstimate(flops=0, bytes_accessed=16 * at * depth * width, transcendentals=0),
        name="assemble",
    )(table, *[r for q in quads for r in q])


class Held:
    def __init__(self, value):
        self.value = value


def tie(main, *held):
    got = lax.optimization_barrier((main,) + tuple(h.value for h in held))
    for h, v in zip(held, got[1:]):
        h.value = v
    return got[0]


class Fetch:
    def __init__(self, plan, shard):
        self.plan, self.shard = plan, Held(shard)
        self.pairs = plan.nx == 2 and plan.ny == 2 and plan.nz % 2 == 0
        self.depth = shard.shape[0]

    def start(self):
        axes = "z" if self.pairs else self.plan.everywhere
        self.near = Held(lax.all_gather(self.shard.value, axes, axis=0, tiled=True))

    def send(self, piece, name):
        return Held(self.plan.exchange(piece.value, name))

    def a(self, main, following=None):
        held = [self.near] + ([following.shard] if following else [])
        main = tie(main, *held)
        if following:
            following.start()
        if self.pairs:
            self.by_x, self.by_y, self.near_twin = [self.send(self.near, n) for n in ("s", "y", "core")]
        return main

    def b(self, main):
        if self.pairs:
            main = tie(main, self.by_x, self.by_y, self.near_twin)
            half = self.by_x.value.shape[0] // 2
            self.low = Held(self.plan.exchange(self.by_y.value[:half], "s"))
            self.high = Held(self.plan.exchange(self.by_x.value[half:], "y"))
            self.x_twin, self.y_twin = self.send(self.by_x, "core"), self.send(self.by_y, "core")
        return main

    def c(self, main):
        return tie(main, self.x_twin, self.y_twin) if self.pairs else main

    def d(self, main):
        if self.pairs:
            main = tie(main, self.low, self.high)
            self.low_twin, self.high_twin = self.send(self.low, "core"), self.send(self.high, "core")
        return main

    def e(self, main):
        if not self.pairs:
            return main, self.near.value
        main = tie(main, self.low_twin, self.high_twin)
        plan = self.plan
        half = self.low.value.shape[0]
        by_y, y_twin = self.by_y.value, self.y_twin.value
        quads = [
            (self.near.value, self.near_twin.value, self.by_x.value, self.x_twin.value),
            (by_y[:half], y_twin[:half], self.low.value, self.low_twin.value),
            (by_y[half:], y_twin[half:], self.high.value, self.high_twin.value),
        ]
        z = jnp.arange(plan.nz, dtype=jnp.int32)
        order = jnp.concatenate([z * 2 + plan.y, z * 2 + (1 - plan.y)])
        table = jnp.concatenate([jnp.stack([plan.core, plan.x]).astype(jnp.int32), order.astype(jnp.int32)])
        whole = Held(assemble(table, quads, self.depth))
        main = tie(main, whole)
        return main, whole.value


def add_low(*terms):
    total = terms[0].astype(jnp.float32)
    for t in terms[1:]:
        total = total + t.astype(jnp.float32)
    return total.astype(jnp.bfloat16)


class Chain:
    def __init__(self, plan, product, order, rows):
        self.plan, self.product, self.rows = plan, product, rows
        self.name_a, self.size_a, _ = plan.axes[order[0]]
        self.name_b, self.size_b, _ = plan.axes[order[1]]
        self.pairs = self.size_a == 2 and self.size_b == 2
        self.part = None

    def one(self):
        self.part = Held(self.product(self.rows // 2, self.rows))
        return self.part

    def send_one(self):
        self.other = Held(self.plan.exchange(self.part.value, "core"))

    def two(self):
        half = self.rows // 2
        if self.pairs:
            quarter = half // 2
            self.part = Held(add_low(self.product(quarter, half), self.other.value[quarter:]))
        else:
            self.part = Held(add_low(self.product(0, half), self.other.value))
        return self.part

    def send_two(self):
        if self.pairs:
            self.far = Held(self.plan.exchange(self.part.value, self.name_a))
        else:
            whole = self.part.value.reshape(self.size_a, self.rows // (2 * self.size_a), -1)
            self.far = Held(lax.psum_scatter(whole, self.name_a, scatter_dimension=0, tiled=False))

    def near(self):
        if self.pairs:
            quarter = self.rows // 4
            self.close_by = Held(add_low(self.product(0, quarter), self.other.value[:quarter]))
            return self.close_by
        return self.far

    def three(self):
        if self.pairs:
            eighth = self.rows // 8
            self.part = Held(add_low(self.close_by.value[eighth:], self.far.value[eighth:]))
        else:
            self.part = self.far
        return self.part

    def send_three(self):
        if self.pairs:
            self.side = Held(self.plan.exchange(self.part.value, self.name_b))
        else:
            whole = self.part.value.reshape(self.size_b, self.part.value.shape[0] // self.size_b, -1)
            self.side = Held(lax.psum_scatter(whole, self.name_b, scatter_dimension=0, tiled=False))

    def close(self):
        nz = self.plan.nz
        if self.pairs:
            eighth = self.rows // 8
            total = add_low(self.close_by.value[:eighth], self.far.value[:eighth], self.side.value)
        else:
            total = self.side.value
        self.piece = Held(total.reshape(nz, total.shape[0] // nz, -1))
        return self.piece


def outer_grad_kernel(count, table_ref, *refs):
    left = jnp.concatenate([r[...] for r in refs[:count]], axis=1)
    refs[-1][...] = dot_tn(left, refs[count][...]).astype(refs[-1].dtype)


def outer_grad(hidden, grad_low, table, start, stop):
    rows, width = grad_low.shape
    count = 4 if (stop - start) % 4 == 0 else 1
    steps = (stop - start) // count
    specs = [pl.BlockSpec((rows, TILE), functools.partial(lambda j, i, t: (0, t[start + i * count + j]), j)) for j in range(count)]
    return pl.pallas_call(
        functools.partial(outer_grad_kernel, count),
        grid_spec=pltpu.PrefetchScalarGridSpec(
            num_scalar_prefetch=1,
            grid=(steps,),
            in_specs=specs + [pl.BlockSpec((rows, width), lambda i, t: (0, 0))],
            out_specs=pl.BlockSpec((count * TILE, width), lambda i, t: (i, 0)),
        ),
        out_shape=jax.ShapeDtypeStruct(((stop - start) * TILE, width), jnp.bfloat16),
        compiler_params=pltpu.CompilerParams(vmem_limit_bytes=32 << 20),
        cost_estimate=pl.CostEstimate(flops=2 * rows * width * (stop - start) * TILE, bytes_accessed=2 * (stop - start) * TILE * (rows + width) + 2 * rows * width, transcendentals=0),
        name="outer_grad",
    )(table, *([hidden] * count), grad_low)


def project(x, gain, w_qkv):
    normed = (x * inv_rms(x) * gain).astype(jnp.bfloat16)
    return normed, matmul_rows(normed, w_qkv).astype(jnp.bfloat16)


def widen(attended, gain, w_inner):
    normed_mlp = (attended * inv_rms(attended) * gain).astype(jnp.bfloat16)
    return (normed_mlp,) + gelu_pair(matmul_rows(normed_mlp, w_inner))


def backward(plan, grad_out, layers, pos, bias, blk, perms, table, output_half):
    low, f32 = jnp.bfloat16, jnp.float32
    previous = None
    results, diags = [], []
    for weights, saved, orders in layers:
        attn_gain, w_qkv, w_output, mlp_gain, w_inner, w_outer = weights
        x, normed, queries, keys, values, context, log_total, attended, normed_mlp, hidden, slope = saved
        width = x.shape[1]
        grad_low = grad_out.astype(low)
        wide = hidden.shape[1]
        blocks = table[orders[1]]

        def outer_rows(a, b, hidden=hidden, grad_low=grad_low, blocks=blocks, wide=wide):
            if wide // blocks.shape[0] == TILE:
                return outer_grad(hidden, grad_low, blocks, a // TILE, b // TILE)
            return plan.take_blocks(matmul_left(hidden, grad_low).astype(low), blocks)[a:b]

        def rows_of(left, right):
            return lambda a, b: matmul_left(left[:, a:b], right).astype(low)

        outer = Chain(plan, outer_rows, orders[1], wide)
        late = [previous.outer.side, previous.inner.side] if previous else []
        grad_out = tie(grad_out, outer.one(), *late)
        outer.send_one()
        grad_pre = (matmul_back(grad_out.astype(low), w_outer) * slope.astype(f32)).astype(low)
        grad_pre = tie(grad_pre, outer.other)
        left_m = matmul_rows(normed_mlp, perms[orders[0]]).astype(low)
        inner = Chain(plan, rows_of(left_m, grad_pre), orders[0], width)
        late = [previous.outer.close(), previous.inner.close()] if previous else []
        grad_pre = tie(grad_pre, outer.two(), inner.one(), *late)
        outer.send_two()
        inner.send_one()
        if previous:
            previous.sum_mlp(plan)
        grad_normed_mlp = matmul_back(grad_pre, w_inner)
        grad_branch, grad_mlp_gain = norm_pull(grad_normed_mlp, attended, mlp_gain)
        grad_attended = grad_out + grad_branch
        late = [previous.qk.far, previous.ov.far] if previous else []
        grad_attended = tie(grad_attended, inner.other, *late)
        late = [part for c in (previous.qk, previous.ov) for part in (c.near(), c.three())] if previous else []
        leaving = Held(output_half)
        grad_attended = tie(grad_attended, inner.two(), *late, *([] if previous else [leaving]))
        inner.send_two()
        if not previous:
            arrived = Held(plan.exchange(leaving.value, "s"))
        if previous:
            previous.qk.send_three()
            previous.ov.send_three()
        attn_low = grad_attended.astype(low)
        grad_context = matmul_back(attn_low, w_output).astype(low)
        left_c = matmul_rows(context, perms[orders[3]]).astype(low)
        left_n = {o: matmul_rows(normed, perms[o]).astype(low) for o in orders[2:]}
        grad_query, dk, dv, diag = attn_bwd(pos, queries, grad_context, context, log_total, keys, values, bias, blk, 0, 1)
        kv_parts = [jnp.concatenate([p, r], axis=1) for p, r in zip(dk, dv)]
        late = [previous.qk.side, previous.ov.side, previous.inner_sum, previous.outer_sum] if previous else [arrived]
        last_part = tie(kv_parts[-1], outer.far, inner.far, *late)
        grad_kv = plan.reduce_keys(kv_parts[:-1] + [last_part]).astype(low)
        late = [previous.qk.close(), previous.ov.close()] if previous else []
        grad_kv = tie(grad_kv, outer.near(), outer.three(), inner.near(), inner.three(), *late)
        outer.send_three()
        inner.send_three()
        if previous:
            previous.sum_attn(plan)
        grad_qk = jnp.concatenate([grad_query, grad_kv[:, :width]], axis=1)
        grad_v = grad_kv[:, width:]

        def ov_rows(a, b, left_c=left_c, left_n=left_n[orders[3]], attn_low=attn_low, grad_v=grad_v):
            return jnp.concatenate([matmul_left(left_c[:, a:b], attn_low).astype(low), matmul_left(left_n[:, a:b], grad_v).astype(low)], axis=1)

        qk = Chain(plan, rows_of(left_n[orders[2]], grad_qk), orders[2], width)
        ov = Chain(plan, ov_rows, orders[3], width)
        grad_qk = tie(grad_qk, qk.one(), ov.one())
        qk.send_one()
        ov.send_one()
        grad_normed = matmul_back(grad_qk, w_qkv[:, :2 * width]) + matmul_back(grad_v, w_qkv[:, 2 * width:])
        grad_flat, grad_attn_gain = norm_pull(grad_normed, x, attn_gain)
        grad_out = tie(grad_attended + grad_flat, qk.other, ov.other)
        grad_out = tie(grad_out, qk.two(), ov.two())
        qk.send_two()
        ov.send_two()
        previous = LayerSums(outer, inner, qk, ov, grad_attn_gain, grad_mlp_gain, width)
        results.append(previous)
        diags.append(diag)
    grad_out = tie(grad_out, outer.side, inner.side, results[0].attn_sum)
    grad_out = tie(grad_out, outer.close(), inner.close(), qk.near(), ov.near())
    previous.sum_mlp(plan)
    grad_out = tie(grad_out, qk.far, ov.far)
    grad_out = tie(grad_out, qk.three(), ov.three())
    qk.send_three()
    ov.send_three()
    qk.close()
    ov.close()
    previous.sum_attn(plan)
    return grad_out, results, diags, arrived.value


class LayerSums:
    def __init__(self, outer, inner, qk, ov, grad_attn_gain, grad_mlp_gain, width):
        self.outer, self.inner, self.qk, self.ov = outer, inner, qk, ov
        self.attn_gain, self.mlp_gain, self.width = grad_attn_gain, grad_mlp_gain, width

    def sum_mlp(self, plan):
        self.inner_sum = Held(plan.sum_z(self.inner.piece.value))
        self.outer_sum = Held(plan.sum_z(self.outer.piece.value))

    def sum_attn(self, plan):
        self.attn_sum = Held(plan.sum_z(jnp.concatenate([c.piece.value for c in (self.qk, self.ov)], axis=2)))

    def grads(self):
        w = self.width
        f32 = jnp.float32
        query, key, output, value = [self.attn_sum.value[:, i * w:(i + 1) * w].astype(f32) for i in range(4)]
        return [self.attn_gain, query, key, value, output, self.mlp_gain, self.inner_sum.value.astype(f32), self.outer_sum.value.astype(f32)]


def body(sizes, inputs, cotangent, lengths, bucket_ids, *params):
    plan = Plan(sizes)
    one, bias_table, two = params[:8], params[8], params[9:]
    blk, width = inputs.shape[1], inputs.shape[2]
    f32, low = jnp.float32, jnp.bfloat16
    gains = jnp.stack([one[0], one[5], two[0], two[5]], axis=1)
    rows = gains.shape[0]
    table_column = jnp.pad(bias_table, (0, rows - bias_table.shape[0]))[:, None] if bias_table.shape[0] < rows else bias_table[:rows, None]
    small = jnp.pad(jnp.concatenate([gains, table_column], axis=1), ((0, 0), (0, TILE - 5)))
    everywhere = plan.everywhere

    length = lax.dynamic_index_in_dim(lengths, plan.s, 0, keepdims=False)
    pos = plan.positions(length, blk)
    row = jnp.arange(blk, dtype=jnp.int32)
    row_pos = jnp.concatenate([row + pos[1] * TILE, row + pos[2] * TILE])
    row_valid = (row_pos < length).astype(f32)[:, None]

    shards = (
        jnp.concatenate([one[1], one[2], one[3], one[4], small], axis=1),
        one[6],
        one[7],
        jnp.concatenate([two[1], two[2], two[3], two[4]], axis=1),
        two[6],
        two[7],
    )
    attn_1, inner_1, outer_1, attn_2, inner_2, outer_2 = [Fetch(plan, piece) for piece in shards]
    attn_1.start()
    x = plan.to_sequences(inputs)
    cotangent = plan.to_sequences(cotangent)
    x = tie(x, inner_1.shard)
    inner_1.start()
    x = attn_1.a(x, outer_1)
    x = attn_1.b(x)
    x = attn_1.c(x)
    x = inner_1.a(x, attn_2)
    x = attn_1.d(x)
    x, first = attn_1.e(x)
    smalls = first[:, 4 * width:].astype(f32)
    gain = smalls[:, :4].T
    whole_table = smalls[:, 4].reshape(-1, rows)[:, :bias_table.shape[0]].reshape(-1)
    heads = width // DK
    buckets = whole_table.shape[0] // heads
    reversed_ids = jnp.concatenate([jnp.full((1,), -1, jnp.int32), bucket_ids[::-1]])
    indicator = (reversed_ids[None, :] == jnp.arange(buckets, dtype=jnp.int32)[:, None]).astype(low)
    bias = Held(toeplitz_tiles(matmul_rows(whole_table.reshape(heads, buckets).astype(low), indicator)))
    x = tie(x, bias)
    bias = bias.value
    x_one = x.astype(f32)
    normed_one, qkv = project(x_one, gain[0:1], first[:, :3 * width])
    qkv = inner_1.b(qkv)
    kv = plan.gather_keys(qkv[:, width:])
    qkv = inner_1.c(qkv)
    qkv = outer_1.a(qkv, inner_2)
    queries_one = qkv[:, :width]
    keys_one, values_one = [p[:, :width] for p in kv], [p[:, width:] for p in kv]
    context_one, log_one = attn_fwd(pos, queries_one, keys_one, values_one, bias, blk)
    context_one = inner_1.d(context_one)
    context_one, w_inner_one = inner_1.e(context_one)
    attended_one = x_one + matmul_rows(context_one, first[:, 3 * width:4 * width])
    attended_one = outer_1.b(attended_one)
    normed_mlp_one, hidden_one, slope_one = widen(attended_one, gain[1:2], w_inner_one)
    hidden_one = outer_1.c(hidden_one)
    hidden_one = attn_2.a(hidden_one, outer_2)
    hidden_one = outer_1.d(hidden_one)
    hidden_one, w_outer_one = outer_1.e(hidden_one)
    x_two = attended_one + matmul_rows(hidden_one, w_outer_one)
    x_two = attn_2.b(x_two)
    x_two = attn_2.c(x_two)
    x_two = inner_2.a(x_two)
    x_two = attn_2.d(x_two)
    x_two, third = attn_2.e(x_two)
    normed_two, qkv = project(x_two, gain[2:3], third[:, :3 * width])
    qkv = inner_2.b(qkv)
    kv = plan.gather_keys(qkv[:, width:])
    qkv = inner_2.c(qkv)
    qkv = outer_2.a(qkv)
    queries_two = qkv[:, :width]
    keys_two, values_two = [p[:, :width] for p in kv], [p[:, width:] for p in kv]
    context_two, log_two = attn_fwd(pos, queries_two, keys_two, values_two, bias, blk)
    context_two = inner_2.d(context_two)
    context_two, w_inner_two = inner_2.e(context_two)
    attended_two = x_two + matmul_rows(context_two, third[:, 3 * width:])
    attended_two = outer_2.b(attended_two)
    normed_mlp_two, hidden_two, slope_two = widen(attended_two, gain[3:4], w_inner_two)
    hidden_two = outer_2.c(hidden_two)
    hidden_two = outer_2.d(hidden_two)
    hidden_two, w_outer_two = outer_2.e(hidden_two)
    final = attended_two + matmul_rows(hidden_two, w_outer_two)
    output_rows = (final * row_valid).astype(low)
    grad_out = cotangent.astype(f32) * row_valid

    weights_one = (gain[0:1], first[:, :3 * width], first[:, 3 * width:4 * width], gain[1:2], w_inner_one, w_outer_one)
    weights_two = (gain[2:3], third[:, :3 * width], third[:, 3 * width:], gain[3:4], w_inner_two, w_outer_two)
    saved_one = (x_one, normed_one, queries_one, keys_one, values_one, context_one, log_one, attended_one, normed_mlp_one, hidden_one, slope_one)
    saved_two = (x_two, normed_two, queries_two, keys_two, values_two, context_two, log_two, attended_two, normed_mlp_two, hidden_two, slope_two)

    xy, yx = ("x", "y"), ("y", "x")
    perms = {o: plan.permutation(o, width) for o in (xy, yx)}
    depth = one[7].shape[0]
    step = TILE if depth % TILE == 0 else depth
    blocks = jnp.arange(saved_one[9].shape[1] // step, dtype=jnp.int32)
    per = depth // step
    table = {o: plan.block_of(o, blocks // per) * per + blocks % per for o in (xy, yx)}
    layers = [(weights_two, saved_two, (xy, yx, yx, xy)), (weights_one, saved_one, (xy, yx, yx, xy))]
    grad_state, sums, diags, arrived = backward(plan, grad_out, layers, pos, bias, blk, perms, table, output_rows[blk:])
    output = plan.in_order(output_rows[:blk], arrived)
    grads_two, grads_one = sums[0].grads(), sums[1].grads()
    input_grad = plan.from_sequences(grad_state.astype(low))

    grad_table = lax.dot_general(diags[0] + diags[1], indicator.astype(f32), (((1,), (1,)), ((), ())), precision=HIGH_PRECISION)
    vectors = jnp.concatenate([grads_one[0], grads_one[5], grads_two[0], grads_two[5], grad_table.reshape(-1)])
    held = Held(vectors)
    grad_state = tie(grad_state, held)
    vectors = plan.sum_vector(held.value)
    device = ((plan.z * plan.ny + plan.y) * plan.nx + plan.x) * 2 + plan.core

    def share(start, count):
        return lax.dynamic_slice_in_dim(vectors, start + device * count, count, 0)

    gain_grads = [share(i * width, rows) for i in range(4)]
    table_grad = share(4 * width, bias_table.shape[0])
    return (
        output,
        input_grad,
        gain_grads[0],
        *grads_one[1:5],
        gain_grads[1],
        *grads_one[6:],
        table_grad,
        gain_grads[2],
        *grads_two[1:5],
        gain_grads[3],
        *grads_two[6:],
    )


def solution(mesh):
    dp, cp = mesh.shape["dp"], mesh.shape["cp"]
    nx = cp // 2
    ny = nx if dp % nx == 0 else 1

    def run(inputs, *rest):
        ns = inputs.shape[0] // dp
        assert ns == 2 and nx % ns == 0
        sizes = (dp // ny, ny, ns, nx // ns)
        finer = Mesh(mesh.devices.reshape(*sizes, 2), ("z", "y", "s", "q", "core"))
        dpn, cpn = ("z", "y"), ("s", "q", "core")
        tokens = P(dpn, cpn, None)
        vector, matrix = P(dpn + cpn), P(dpn + cpn, None)
        layer = (vector, matrix, matrix, matrix, matrix, vector, matrix, matrix)
        return jax.shard_map(
            functools.partial(body, sizes),
            mesh=finer,
            in_specs=(tokens, tokens, P(dpn), P()) + layer + (vector,) + layer,
            out_specs=(tokens, tokens) + layer + (vector,) + layer,
            check_vma=False,
        )(inputs, *rest)

    return run
```

```python
import functools

import jax
import jax.numpy as jnp
import numpy as np
from jax import lax
from jax.experimental import pallas as pl
from jax.experimental.pallas import tpu as pltpu
from jax.sharding import Mesh
from jax.sharding import PartitionSpec as P

DK = 64
TILE = 128
EPS = 1e-06
NEGATIVE = -1e30
HIGH_PRECISION = lax.Precision.HIGHEST
BRIEF = pl.CostEstimate(flops=1024, bytes_accessed=1024, transcendentals=0)


def toeplitz_kernel(span, u_ref, t_ref):
    for e in range(span):
        base = TILE * (span - 1 - e)
        w = jnp.broadcast_to(u_ref[0, :, base:base + 2 * TILE], (TILE, 2 * TILE))
        t_ref[0, e] = pltpu.roll(w, TILE, 1, stride=1, stride_axis=0)[:, :TILE].astype(t_ref.dtype)

def toeplitz_tiles(u):
    heads, width = u.shape
    span = width // TILE - 1
    return pl.pallas_call(
        functools.partial(toeplitz_kernel, span),
        grid=(heads,),
        in_specs=[pl.BlockSpec((1, 1, width), lambda h: (h, 0, 0))],
        out_specs=pl.BlockSpec((1, span, TILE, TILE), lambda h: (h, 0, 0, 0)),
        out_shape=jax.ShapeDtypeStruct((heads, span, TILE, TILE), jnp.bfloat16),
        cost_estimate=BRIEF,
        name="toeplitz",
    )(u.reshape(heads, 1, width))

def head_lanes(h, x):
    lane = lax.broadcasted_iota(jnp.int32, x.shape, 1)
    return jnp.where((lane // DK) == h, x, jnp.zeros_like(x))

def dot_nt(a, b):
    return lax.dot_general(a, b, (((1,), (1,)), ((), ())), preferred_element_type=jnp.float32)

def dot_tn(a, b):
    return lax.dot_general(a, b, (((0,), (0,)), ((), ())), preferred_element_type=jnp.float32)

def dot_nn(a, b):
    return lax.dot_general(a, b, (((1,), (0,)), ((), ())), preferred_element_type=jnp.float32)

def key_chunks(parts, rows, chunk):
    return [(i, s) for i in range(parts) for s in range(0, rows, chunk)]

def chunk_scores(pos_ref, k_chunk, q_head, bias_ref, h, c, chunk, blk, q_rows):
    n = chunk // blk
    sub = blk // TILE
    nq = q_rows // blk
    s = dot_nt(k_chunk, q_head)
    half = bias_ref.shape[1] // 2
    rows = []
    for kb in range(n):
        kpos = pos_ref[1 + nq + c * n + kb]
        for kk in range(sub):
            cols = []
            for qb in range(nq):
                e0 = (kpos - pos_ref[1 + qb]) + half + kk
                for qq in range(sub):
                    cols.append(bias_ref[h, e0 - qq])
            rows.append(jnp.concatenate(cols, axis=1))
    bias = jnp.concatenate(rows, axis=0).astype(jnp.float32)
    s = s + bias
    valid = []
    for kb in range(n):
        limit = pos_ref[0] - pos_ref[1 + nq + c * n + kb] * TILE
        valid.append(lax.broadcasted_iota(jnp.int32, (blk, 1), 0) < limit)
    ok = valid[0] if n == 1 else jnp.concatenate([v.astype(jnp.int32) for v in valid], axis=0) > 0
    return s, ok

def attn_fwd_kernel(parts, chunk, blk, pos_ref, q_ref, *refs):
    k_refs, v_refs = refs[:parts], refs[parts:2 * parts]
    bias_ref, o_ref, lse_ref, s_ref = refs[2 * parts:]
    q_rows = q_ref.shape[0]
    rows = k_refs[0].shape[0]
    chunks = key_chunks(parts, rows, chunk)
    outs = []
    for h in range(2):
        qh = head_lanes(h, q_ref[...])
        top = None
        for c, (i, s0) in enumerate(chunks):
            s, ok = chunk_scores(pos_ref, k_refs[i][s0:s0 + chunk, :], qh, bias_ref, h, c, chunk, blk, q_rows)
            s = jnp.where(ok, s, NEGATIVE)
            s_ref[c * chunk:(c + 1) * chunk, :] = s
            m = jnp.max(s, axis=0, keepdims=True)
            top = m if top is None else jnp.maximum(top, m)
        total = jnp.zeros((1, q_rows), jnp.float32)
        acc = jnp.zeros((2 * DK, q_rows), jnp.float32)
        for c, (i, s0) in enumerate(chunks):
            p = jnp.exp(s_ref[c * chunk:(c + 1) * chunk, :] - top)
            total = total + jnp.sum(p, axis=0, keepdims=True)
            acc = acc + dot_tn(v_refs[i][s0:s0 + chunk, :], p.astype(jnp.bfloat16))
        outs.append((acc / total)[h * DK:(h + 1) * DK])
        lse_ref[0, h:h + 1, :] = top + jnp.log(total)
    o_ref[...] = jnp.concatenate(outs, axis=0).T.astype(o_ref.dtype)

def attn_fwd(pos, q, ks, vs, bias, blk):
    q_rows, width = q.shape
    parts, rows = len(ks), ks[0].shape[0]
    keys = parts * rows
    heads = width // DK
    span = bias.shape[1]
    chunk = min(256, rows)
    spec_q = pl.BlockSpec((q_rows, 2 * DK), lambda p, s: (0, p))
    spec_k = pl.BlockSpec((rows, 2 * DK), lambda p, s: (0, p))
    o, lse = pl.pallas_call(
        functools.partial(attn_fwd_kernel, parts, chunk, blk),
        grid_spec=pltpu.PrefetchScalarGridSpec(
            num_scalar_prefetch=1,
            grid=(heads // 2,),
            in_specs=[spec_q] + [spec_k] * (2 * parts) + [pl.BlockSpec((2, span, TILE, TILE), lambda p, s: (p, 0, 0, 0))],
            out_specs=[spec_q, pl.BlockSpec((1, 2, q_rows), lambda p, s: (p, 0, 0))],
            scratch_shapes=[pltpu.VMEM((keys, q_rows), jnp.float32)],
        ),
        out_shape=[jax.ShapeDtypeStruct((q_rows, width), jnp.bfloat16), jax.ShapeDtypeStruct((heads // 2, 2, q_rows), jnp.float32)],
        compiler_params=pltpu.CompilerParams(vmem_limit_bytes=48 << 20),
        cost_estimate=BRIEF,
        name="attn_fwd",
    )(pos, q, *ks, *vs, bias)
    return o, lse

def skew_rows(x):
    width = 2 * x.shape[1]
    x = jnp.concatenate([jnp.zeros_like(x), x], axis=1)
    rows = x.shape[0]
    while rows > 8:
        rows //= 2
        x = x[:rows] + pltpu.roll(x[rows:], width - rows, 1)
    row = lax.broadcasted_iota(jnp.int32, x.shape, 0)
    for bit in (1, 2, 4):
        x = jnp.where((row & bit) != 0, pltpu.roll(x, width - bit, 1), x)
    return x

def attn_bwd_kernel(parts, chunk, blk, pos_ref, q_ref, do_ref, o_ref, lse_ref, *refs):
    k_refs, v_refs = refs[:parts], refs[parts:2 * parts]
    bias_ref, dq_ref = refs[2 * parts:2 * parts + 2]
    dk_refs, dv_refs = refs[2 * parts + 2:3 * parts + 2], refs[3 * parts + 2:4 * parts + 2]
    d_ref, e_ref = refs[4 * parts + 2:]
    q_rows = q_ref.shape[0]
    rows = k_refs[0].shape[0]
    chunks = key_chunks(parts, rows, chunk)
    span = bias_ref.shape[1]
    half = span // 2
    n, sub, nq = chunk // blk, blk // TILE, q_rows // blk
    prod = (do_ref[...].astype(jnp.float32) * o_ref[...].astype(jnp.float32)).T
    outs = []
    for h in range(2):
        qh = head_lanes(h, q_ref[...])
        doh = head_lanes(h, do_ref[...])
        inner = jnp.sum(prod[h * DK:(h + 1) * DK], axis=0, keepdims=True)
        lse = lse_ref[0, h:h + 1, :]
        acc = jnp.zeros((2 * DK, q_rows), jnp.float32)
        e_ref[...] = jnp.zeros_like(e_ref)
        for c, (i, s0) in enumerate(chunks):
            k_chunk = k_refs[i][s0:s0 + chunk, :]
            s, ok = chunk_scores(pos_ref, k_chunk, qh, bias_ref, h, c, chunk, blk, q_rows)
            p = jnp.where(ok, jnp.exp(s - lse), 0.0)
            dp = dot_nt(v_refs[i][s0:s0 + chunk, :], doh)
            ds = p * (dp - inner)
            dsb = ds.astype(jnp.bfloat16)
            dv = dot_nn(p.astype(jnp.bfloat16), doh)
            dk = dot_nn(dsb, qh)
            at = pl.ds(s0, chunk)
            if h == 0:
                dk_refs[i][at, :] = dk.astype(jnp.bfloat16)
                dv_refs[i][at, :] = dv.astype(jnp.bfloat16)
            else:
                dk_refs[i][at, :] = (dk_refs[i][at, :].astype(jnp.float32) + dk).astype(jnp.bfloat16)
                dv_refs[i][at, :] = (dv_refs[i][at, :].astype(jnp.float32) + dv).astype(jnp.bfloat16)
            acc = acc + dot_tn(k_chunk, dsb)
            for kb in range(n):
                kpos = pos_ref[1 + nq + c * n + kb]
                for qb in range(nq):
                    e0 = (kpos - pos_ref[1 + qb]) + half
                    for d in range(1 - sub, sub):
                        tot = None
                        for kk in range(sub):
                            qq = kk - d
                            if 0 <= qq < sub:
                                r0, c0 = kb * blk + kk * TILE, qb * blk + qq * TILE
                                t = ds[r0:r0 + TILE, c0:c0 + TILE]
                                tot = t if tot is None else tot + t
                        e_ref[e0 + d] += tot
        outs.append(acc[h * DK:(h + 1) * DK])
        pieces = [jnp.zeros((1, TILE), jnp.float32) for _ in range(span + 1)]
        for e in range(span):
            r = jnp.sum(skew_rows(e_ref[e]), axis=0, keepdims=True)
            b = span - 1 - e
            pieces[b] = pieces[b] + r[:, :TILE]
            pieces[b + 1] = pieces[b + 1] + r[:, TILE:]
        d_ref[0, h:h + 1, :] = jnp.concatenate(pieces, axis=1)
    dq_ref[...] = jnp.concatenate(outs, axis=0).T.astype(dq_ref.dtype)

def attn_bwd(pos, q, do, o, lse, ks, vs, bias, blk, share, shares):
    q_rows, width = q.shape
    parts, rows = len(ks), ks[0].shape[0]
    keys = parts * rows
    heads = width // DK // shares
    width = width // shares
    span = bias.shape[1]
    chunk = min(256, rows)
    first = share * (heads // 2)
    spec_q = pl.BlockSpec((q_rows, 2 * DK), lambda p, s: (0, first + p))
    spec_k = pl.BlockSpec((rows, 2 * DK), lambda p, s: (0, first + p))
    spec_l = pl.BlockSpec((1, 2, q_rows), lambda p, s: (first + p, 0, 0))
    spec_b = pl.BlockSpec((2, span, TILE, TILE), lambda p, s: (first + p, 0, 0, 0))
    out_q = pl.BlockSpec((q_rows, 2 * DK), lambda p, s: (0, p))
    out_k = pl.BlockSpec((rows, 2 * DK), lambda p, s: (0, p))
    out = pl.pallas_call(
        functools.partial(attn_bwd_kernel, parts, chunk, blk),
        grid_spec=pltpu.PrefetchScalarGridSpec(
            num_scalar_prefetch=1,
            grid=(heads // 2,),
            in_specs=[spec_q, spec_q, spec_q, spec_l] + [spec_k] * (2 * parts) + [spec_b],
            out_specs=[out_q] + [out_k] * (2 * parts) + [pl.BlockSpec((1, 2, (span + 1) * TILE), lambda p, s: (p, 0, 0))],
            scratch_shapes=[pltpu.VMEM((span, TILE, TILE), jnp.float32)],
        ),
        out_shape=[jax.ShapeDtypeStruct((q_rows, width), jnp.bfloat16)]
        + [jax.ShapeDtypeStruct((rows, width), jnp.bfloat16)] * (2 * parts)
        + [jax.ShapeDtypeStruct((heads // 2, 2, (span + 1) * TILE), jnp.float32)],
        compiler_params=pltpu.CompilerParams(vmem_limit_bytes=48 << 20),
        cost_estimate=BRIEF,
        name="attn_bwd",
    )(pos, q, do, o, lse, *ks, *vs, bias)
    dq, dks, dvs, d = out[0], out[1:1 + parts], out[1 + parts:1 + 2 * parts], out[-1]
    return dq, dks, dvs, d.reshape(heads, (span + 1) * TILE)


def matmul_rows(left, right):
    return jnp.dot(left, right, preferred_element_type=jnp.float32)


def matmul_left(left, right):
    return lax.dot_general(left, right, (((0,), (0,)), ((), ())), preferred_element_type=jnp.float32)


def matmul_back(left, right):
    return lax.dot_general(left, right, (((1,), (1,)), ((), ())), preferred_element_type=jnp.float32)


def inv_rms(values):
    return lax.rsqrt(jnp.mean(values * values, axis=-1, keepdims=True) + EPS)


def norm_back(grad, values, gain):
    scale = inv_rms(values)
    weighted = gain * grad
    mean = jnp.mean(weighted * values, axis=-1, keepdims=True)
    grad_in = scale * weighted - values * (scale * scale * scale) * mean
    return grad_in, jnp.sum(grad * values * scale, axis=0, keepdims=True)


def mlp_back_kernel(grad_ref, value_ref, gain_ref, outer_ref, inner_ref, slope_ref, pre_ref, out_ref, low_ref, gain_grad_ref, acc_ref, left_ref):
    i = pl.program_id(0)

    @pl.when(i == 0)
    def _():
        left_ref[...] = grad_ref[...].astype(jnp.bfloat16)
        acc_ref[...] = jnp.zeros_like(acc_ref)

    grad_pre = (dot_nt(left_ref[...], outer_ref[...]) * slope_ref[...].astype(jnp.float32)).astype(jnp.bfloat16)
    pre_ref[...] = grad_pre
    acc_ref[...] += dot_nt(grad_pre, inner_ref[...])

    @pl.when(i == pl.num_programs(0) - 1)
    def _():
        grad_in, grad_gain = norm_back(acc_ref[...], value_ref[...], gain_ref[...])
        total = grad_ref[...] + grad_in
        out_ref[...] = total
        low_ref[...] = total.astype(jnp.bfloat16)
        gain_grad_ref[...] = grad_gain


def mlp_back(grad_out, attended, gain, w_outer, w_inner, slope):
    rows, width = grad_out.shape
    wide = w_outer.shape[0]
    tile = 512
    whole = pl.BlockSpec((rows, width), lambda i: (0, 0))
    line = pl.BlockSpec((1, width), lambda i: (0, 0))
    return pl.pallas_call(
        mlp_back_kernel,
        grid=(wide // tile,),
        in_specs=[
            whole,
            whole,
            line,
            pl.BlockSpec((tile, width), lambda i: (i, 0)),
            pl.BlockSpec((width, tile), lambda i: (0, i)),
            pl.BlockSpec((rows, tile), lambda i: (0, i)),
        ],
        out_specs=[pl.BlockSpec((rows, tile), lambda i: (0, i)), whole, whole, line],
        out_shape=[
            jax.ShapeDtypeStruct((rows, wide), jnp.bfloat16),
            jax.ShapeDtypeStruct((rows, width), jnp.float32),
            jax.ShapeDtypeStruct((rows, width), jnp.bfloat16),
            jax.ShapeDtypeStruct((1, width), jnp.float32),
        ],
        scratch_shapes=[pltpu.VMEM((rows, width), jnp.float32), pltpu.VMEM((rows, width), jnp.bfloat16)],
        compiler_params=pltpu.CompilerParams(vmem_limit_bytes=48 << 20),
        cost_estimate=BRIEF,
        name="mlp_back",
    )(grad_out, attended, gain, w_outer, w_inner, slope)


def project_back_kernel(add_ref, value_ref, gain_ref, q_ref, k_ref, v_ref, w_ref, out_ref, gain_grad_ref, acc_ref):
    i = pl.program_id(0)
    for j, r in enumerate((q_ref, k_ref, v_ref)):

        @pl.when(i == j)
        def _(j=j, r=r):
            part = dot_nt(r[...], w_ref[...])
            acc_ref[...] = part if j == 0 else acc_ref[...] + part

    @pl.when(i == 2)
    def _():
        grad_in, grad_gain = norm_back(acc_ref[...], value_ref[...], gain_ref[...])
        out_ref[...] = add_ref[...] + grad_in
        gain_grad_ref[...] = grad_gain


def project_back(grad_attended, x, gain, grad_query, grad_k, grad_v, w):
    rows, width = x.shape
    whole = pl.BlockSpec((rows, width), lambda i: (0, 0))
    line = pl.BlockSpec((1, width), lambda i: (0, 0))
    return pl.pallas_call(
        project_back_kernel,
        grid=(3,),
        in_specs=[whole, whole, line, whole, whole, whole, pl.BlockSpec((width, width), lambda i: (0, i))],
        out_specs=[whole, line],
        out_shape=[jax.ShapeDtypeStruct((rows, width), jnp.float32), jax.ShapeDtypeStruct((1, width), jnp.float32)],
        scratch_shapes=[pltpu.VMEM((rows, width), jnp.float32)],
        compiler_params=pltpu.CompilerParams(vmem_limit_bytes=48 << 20),
        cost_estimate=BRIEF,
        name="project_back",
    )(grad_attended, x, gain, grad_query, grad_k, grad_v, w)


def gelu_pair(pre):
    c = np.float32(np.sqrt(2.0 / np.pi))
    sq = pre * pre
    t = jnp.tanh(c * (pre + 0.044715 * (sq * pre)))
    half = 0.5 * (1.0 + t)
    slope = half + (0.5 * c) * pre * (1.0 - t * t) * (1.0 + 0.134145 * sq)
    return (pre * half).astype(jnp.bfloat16), slope.astype(jnp.bfloat16)


SWAP = [(0, 1), (1, 0)]


class Plan:
    def __init__(self, sizes):
        self.nz, self.ny, self.ns, self.m = sizes
        self.nx = self.ns * self.m
        self.z = lax.axis_index("z")
        self.y = lax.axis_index("y")
        self.s = lax.axis_index("s")
        self.q = lax.axis_index("q")
        self.core = lax.axis_index("core")
        self.x = self.s * self.m + self.q
        self.everywhere = ("z", "y", "s", "q", "core")
        self.axes = {"x": (("s", "q") if self.m > 1 else "s", self.nx, self.x), "y": ("y", self.ny, self.y)}

    def block_of(self, order, n):
        n_z = n % self.nz
        n = n // self.nz
        place = {}
        for name in reversed(order):
            _, size, mine = self.axes[name]
            part = n % size
            n = n // size
            place[name] = part ^ mine if size == 2 else part
        core = n ^ self.core
        return ((n_z * self.ny + place["y"]) * self.nx + place["x"]) * 2 + core

    def permutation(self, order, width):
        depth = width // (self.nz * self.ny * self.nx * 2)
        n = lax.broadcasted_iota(jnp.int32, (width, width), 1)
        i = lax.broadcasted_iota(jnp.int32, (width, width), 0)
        source = self.block_of(order, n // depth) * depth + n % depth
        return (i == source).astype(jnp.bfloat16)

    def take_blocks(self, rows, table):
        return jnp.take(rows.reshape(table.shape[0], -1, rows.shape[1]), table, axis=0).reshape(rows.shape)

    def exchange(self, piece, name):
        return lax.ppermute(piece, name, SWAP)

    def sum_z(self, piece):
        if self.nz == 1:
            return piece[0]
        return lax.psum_scatter(piece, "z", scatter_dimension=0, tiled=False)

    def sum_vector(self, vector):
        for name, size in (("core", 2), ("z", self.nz), ("y", self.ny), ("q", self.m), ("s", self.ns)):
            if size & (size - 1):
                vector = lax.psum(vector, name)
                continue
            step = 1
            while step < size:
                vector = vector + lax.ppermute(vector, name, [(i, i ^ step) for i in range(size)])
                step *= 2
        return vector

    def to_sequences(self, local):
        own = lax.dynamic_index_in_dim(local, self.s, 0, keepdims=False)
        other = lax.dynamic_index_in_dim(local, 1 - self.s, 0, keepdims=False)
        return jnp.concatenate([own, self.exchange(other, "s")], axis=0)

    def from_sequences(self, rows):
        blk = rows.shape[0] // 2
        return self.in_order(rows[:blk], self.exchange(rows[blk:], "s"))

    def in_order(self, own, other):
        first = self.s == 0
        return jnp.stack([jnp.where(first, own, other), jnp.where(first, other, own)], axis=0)

    def gather_keys(self, rows):
        if self.m == 1:
            return [rows, self.exchange(rows, "core")]
        return [lax.all_gather(rows, ("q", "core"), axis=0, tiled=True)]

    def reduce_keys(self, parts):
        if self.m == 1:
            return parts[0].astype(jnp.float32) + self.exchange(parts[1], "core").astype(jnp.float32)
        return lax.psum_scatter(parts[0], ("q", "core"), scatter_dimension=0, tiled=True).astype(jnp.float32)

    def positions(self, length, blk):
        unit = blk // TILE
        mine = [(((self.s ^ j) * self.m + self.q) * 2 + self.core) * unit for j in range(2)]
        if self.m == 1:
            keys = [(((self.s ^ j) * self.m + self.q) * 2 + (self.core ^ c)) * unit for c in range(2) for j in range(2)]
        else:
            keys = [(((self.s ^ j) * self.m + q) * 2 + c) * unit for q in range(self.m) for c in range(2) for j in range(2)]
        return jnp.stack([length] + mine + keys).astype(jnp.int32)


def assemble_kernel(steps, depth, table_ref, *refs):
    i = pl.program_id(0)
    out = refs[-1]
    core, x = table_ref[0], table_ref[1]
    quads = [refs[j:j + 4] for j in range(0, len(refs) - 1, 4)]
    for quad, (start, count) in zip(quads, steps):

        @pl.when(jnp.logical_and(i >= start, i < start + count))
        def _(quad=quad):
            for j, r in enumerate(quad):
                place = (x ^ (j // 2)) * 2 + (core ^ (j % 2))
                out[pl.ds(pl.multiple_of(place * depth, depth), depth), :] = r[...]


def assemble(table, quads, depth):
    width = quads[0][0].shape[1]
    steps, at = [], 0
    for q in quads:
        steps.append((at, q[0].shape[0] // depth))
        at += q[0].shape[0] // depth

    def source_map(start, count):
        return lambda i, t: (jnp.clip(i - start, 0, count - 1), 0)

    return pl.pallas_call(
        functools.partial(assemble_kernel, steps, depth),
        grid_spec=pltpu.PrefetchScalarGridSpec(
            num_scalar_prefetch=1,
            grid=(at,),
            in_specs=[pl.BlockSpec((depth, width), source_map(*s)) for s in steps for _ in range(4)],
            out_specs=pl.BlockSpec((4 * depth, width), lambda i, t: (t[2 + i], 0)),
        ),
        out_shape=jax.ShapeDtypeStruct((at * 4 * depth, width), quads[0][0].dtype),
        compiler_params=pltpu.CompilerParams(vmem_limit_bytes=48 << 20),
        cost_estimate=BRIEF,
        name="assemble",
    )(table, *[r for q in quads for r in q])


class Held:
    def __init__(self, value):
        self.value = value


def tie(main, *held):
    got = lax.optimization_barrier((main,) + tuple(h.value for h in held))
    for h, v in zip(held, got[1:]):
        h.value = v
    return got[0]


class Fetch:
    def __init__(self, plan, shard):
        self.plan, self.shard = plan, Held(shard)
        self.pairs = plan.nx == 2 and plan.ny == 2 and plan.nz % 2 == 0
        self.depth = shard.shape[0]

    def start(self):
        axes = "z" if self.pairs else self.plan.everywhere
        self.near = Held(lax.all_gather(self.shard.value, axes, axis=0, tiled=True))

    def send(self, piece, name):
        return Held(self.plan.exchange(piece.value, name))

    def send_in_plane(self):
        if self.pairs:
            self.by_x, self.by_y, self.near_twin = [self.send(self.near, n) for n in ("s", "y", "core")]

    def a(self, main, following=None):
        main = tie(main, self.near, *([following.shard] if following else []))
        if following:
            following.start()
        self.send_in_plane()
        return main

    def b(self, main):
        if not self.pairs:
            return main
        main = tie(main, self.by_x, self.by_y, self.near_twin)
        half = self.by_x.value.shape[0] // 2
        self.low = Held(self.plan.exchange(self.by_y.value[:half], "s"))
        self.high = Held(self.plan.exchange(self.by_x.value[half:], "y"))
        self.x_twin, self.y_twin = self.send(self.by_x, "core"), self.send(self.by_y, "core")
        return tie(main, self.x_twin, self.y_twin)

    def c(self, main):
        if not self.pairs:
            return main, self.near.value
        plan = self.plan
        main = tie(main, self.low, self.high)
        twins = [self.send(p, "core") for p in (self.low, self.high)]
        main = tie(main, *twins)
        low_twin, high_twin = [t.value for t in twins]
        half = self.low.value.shape[0]
        by_y, y_twin = self.by_y.value, self.y_twin.value
        quads = [
            (self.near.value, self.near_twin.value, self.by_x.value, self.x_twin.value),
            (by_y[:half], y_twin[:half], self.low.value, low_twin),
            (by_y[half:], y_twin[half:], self.high.value, high_twin),
        ]
        z = jnp.arange(plan.nz, dtype=jnp.int32)
        order = jnp.concatenate([z * 2 + plan.y, z * 2 + (1 - plan.y)])
        table = jnp.concatenate([jnp.stack([plan.core, plan.x]).astype(jnp.int32), order.astype(jnp.int32)])
        whole = Held(assemble(table, quads, self.depth))
        main = tie(main, whole)
        return main, whole.value


def add_low(*terms):
    total = terms[0].astype(jnp.float32)
    for t in terms[1:]:
        total = total + t.astype(jnp.float32)
    return total.astype(jnp.bfloat16)


class Chain:
    def __init__(self, plan, product, order, rows):
        self.plan, self.product, self.rows = plan, product, rows
        self.name_a, self.size_a, _ = plan.axes[order[0]]
        self.name_b, self.size_b, _ = plan.axes[order[1]]
        self.pairs = self.size_a == 2 and self.size_b == 2
        self.part = None

    def one(self):
        self.part = Held(self.product(self.rows // 2, self.rows, None))
        return self.part

    def send_one(self):
        self.other = Held(self.plan.exchange(self.part.value, "core"))

    def two(self):
        half = self.rows // 2
        if self.pairs:
            quarter = half // 2
            self.part = Held(self.product(quarter, half, (self.other.value, quarter)))
        else:
            self.part = Held(self.product(0, half, (self.other.value, 0)))
        return self.part

    def send_two(self):
        if self.pairs:
            self.far = Held(self.plan.exchange(self.part.value, self.name_a))
        else:
            whole = self.part.value.reshape(self.size_a, self.rows // (2 * self.size_a), -1)
            self.far = Held(lax.psum_scatter(whole, self.name_a, scatter_dimension=0, tiled=False))

    def near(self):
        if self.pairs:
            quarter = self.rows // 4
            self.close_by = Held(self.product(0, quarter, (self.other.value, 0)))
            return self.close_by
        return self.far

    def three(self):
        if self.pairs:
            eighth = self.rows // 8
            self.part = Held(add_low(self.close_by.value[eighth:], self.far.value[eighth:]))
        else:
            self.part = self.far
        return self.part

    def send_three(self):
        if self.pairs:
            self.side = Held(self.plan.exchange(self.part.value, self.name_b))
        else:
            whole = self.part.value.reshape(self.size_b, self.part.value.shape[0] // self.size_b, -1)
            self.side = Held(lax.psum_scatter(whole, self.name_b, scatter_dimension=0, tiled=False))

    def close(self):
        nz = self.plan.nz
        if self.pairs:
            eighth = self.rows // 8
            total = add_low(self.close_by.value[:eighth], self.far.value[:eighth], self.side.value)
        else:
            total = self.side.value
        self.piece = Held(total.reshape(nz, total.shape[0] // nz, -1))
        return self.piece


def grad_kernel(lefts, starts, with_add, table_ref, *refs):
    j = pl.program_id(1)
    out = refs[-1]
    at = 0
    for (start, count), number in zip(starts, lefts):
        left_refs, right = refs[at:at + number], refs[at + number]
        at += number + 1

        @pl.when(jnp.logical_and(j >= start, j < start + count))
        def _(left_refs=left_refs, right=right):
            left = left_refs[0][...] if len(left_refs) == 1 else jnp.concatenate([r[...] for r in left_refs], axis=1)
            total = dot_tn(left, right[...])
            if with_add:
                total = total + refs[-2][...].astype(jnp.float32)
            out[...] = total.astype(out.dtype)


def grad_rows(pairs, start, stop, add=None, table=None):
    depth = pairs[0][0].shape[0]
    tile_n = 1024
    count = stop - start
    tile_m = min(512, count)
    specs, operands, lefts, starts, at = [], [], [], [], 0

    def column_map(first, begin, n):
        return lambda i, j, t: (0, first + jnp.clip(j - begin, 0, n - 1))

    for left, right, first, n in pairs:
        if table is None:
            block = start // tile_m
            specs.append(pl.BlockSpec((depth, tile_m), lambda i, j, t, block=block: (0, block + i)))
            operands.append(left)
            lefts.append(1)
        else:
            per = tile_m // TILE
            for k in range(per):
                specs.append(pl.BlockSpec((depth, TILE), lambda i, j, t, k=k, per=per: (0, t[start // TILE + i * per + k])))
                operands.append(left)
            lefts.append(per)
        specs.append(pl.BlockSpec((depth, tile_n), column_map(first, at, n)))
        operands.append(right)
        starts.append((at, n))
        at += n
    if add is not None:
        base = add[1] // tile_m
        specs.append(pl.BlockSpec((tile_m, tile_n), lambda i, j, t: (base + i, j)))
        operands.append(add[0])
    width = at * tile_n
    return pl.pallas_call(
        functools.partial(grad_kernel, lefts, starts, add is not None),
        grid_spec=pltpu.PrefetchScalarGridSpec(
            num_scalar_prefetch=1,
            grid=(count // tile_m, at),
            in_specs=specs,
            out_specs=pl.BlockSpec((tile_m, tile_n), lambda i, j, t: (i, j)),
        ),
        out_shape=jax.ShapeDtypeStruct((count, width), jnp.bfloat16),
        compiler_params=pltpu.CompilerParams(vmem_limit_bytes=32 << 20),
        cost_estimate=BRIEF,
        name="grad_rows",
    )(jnp.zeros((1,), jnp.int32) if table is None else table, *operands)


def project(x, gain, w_qkv):
    normed = (x * inv_rms(x) * gain).astype(jnp.bfloat16)
    return normed, matmul_rows(normed, w_qkv).astype(jnp.bfloat16)


def widen(attended, gain, w_inner):
    normed_mlp = (attended * inv_rms(attended) * gain).astype(jnp.bfloat16)
    return (normed_mlp,) + gelu_pair(matmul_rows(normed_mlp, w_inner))


def backward(plan, grad_out, layers, pos, bias, blk, perms, table, output_half):
    low, f32 = jnp.bfloat16, jnp.float32
    previous = None
    results, diags = [], []
    for weights, saved, orders in layers:
        attn_gain, w_qkv, w_output, mlp_gain, w_inner, w_outer = weights
        x, normed, queries, keys, values, context, log_total, attended, normed_mlp, hidden, slope = saved
        width = x.shape[1]
        grad_low = grad_out.astype(low)
        wide = hidden.shape[1]
        blocks = table[orders[1]]

        def outer_rows(a, b, add, hidden=hidden, grad_low=grad_low, blocks=blocks, wide=wide):
            if wide // blocks.shape[0] == TILE:
                return grad_rows([(hidden, grad_low, 0, 1)], a, b, add, blocks)
            rows = plan.take_blocks(matmul_left(hidden, grad_low).astype(low), blocks)[a:b]
            return rows if add is None else add_low(rows, add[0][add[1]:add[1] + b - a])

        def rows_of(*pairs):
            return lambda a, b, add: grad_rows(pairs, a, b, add)

        outer = Chain(plan, outer_rows, orders[1], wide)
        leaving = Held(output_half)
        late = [previous.outer.side, previous.inner.side] if previous else [leaving]
        grad_out = tie(grad_out, outer.one(), *late)
        outer.send_one()
        if not previous:
            arrived = Held(plan.exchange(leaving.value, "s"))
        grad_pre, grad_attended, attn_low, grad_mlp_gain = mlp_back(grad_out, attended, mlp_gain, w_outer, w_inner, slope)
        late = [previous.qk.far, previous.ov.far] if previous else [arrived]
        grad_pre = tie(grad_pre, outer.other, *late)
        left_m = matmul_rows(normed_mlp, perms[orders[0]]).astype(low)
        inner = Chain(plan, rows_of((left_m, grad_pre, 0, wide // 1024)), orders[0], width)
        late = []
        if previous:
            late = [part for c in (previous.qk, previous.ov) for part in (c.near(), c.three())]
            late += [previous.outer.close(), previous.inner.close()]
        grad_pre = tie(grad_pre, outer.two(), inner.one(), *late)
        outer.send_two()
        inner.send_one()
        if previous:
            previous.qk.send_three()
            previous.ov.send_three()
            previous.sum_mlp(plan)
        late = [previous.qk.side, previous.ov.side] if previous else []
        attn_low = tie(attn_low, inner.other, *late)
        late = [previous.qk.close(), previous.ov.close()] if previous else []
        attn_low = tie(attn_low, inner.two(), *late)
        inner.send_two()
        if previous:
            previous.sum_attn(plan)
        grad_context = matmul_back(attn_low, w_output).astype(low)
        ready = [outer.near(), inner.near()]
        left_c = matmul_rows(context, perms[orders[3]]).astype(low)
        left_n = {o: matmul_rows(normed, perms[o]).astype(low) for o in orders[2:]}
        left_c, n_q, n_v = Held(left_c), Held(left_n[orders[2]]), Held(left_n[orders[3]])
        grad_context = tie(grad_context, *ready, left_c, n_q, n_v)
        left_c, left_n = left_c.value, {orders[2]: n_q.value, orders[3]: n_v.value}
        grad_query, dk, dv, diag = attn_bwd(pos, queries, grad_context, context, log_total, keys, values, bias, blk, 0, 1)
        late = [previous.mlp_sum] if previous else []
        last = tie(dv[-1], outer.far, inner.far, *late)
        grad_k = plan.reduce_keys(dk).astype(low)
        grad_v = plan.reduce_keys(list(dv[:-1]) + [last]).astype(low)
        grad_v = tie(grad_v, outer.three(), inner.three())
        outer.send_three()
        inner.send_three()
        tiles = width // 1024
        qk = Chain(plan, rows_of((left_n[orders[2]], grad_query, 0, tiles), (left_n[orders[2]], grad_k, 0, tiles)), orders[2], width)
        ov = Chain(plan, rows_of((left_c, attn_low, 0, tiles), (left_n[orders[3]], grad_v, 0, tiles)), orders[3], width)
        late = [previous.attn_sum] if previous else []
        grad_v = tie(grad_v, qk.one(), ov.one(), *late)
        qk.send_one()
        ov.send_one()
        grad_out, grad_attn_gain = project_back(grad_attended, x, attn_gain, grad_query, grad_k, grad_v, w_qkv)
        grad_out = tie(grad_out, qk.other, ov.other)
        grad_out = tie(grad_out, qk.two(), ov.two())
        qk.send_two()
        ov.send_two()
        previous = LayerSums(outer, inner, qk, ov, grad_attn_gain, grad_mlp_gain, width)
        results.append(previous)
        diags.append(diag)
    grad_out = tie(grad_out, outer.side, inner.side)
    outer.close()
    inner.close()
    previous.sum_mlp(plan)
    grad_out = tie(grad_out, qk.far, ov.far, qk.near(), ov.near())
    grad_out = tie(grad_out, qk.three(), ov.three())
    qk.send_three()
    ov.send_three()
    qk.close()
    qk.piece.value = tie(qk.piece.value, ov.close(), previous.mlp_sum)
    previous.sum_attn(plan)
    return grad_out, results, diags, arrived.value


class LayerSums:
    def __init__(self, outer, inner, qk, ov, grad_attn_gain, grad_mlp_gain, width):
        self.outer, self.inner, self.qk, self.ov = outer, inner, qk, ov
        self.attn_gain, self.mlp_gain, self.width = grad_attn_gain, grad_mlp_gain, width

    def sum_mlp(self, plan):
        w = self.width
        inner, outer = self.inner.piece.value, self.outer.piece.value
        self.runs, self.depth = inner.shape[2] // w, inner.shape[1]
        stacked = [inner[:, :, i * w:(i + 1) * w] for i in range(self.runs)]
        self.mlp_sum = Held(plan.sum_z(jnp.concatenate(stacked + [outer], axis=1)))

    def sum_attn(self, plan):
        self.attn_sum = Held(plan.sum_z(jnp.concatenate([c.piece.value for c in (self.qk, self.ov)], axis=2)))

    def grads(self):
        w = self.width
        f32 = jnp.float32
        query, key, output, value = [self.attn_sum.value[:, i * w:(i + 1) * w].astype(f32) for i in range(4)]
        both = self.mlp_sum.value.astype(f32)
        d = self.depth
        inner = jnp.concatenate([both[i * d:(i + 1) * d] for i in range(self.runs)], axis=1)
        return [self.attn_gain, query, key, value, output, self.mlp_gain, inner, both[self.runs * d:]]


def body(sizes, inputs, cotangent, lengths, bucket_ids, *params):
    plan = Plan(sizes)
    one, bias_table, two = params[:8], params[8], params[9:]
    blk, width = inputs.shape[1], inputs.shape[2]
    f32, low = jnp.float32, jnp.bfloat16
    gains = jnp.stack([one[0], one[5], two[0], two[5]], axis=1)
    rows = gains.shape[0]
    table_column = jnp.pad(bias_table, (0, rows - bias_table.shape[0]))[:, None] if bias_table.shape[0] < rows else bias_table[:rows, None]
    small = jnp.pad(jnp.concatenate([gains, table_column], axis=1), ((0, 0), (0, TILE - 5)))
    everywhere = plan.everywhere

    length = lax.dynamic_index_in_dim(lengths, plan.s, 0, keepdims=False)
    pos = plan.positions(length, blk)
    row = jnp.arange(blk, dtype=jnp.int32)
    row_pos = jnp.concatenate([row + pos[1] * TILE, row + pos[2] * TILE])
    row_valid = (row_pos < length).astype(f32)[:, None]

    shards = (
        jnp.concatenate([one[1], one[2], one[3], one[4], small], axis=1),
        one[6],
        one[7],
        jnp.concatenate([two[1], two[2], two[3], two[4]], axis=1),
        two[6],
        two[7],
    )
    attn_1, inner_1, outer_1, attn_2, inner_2, outer_2 = [Fetch(plan, piece) for piece in shards]
    attn_1.start()
    x = plan.to_sequences(inputs)
    cotangent = plan.to_sequences(cotangent)
    x = tie(x, inner_1.shard)
    inner_1.start()
    x = attn_1.a(x, outer_1)
    x = attn_1.b(x)
    x = inner_1.a(x, attn_2)
    x, first = attn_1.c(x)
    picks = jnp.eye(8, TILE, dtype=low)
    smalls = matmul_back(picks, first[:, 4 * width:])
    gain = smalls[:4]
    whole_table = smalls[4].reshape(-1, rows)[:, :bias_table.shape[0]].reshape(-1)
    heads = width // DK
    buckets = whole_table.shape[0] // heads
    reversed_ids = jnp.concatenate([jnp.full((1,), -1, jnp.int32), bucket_ids[::-1]])
    indicator = (reversed_ids[None, :] == jnp.arange(buckets, dtype=jnp.int32)[:, None]).astype(low)
    vector = Held(matmul_rows(whole_table.reshape(heads, buckets).astype(low), indicator))
    x_one = x.astype(f32)
    normed_one, qkv = project(x_one, gain[0:1], first[:, :3 * width])
    qkv = inner_1.b(qkv)
    qkv = outer_1.a(qkv, inner_2)
    kv = plan.gather_keys(qkv[:, width:])
    qkv = tie(qkv, vector)
    bias = Held(toeplitz_tiles(vector.value))
    qkv = tie(qkv, bias)
    bias = bias.value
    queries_one = qkv[:, :width]
    keys_one, values_one = [p[:, :width] for p in kv], [p[:, width:] for p in kv]
    context_one, log_one = attn_fwd(pos, queries_one, keys_one, values_one, bias, blk)
    context_one, w_inner_one = inner_1.c(context_one)
    context_one = outer_1.b(context_one)
    context_one = attn_2.a(context_one, outer_2)
    attended_one = x_one + matmul_rows(context_one, first[:, 3 * width:4 * width])
    normed_mlp_one, hidden_one, slope_one = widen(attended_one, gain[1:2], w_inner_one)
    slope_one = Held(slope_one)
    hidden_one = tie(hidden_one, slope_one)
    slope_one = slope_one.value
    hidden_one, w_outer_one = outer_1.c(hidden_one)
    hidden_one = attn_2.b(hidden_one)
    hidden_one = inner_2.a(hidden_one)
    x_two = attended_one + matmul_rows(hidden_one, w_outer_one)
    x_two, third = attn_2.c(x_two)
    normed_two, qkv = project(x_two, gain[2:3], third[:, :3 * width])
    qkv = inner_2.b(qkv)
    qkv = outer_2.a(qkv)
    kv = plan.gather_keys(qkv[:, width:])
    queries_two = qkv[:, :width]
    keys_two, values_two = [p[:, :width] for p in kv], [p[:, width:] for p in kv]
    context_two, log_two = attn_fwd(pos, queries_two, keys_two, values_two, bias, blk)
    context_two, w_inner_two = inner_2.c(context_two)
    context_two = outer_2.b(context_two)
    attended_two = x_two + matmul_rows(context_two, third[:, 3 * width:])
    normed_mlp_two, hidden_two, slope_two = widen(attended_two, gain[3:4], w_inner_two)
    slope_two = Held(slope_two)
    hidden_two = tie(hidden_two, slope_two)
    slope_two = slope_two.value
    hidden_two, w_outer_two = outer_2.c(hidden_two)
    final = attended_two + matmul_rows(hidden_two, w_outer_two)
    output_rows = (final * row_valid).astype(low)
    grad_out = cotangent.astype(f32) * row_valid

    weights_one = (gain[0:1], first, first[:, 3 * width:4 * width], gain[1:2], w_inner_one, w_outer_one)
    weights_two = (gain[2:3], third, third[:, 3 * width:], gain[3:4], w_inner_two, w_outer_two)
    saved_one = (x_one, normed_one, queries_one, keys_one, values_one, context_one, log_one, attended_one, normed_mlp_one, hidden_one, slope_one)
    saved_two = (x_two, normed_two, queries_two, keys_two, values_two, context_two, log_two, attended_two, normed_mlp_two, hidden_two, slope_two)

    xy, yx = ("x", "y"), ("y", "x")
    perms = {o: plan.permutation(o, width) for o in (xy, yx)}
    depth = one[7].shape[0]
    step = TILE if depth % TILE == 0 else depth
    blocks = jnp.arange(saved_one[9].shape[1] // step, dtype=jnp.int32)
    per = depth // step
    table = {o: plan.block_of(o, blocks // per) * per + blocks % per for o in (xy, yx)}
    layers = [(weights_two, saved_two, (xy, yx, yx, xy)), (weights_one, saved_one, (xy, yx, yx, xy))]
    grad_state, sums, diags, arrived = backward(plan, grad_out, layers, pos, bias, blk, perms, table, output_rows[blk:])
    output = plan.in_order(output_rows[:blk], arrived)
    grads_two, grads_one = sums[0].grads(), sums[1].grads()
    input_grad = plan.from_sequences(grad_state.astype(low))

    grad_table = lax.dot_general(diags[0] + diags[1], indicator.astype(f32), (((1,), (1,)), ((), ())), precision=HIGH_PRECISION)
    vectors = jnp.concatenate([grads_one[0][0], grads_one[5][0], grads_two[0][0], grads_two[5][0], grad_table.reshape(-1)])
    held = Held(vectors)
    grad_state = tie(grad_state, held)
    vectors = plan.sum_vector(held.value)
    device = ((plan.z * plan.ny + plan.y) * plan.nx + plan.x) * 2 + plan.core

    def share(start, count):
        return lax.dynamic_slice_in_dim(vectors, start + device * count, count, 0)

    gain_grads = [share(i * width, rows) for i in range(4)]
    table_grad = share(4 * width, bias_table.shape[0])
    return (
        output,
        input_grad,
        gain_grads[0],
        *grads_one[1:5],
        gain_grads[1],
        *grads_one[6:],
        table_grad,
        gain_grads[2],
        *grads_two[1:5],
        gain_grads[3],
        *grads_two[6:],
    )


def solution(mesh):
    dp, cp = mesh.shape["dp"], mesh.shape["cp"]
    nx = cp // 2
    ny = nx if dp % nx == 0 else 1

    def run(inputs, *rest):
        ns = inputs.shape[0] // dp
        assert ns == 2 and nx % ns == 0
        sizes = (dp // ny, ny, ns, nx // ns)
        finer = Mesh(mesh.devices.reshape(*sizes, 2), ("z", "y", "s", "q", "core"))
        dpn, cpn = ("z", "y"), ("s", "q", "core")
        tokens = P(dpn, cpn, None)
        vector, matrix = P(dpn + cpn), P(dpn + cpn, None)
        layer = (vector, matrix, matrix, matrix, matrix, vector, matrix, matrix)
        return jax.shard_map(
            functools.partial(body, sizes),
            mesh=finer,
            in_specs=(tokens, tokens, P(dpn), P()) + layer + (vector,) + layer,
            out_specs=(tokens, tokens) + layer + (vector,) + layer,
            check_vma=False,
        )(inputs, *rest)

    return run
```

```python
import functools

import jax
import jax.numpy as jnp
import numpy as np
from jax import lax
from jax.experimental import pallas as pl
from jax.experimental.pallas import tpu as pltpu
from jax.sharding import Mesh
from jax.sharding import PartitionSpec as P

DK = 64
TILE = 128
EPS = 1e-06
NEGATIVE = -1e30
HIGH_PRECISION = lax.Precision.HIGHEST
BRIEF = pl.CostEstimate(flops=1024, bytes_accessed=1024, transcendentals=0)


def toeplitz_kernel(span, u_ref, t_ref):
    for e in range(span):
        base = TILE * (span - 1 - e)
        w = jnp.broadcast_to(u_ref[0, :, base:base + 2 * TILE], (TILE, 2 * TILE))
        t_ref[0, e] = pltpu.roll(w, TILE, 1, stride=1, stride_axis=0)[:, :TILE].astype(t_ref.dtype)

def toeplitz_tiles(u):
    heads, width = u.shape
    span = width // TILE - 1
    return pl.pallas_call(
        functools.partial(toeplitz_kernel, span),
        grid=(heads,),
        in_specs=[pl.BlockSpec((1, 1, width), lambda h: (h, 0, 0))],
        out_specs=pl.BlockSpec((1, span, TILE, TILE), lambda h: (h, 0, 0, 0)),
        out_shape=jax.ShapeDtypeStruct((heads, span, TILE, TILE), jnp.bfloat16),
        cost_estimate=BRIEF,
        name="toeplitz",
    )(u.reshape(heads, 1, width))

def head_lanes(h, x):
    lane = lax.broadcasted_iota(jnp.int32, x.shape, 1)
    return jnp.where((lane // DK) == h, x, jnp.zeros_like(x))

def dot_nt(a, b):
    return lax.dot_general(a, b, (((1,), (1,)), ((), ())), preferred_element_type=jnp.float32)

def dot_tn(a, b):
    return lax.dot_general(a, b, (((0,), (0,)), ((), ())), preferred_element_type=jnp.float32)

def dot_nn(a, b):
    return lax.dot_general(a, b, (((1,), (0,)), ((), ())), preferred_element_type=jnp.float32)

def key_chunks(parts, rows, chunk):
    return [(i, s) for i in range(parts) for s in range(0, rows, chunk)]

def chunk_scores(pos_ref, k_chunk, q_head, bias_ref, h, c, chunk, blk, q_rows):
    n = chunk // blk
    sub = blk // TILE
    nq = q_rows // blk
    s = dot_nt(k_chunk, q_head)
    half = bias_ref.shape[1] // 2
    rows = []
    for kb in range(n):
        kpos = pos_ref[1 + nq + c * n + kb]
        for kk in range(sub):
            cols = []
            for qb in range(nq):
                e0 = (kpos - pos_ref[1 + qb]) + half + kk
                for qq in range(sub):
                    cols.append(bias_ref[h, e0 - qq])
            rows.append(jnp.concatenate(cols, axis=1))
    bias = jnp.concatenate(rows, axis=0).astype(jnp.float32)
    s = s + bias
    valid = []
    for kb in range(n):
        limit = pos_ref[0] - pos_ref[1 + nq + c * n + kb] * TILE
        valid.append(lax.broadcasted_iota(jnp.int32, (blk, 1), 0) < limit)
    ok = valid[0] if n == 1 else jnp.concatenate([v.astype(jnp.int32) for v in valid], axis=0) > 0
    return s, ok

def attn_fwd_kernel(parts, chunk, blk, pos_ref, q_ref, *refs):
    k_refs, v_refs = refs[:parts], refs[parts:2 * parts]
    bias_ref, o_ref, lse_ref, s_ref = refs[2 * parts:]
    q_rows = q_ref.shape[0]
    rows = k_refs[0].shape[0]
    chunks = key_chunks(parts, rows, chunk)
    outs = []
    for h in range(2):
        qh = head_lanes(h, q_ref[...])
        top = None
        for c, (i, s0) in enumerate(chunks):
            s, ok = chunk_scores(pos_ref, k_refs[i][s0:s0 + chunk, :], qh, bias_ref, h, c, chunk, blk, q_rows)
            s = jnp.where(ok, s, NEGATIVE)
            s_ref[c * chunk:(c + 1) * chunk, :] = s
            m = jnp.max(s, axis=0, keepdims=True)
            top = m if top is None else jnp.maximum(top, m)
        total = jnp.zeros((1, q_rows), jnp.float32)
        acc = jnp.zeros((2 * DK, q_rows), jnp.float32)
        for c, (i, s0) in enumerate(chunks):
            p = jnp.exp(s_ref[c * chunk:(c + 1) * chunk, :] - top)
            total = total + jnp.sum(p, axis=0, keepdims=True)
            acc = acc + dot_tn(v_refs[i][s0:s0 + chunk, :], p.astype(jnp.bfloat16))
        outs.append((acc / total)[h * DK:(h + 1) * DK])
        lse_ref[0, h:h + 1, :] = top + jnp.log(total)
    o_ref[...] = jnp.concatenate(outs, axis=0).T.astype(o_ref.dtype)

def attn_fwd(pos, q, ks, vs, bias, blk):
    q_rows, width = q.shape
    parts, rows = len(ks), ks[0].shape[0]
    keys = parts * rows
    heads = width // DK
    span = bias.shape[1]
    chunk = min(256, rows)
    spec_q = pl.BlockSpec((q_rows, 2 * DK), lambda p, s: (0, p))
    spec_k = pl.BlockSpec((rows, 2 * DK), lambda p, s: (0, p))
    o, lse = pl.pallas_call(
        functools.partial(attn_fwd_kernel, parts, chunk, blk),
        grid_spec=pltpu.PrefetchScalarGridSpec(
            num_scalar_prefetch=1,
            grid=(heads // 2,),
            in_specs=[spec_q] + [spec_k] * (2 * parts) + [pl.BlockSpec((2, span, TILE, TILE), lambda p, s: (p, 0, 0, 0))],
            out_specs=[spec_q, pl.BlockSpec((1, 2, q_rows), lambda p, s: (p, 0, 0))],
            scratch_shapes=[pltpu.VMEM((keys, q_rows), jnp.float32)],
        ),
        out_shape=[jax.ShapeDtypeStruct((q_rows, width), jnp.bfloat16), jax.ShapeDtypeStruct((heads // 2, 2, q_rows), jnp.float32)],
        compiler_params=pltpu.CompilerParams(vmem_limit_bytes=48 << 20),
        cost_estimate=BRIEF,
        name="attn_fwd",
    )(pos, q, *ks, *vs, bias)
    return o, lse

def skew_rows(x):
    width = 2 * x.shape[1]
    x = jnp.concatenate([jnp.zeros_like(x), x], axis=1)
    rows = x.shape[0]
    while rows > 8:
        rows //= 2
        x = x[:rows] + pltpu.roll(x[rows:], width - rows, 1)
    row = lax.broadcasted_iota(jnp.int32, x.shape, 0)
    for bit in (1, 2, 4):
        x = jnp.where((row & bit) != 0, pltpu.roll(x, width - bit, 1), x)
    return x

def attn_bwd_kernel(parts, chunk, blk, pos_ref, q_ref, do_ref, o_ref, lse_ref, *refs):
    k_refs, v_refs = refs[:parts], refs[parts:2 * parts]
    bias_ref, dq_ref = refs[2 * parts:2 * parts + 2]
    dk_refs, dv_refs = refs[2 * parts + 2:3 * parts + 2], refs[3 * parts + 2:4 * parts + 2]
    d_ref, e_ref = refs[4 * parts + 2:]
    q_rows = q_ref.shape[0]
    rows = k_refs[0].shape[0]
    chunks = key_chunks(parts, rows, chunk)
    span = bias_ref.shape[1]
    half = span // 2
    n, sub, nq = chunk // blk, blk // TILE, q_rows // blk
    prod = (do_ref[...].astype(jnp.float32) * o_ref[...].astype(jnp.float32)).T
    outs = []
    for h in range(2):
        qh = head_lanes(h, q_ref[...])
        doh = head_lanes(h, do_ref[...])
        inner = jnp.sum(prod[h * DK:(h + 1) * DK], axis=0, keepdims=True)
        lse = lse_ref[0, h:h + 1, :]
        acc = jnp.zeros((2 * DK, q_rows), jnp.float32)
        e_ref[...] = jnp.zeros_like(e_ref)
        for c, (i, s0) in enumerate(chunks):
            k_chunk = k_refs[i][s0:s0 + chunk, :]
            s, ok = chunk_scores(pos_ref, k_chunk, qh, bias_ref, h, c, chunk, blk, q_rows)
            p = jnp.where(ok, jnp.exp(s - lse), 0.0)
            dp = dot_nt(v_refs[i][s0:s0 + chunk, :], doh)
            ds = p * (dp - inner)
            dsb = ds.astype(jnp.bfloat16)
            dv = dot_nn(p.astype(jnp.bfloat16), doh)
            dk = dot_nn(dsb, qh)
            at = pl.ds(s0, chunk)
            if h == 0:
                dk_refs[i][at, :] = dk.astype(jnp.bfloat16)
                dv_refs[i][at, :] = dv.astype(jnp.bfloat16)
            else:
                dk_refs[i][at, :] = (dk_refs[i][at, :].astype(jnp.float32) + dk).astype(jnp.bfloat16)
                dv_refs[i][at, :] = (dv_refs[i][at, :].astype(jnp.float32) + dv).astype(jnp.bfloat16)
            acc = acc + dot_tn(k_chunk, dsb)
            for kb in range(n):
                kpos = pos_ref[1 + nq + c * n + kb]
                for qb in range(nq):
                    e0 = (kpos - pos_ref[1 + qb]) + half
                    for d in range(1 - sub, sub):
                        tot = None
                        for kk in range(sub):
                            qq = kk - d
                            if 0 <= qq < sub:
                                r0, c0 = kb * blk + kk * TILE, qb * blk + qq * TILE
                                t = ds[r0:r0 + TILE, c0:c0 + TILE]
                                tot = t if tot is None else tot + t
                        e_ref[e0 + d] += tot
        outs.append(acc[h * DK:(h + 1) * DK])
        pieces = [jnp.zeros((1, TILE), jnp.float32) for _ in range(span + 1)]
        for e in range(span):
            r = jnp.sum(skew_rows(e_ref[e]), axis=0, keepdims=True)
            b = span - 1 - e
            pieces[b] = pieces[b] + r[:, :TILE]
            pieces[b + 1] = pieces[b + 1] + r[:, TILE:]
        d_ref[0, h:h + 1, :] = jnp.concatenate(pieces, axis=1)
    dq_ref[...] = jnp.concatenate(outs, axis=0).T.astype(dq_ref.dtype)

def attn_bwd(pos, q, do, o, lse, ks, vs, bias, blk, share, shares):
    q_rows, width = q.shape
    parts, rows = len(ks), ks[0].shape[0]
    keys = parts * rows
    heads = width // DK // shares
    width = width // shares
    span = bias.shape[1]
    chunk = min(256, rows)
    first = share * (heads // 2)
    spec_q = pl.BlockSpec((q_rows, 2 * DK), lambda p, s: (0, first + p))
    spec_k = pl.BlockSpec((rows, 2 * DK), lambda p, s: (0, first + p))
    spec_l = pl.BlockSpec((1, 2, q_rows), lambda p, s: (first + p, 0, 0))
    spec_b = pl.BlockSpec((2, span, TILE, TILE), lambda p, s: (first + p, 0, 0, 0))
    out_q = pl.BlockSpec((q_rows, 2 * DK), lambda p, s: (0, p))
    out_k = pl.BlockSpec((rows, 2 * DK), lambda p, s: (0, p))
    out = pl.pallas_call(
        functools.partial(attn_bwd_kernel, parts, chunk, blk),
        grid_spec=pltpu.PrefetchScalarGridSpec(
            num_scalar_prefetch=1,
            grid=(heads // 2,),
            in_specs=[spec_q, spec_q, spec_q, spec_l] + [spec_k] * (2 * parts) + [spec_b],
            out_specs=[out_q] + [out_k] * (2 * parts) + [pl.BlockSpec((1, 2, (span + 1) * TILE), lambda p, s: (p, 0, 0))],
            scratch_shapes=[pltpu.VMEM((span, TILE, TILE), jnp.float32)],
        ),
        out_shape=[jax.ShapeDtypeStruct((q_rows, width), jnp.bfloat16)]
        + [jax.ShapeDtypeStruct((rows, width), jnp.bfloat16)] * (2 * parts)
        + [jax.ShapeDtypeStruct((heads // 2, 2, (span + 1) * TILE), jnp.float32)],
        compiler_params=pltpu.CompilerParams(vmem_limit_bytes=48 << 20),
        cost_estimate=pl.CostEstimate(flops=40 * q_rows * keys * width, bytes_accessed=8 * keys * width + 8 * q_rows * width, transcendentals=heads * q_rows * keys),
        name="attn_bwd",
    )(pos, q, do, o, lse, *ks, *vs, bias)
    dq, dks, dvs, d = out[0], out[1:1 + parts], out[1 + parts:1 + 2 * parts], out[-1]
    return dq, dks, dvs, d.reshape(heads, (span + 1) * TILE)


def matmul_rows(left, right):
    return jnp.dot(left, right, preferred_element_type=jnp.float32)


def matmul_left(left, right):
    return lax.dot_general(left, right, (((0,), (0,)), ((), ())), preferred_element_type=jnp.float32)


def matmul_back(left, right):
    return lax.dot_general(left, right, (((1,), (1,)), ((), ())), preferred_element_type=jnp.float32)


def inv_rms(values):
    return lax.rsqrt(jnp.mean(values * values, axis=-1, keepdims=True) + EPS)


def norm_back(grad, values, gain):
    scale = inv_rms(values)
    weighted = gain * grad
    mean = jnp.mean(weighted * values, axis=-1, keepdims=True)
    grad_in = scale * weighted - values * (scale * scale * scale) * mean
    return grad_in, jnp.sum(grad * values * scale, axis=0, keepdims=True)


def mlp_back_kernel(grad_ref, value_ref, gain_ref, outer_ref, inner_ref, slope_ref, pre_ref, out_ref, low_ref, gain_grad_ref, acc_ref, left_ref):
    i = pl.program_id(0)

    @pl.when(i == 0)
    def _():
        left_ref[...] = grad_ref[...].astype(jnp.bfloat16)
        acc_ref[...] = jnp.zeros_like(acc_ref)

    grad_pre = (dot_nt(left_ref[...], outer_ref[...]) * slope_ref[...].astype(jnp.float32)).astype(jnp.bfloat16)
    pre_ref[...] = grad_pre
    acc_ref[...] += dot_nt(grad_pre, inner_ref[...])

    @pl.when(i == pl.num_programs(0) - 1)
    def _():
        grad_in, grad_gain = norm_back(acc_ref[...], value_ref[...], gain_ref[...])
        total = grad_ref[...] + grad_in
        out_ref[...] = total
        low_ref[...] = total.astype(jnp.bfloat16)
        gain_grad_ref[...] = grad_gain


def mlp_back(grad_out, attended, gain, w_outer, w_inner, slope):
    rows, width = grad_out.shape
    wide = w_outer.shape[0]
    tile = min(1024, wide)
    whole = pl.BlockSpec((rows, width), lambda i: (0, 0))
    line = pl.BlockSpec((1, width), lambda i: (0, 0))
    return pl.pallas_call(
        mlp_back_kernel,
        grid=(wide // tile,),
        in_specs=[
            whole,
            whole,
            line,
            pl.BlockSpec((tile, width), lambda i: (i, 0)),
            pl.BlockSpec((width, tile), lambda i: (0, i)),
            pl.BlockSpec((rows, tile), lambda i: (0, i)),
        ],
        out_specs=[pl.BlockSpec((rows, tile), lambda i: (0, i)), whole, whole, line],
        out_shape=[
            jax.ShapeDtypeStruct((rows, wide), jnp.bfloat16),
            jax.ShapeDtypeStruct((rows, width), jnp.float32),
            jax.ShapeDtypeStruct((rows, width), jnp.bfloat16),
            jax.ShapeDtypeStruct((1, width), jnp.float32),
        ],
        scratch_shapes=[pltpu.VMEM((rows, width), jnp.float32), pltpu.VMEM((rows, width), jnp.bfloat16)],
        compiler_params=pltpu.CompilerParams(vmem_limit_bytes=48 << 20),
        cost_estimate=BRIEF,
        name="mlp_back",
    )(grad_out, attended, gain, w_outer, w_inner, slope)


def project_back_kernel(add_ref, value_ref, gain_ref, q_ref, k_ref, v_ref, w_ref, out_ref, gain_grad_ref, acc_ref):
    i = pl.program_id(0)
    for j, r in enumerate((q_ref, k_ref, v_ref)):

        @pl.when(i == j)
        def _(j=j, r=r):
            part = dot_nt(r[...], w_ref[...])
            acc_ref[...] = part if j == 0 else acc_ref[...] + part

    @pl.when(i == 2)
    def _():
        grad_in, grad_gain = norm_back(acc_ref[...], value_ref[...].astype(jnp.float32), gain_ref[...])
        out_ref[...] = add_ref[...] + grad_in
        gain_grad_ref[...] = grad_gain


def project_back(grad_attended, x, gain, grad_query, grad_k, grad_v, w):
    rows, width = x.shape
    whole = pl.BlockSpec((rows, width), lambda i: (0, 0))
    line = pl.BlockSpec((1, width), lambda i: (0, 0))
    return pl.pallas_call(
        project_back_kernel,
        grid=(3,),
        in_specs=[whole, whole, line, whole, whole, whole, pl.BlockSpec((width, width), lambda i: (0, i))],
        out_specs=[whole, line],
        out_shape=[jax.ShapeDtypeStruct((rows, width), jnp.float32), jax.ShapeDtypeStruct((1, width), jnp.float32)],
        scratch_shapes=[pltpu.VMEM((rows, width), jnp.float32)],
        compiler_params=pltpu.CompilerParams(vmem_limit_bytes=48 << 20),
        cost_estimate=BRIEF,
        name="project_back",
    )(grad_attended, x, gain, grad_query, grad_k, grad_v, w)


def gelu_pair(pre):
    c = np.float32(np.sqrt(2.0 / np.pi))
    sq = pre * pre
    t = jnp.tanh(c * (pre + 0.044715 * (sq * pre)))
    half = 0.5 * (1.0 + t)
    slope = half + (0.5 * c) * pre * (1.0 - t * t) * (1.0 + 0.134145 * sq)
    return (pre * half).astype(jnp.bfloat16), slope.astype(jnp.bfloat16)


SWAP = [(0, 1), (1, 0)]


class Plan:
    def __init__(self, sizes):
        self.nz, self.ny, self.ns, self.m = sizes
        self.nx = self.ns * self.m
        self.z = lax.axis_index("z")
        self.y = lax.axis_index("y")
        self.s = lax.axis_index("s")
        self.q = lax.axis_index("q")
        self.core = lax.axis_index("core")
        self.x = self.s * self.m + self.q
        self.everywhere = ("z", "y", "s", "q", "core")
        self.axes = {"x": (("s", "q") if self.m > 1 else "s", self.nx, self.x), "y": ("y", self.ny, self.y)}

    def block_of(self, order, n):
        n_z = n % self.nz
        n = n // self.nz
        place = {}
        for name in reversed(order):
            _, size, mine = self.axes[name]
            part = n % size
            n = n // size
            place[name] = part ^ mine if size == 2 else part
        core = n ^ self.core
        return ((n_z * self.ny + place["y"]) * self.nx + place["x"]) * 2 + core

    def permutation(self, order, width):
        depth = width // (self.nz * self.ny * self.nx * 2)
        n = lax.broadcasted_iota(jnp.int32, (width, width), 1)
        i = lax.broadcasted_iota(jnp.int32, (width, width), 0)
        source = self.block_of(order, n // depth) * depth + n % depth
        return (i == source).astype(jnp.bfloat16)

    def take_blocks(self, rows, table):
        return jnp.take(rows.reshape(table.shape[0], -1, rows.shape[1]), table, axis=0).reshape(rows.shape)

    def exchange(self, piece, name):
        return lax.ppermute(piece, name, SWAP)

    def sum_z(self, piece):
        if self.nz == 1:
            return piece[0]
        return lax.psum_scatter(piece, "z", scatter_dimension=0, tiled=False)

    def sum_vector(self, vector):
        for name, size in (("core", 2), ("z", self.nz), ("y", self.ny), ("q", self.m), ("s", self.ns)):
            if size & (size - 1):
                vector = lax.psum(vector, name)
                continue
            step = 1
            while step < size:
                vector = vector + lax.ppermute(vector, name, [(i, i ^ step) for i in range(size)])
                step *= 2
        return vector

    def to_sequences(self, local):
        own = lax.dynamic_index_in_dim(local, self.s, 0, keepdims=False)
        other = lax.dynamic_index_in_dim(local, 1 - self.s, 0, keepdims=False)
        return jnp.concatenate([own, self.exchange(other, "s")], axis=0)

    def from_sequences(self, rows):
        blk = rows.shape[0] // 2
        return self.in_order(rows[:blk], self.exchange(rows[blk:], "s"))

    def in_order(self, own, other):
        first = self.s == 0
        return jnp.stack([jnp.where(first, own, other), jnp.where(first, other, own)], axis=0)

    def gather_keys(self, rows):
        if self.m == 1:
            return [rows, self.exchange(rows, "core")]
        return [lax.all_gather(rows, ("q", "core"), axis=0, tiled=True)]

    def reduce_keys(self, parts):
        if self.m == 1:
            return add_rows(parts[0].shape[0], (parts[0], 0), (self.exchange(parts[1], "core"), 0))
        return lax.psum_scatter(parts[0], ("q", "core"), scatter_dimension=0, tiled=True).astype(jnp.float32)

    def positions(self, length, blk):
        unit = blk // TILE
        mine = [(((self.s ^ j) * self.m + self.q) * 2 + self.core) * unit for j in range(2)]
        if self.m == 1:
            keys = [(((self.s ^ j) * self.m + self.q) * 2 + (self.core ^ c)) * unit for c in range(2) for j in range(2)]
        else:
            keys = [(((self.s ^ j) * self.m + q) * 2 + c) * unit for q in range(self.m) for c in range(2) for j in range(2)]
        return jnp.stack([length] + mine + keys).astype(jnp.int32)


def assemble_kernel(steps, depth, table_ref, *refs):
    i = pl.program_id(0)
    out = refs[-1]
    core, x = table_ref[0], table_ref[1]
    quads = [refs[j:j + 4] for j in range(0, len(refs) - 1, 4)]
    for quad, (start, count) in zip(quads, steps):

        @pl.when(jnp.logical_and(i >= start, i < start + count))
        def _(quad=quad):
            for j, r in enumerate(quad):
                place = (x ^ (j // 2)) * 2 + (core ^ (j % 2))
                out[pl.ds(pl.multiple_of(place * depth, depth), depth), :] = r[...]


def assemble(table, quads, depth):
    width = quads[0][0].shape[1]
    steps, at = [], 0
    for q in quads:
        steps.append((at, q[0].shape[0] // depth))
        at += q[0].shape[0] // depth

    def source_map(start, count):
        return lambda i, t: (jnp.clip(i - start, 0, count - 1), 0)

    return pl.pallas_call(
        functools.partial(assemble_kernel, steps, depth),
        grid_spec=pltpu.PrefetchScalarGridSpec(
            num_scalar_prefetch=1,
            grid=(at,),
            in_specs=[pl.BlockSpec((depth, width), source_map(*s)) for s in steps for _ in range(4)],
            out_specs=pl.BlockSpec((4 * depth, width), lambda i, t: (t[2 + i], 0)),
        ),
        out_shape=jax.ShapeDtypeStruct((at * 4 * depth, width), quads[0][0].dtype),
        compiler_params=pltpu.CompilerParams(vmem_limit_bytes=48 << 20),
        cost_estimate=BRIEF,
        name="assemble",
    )(table, *[r for q in quads for r in q])


class Held:
    def __init__(self, value):
        self.value = value


def tie(main, *held):
    got = lax.optimization_barrier((main,) + tuple(h.value for h in held))
    for h, v in zip(held, got[1:]):
        h.value = v
    return got[0]


class Fetch:
    def __init__(self, plan, shard):
        self.plan, self.shard = plan, Held(shard)
        self.pairs = plan.nx == 2 and plan.ny == 2 and plan.nz % 2 == 0
        self.depth = shard.shape[0]

    def start(self):
        axes = "z" if self.pairs else self.plan.everywhere
        self.near = Held(lax.all_gather(self.shard.value, axes, axis=0, tiled=True))

    def send(self, piece, name):
        return Held(self.plan.exchange(piece.value, name))

    def send_in_plane(self):
        if self.pairs:
            self.by_x, self.by_y, self.near_twin = [self.send(self.near, n) for n in ("s", "y", "core")]

    def a(self, main, following=None):
        main = tie(main, self.near, *([following.shard] if following else []))
        if following:
            following.start()
        self.send_in_plane()
        return main

    def b(self, main):
        if not self.pairs:
            return main
        main = tie(main, self.by_x, self.by_y, self.near_twin)
        half = self.by_x.value.shape[0] // 2
        self.low = Held(self.plan.exchange(self.by_y.value[:half], "s"))
        self.high = Held(self.plan.exchange(self.by_x.value[half:], "y"))
        self.x_twin, self.y_twin = self.send(self.by_x, "core"), self.send(self.by_y, "core")
        return tie(main, self.x_twin, self.y_twin)

    def c(self, main, between=None):
        if not self.pairs:
            return (between(main) if between else main), self.near.value
        plan = self.plan
        main = tie(main, self.low, self.high)
        twins = [self.send(p, "core") for p in (self.low, self.high)]
        main = tie(main, *twins)
        main = between(main) if between else main
        low_twin, high_twin = [t.value for t in twins]
        half = self.low.value.shape[0]
        by_y, y_twin = self.by_y.value, self.y_twin.value
        quads = [
            (self.near.value, self.near_twin.value, self.by_x.value, self.x_twin.value),
            (by_y[:half], y_twin[:half], self.low.value, low_twin),
            (by_y[half:], y_twin[half:], self.high.value, high_twin),
        ]
        z = jnp.arange(plan.nz, dtype=jnp.int32)
        order = jnp.concatenate([z * 2 + plan.y, z * 2 + (1 - plan.y)])
        table = jnp.concatenate([jnp.stack([plan.core, plan.x]).astype(jnp.int32), order.astype(jnp.int32)])
        whole = Held(assemble(table, quads, self.depth))
        main = tie(main, whole)
        return main, whole.value


def add_kernel(*refs):
    total = refs[0][...].astype(jnp.float32)
    for r in refs[1:-1]:
        total = total + r[...].astype(jnp.float32)
    refs[-1][...] = total.astype(refs[-1].dtype)


def add_rows(count, *terms):
    width = terms[0][0].shape[1]
    tile = count // 2
    return pl.pallas_call(
        add_kernel,
        grid=(2,),
        in_specs=[pl.BlockSpec((tile, width), lambda i, base=first // tile: (base + i, 0)) for _, first in terms],
        out_specs=pl.BlockSpec((tile, width), lambda i: (i, 0)),
        out_shape=jax.ShapeDtypeStruct((count, width), jnp.bfloat16),
        compiler_params=pltpu.CompilerParams(vmem_limit_bytes=32 << 20),
        cost_estimate=BRIEF,
        name="add_rows",
    )(*[array for array, _ in terms])


def add_low(*terms):
    total = terms[0].astype(jnp.float32)
    for t in terms[1:]:
        total = total + t.astype(jnp.float32)
    return total.astype(jnp.bfloat16)


class Chain:
    def __init__(self, plan, product, order, rows):
        self.plan, self.product, self.rows = plan, product, rows
        self.name_a, self.size_a, _ = plan.axes[order[0]]
        self.name_b, self.size_b, _ = plan.axes[order[1]]
        self.pairs = self.size_a == 2 and self.size_b == 2
        self.part = None

    def one(self):
        self.part = Held(self.product(self.rows // 2, self.rows, None))
        return self.part

    def send_one(self):
        self.other = Held(self.plan.exchange(self.part.value, "core"))

    def two(self):
        half = self.rows // 2
        if self.pairs:
            quarter = half // 2
            self.part = Held(self.product(quarter, half, (self.other.value, quarter)))
        else:
            self.part = Held(self.product(0, half, (self.other.value, 0)))
        return self.part

    def send_two(self):
        if self.pairs:
            self.far = Held(self.plan.exchange(self.part.value, self.name_a))
        else:
            whole = self.part.value.reshape(self.size_a, self.rows // (2 * self.size_a), -1)
            self.far = Held(lax.psum_scatter(whole, self.name_a, scatter_dimension=0, tiled=False))

    def near(self):
        if self.pairs:
            quarter = self.rows // 4
            self.close_by = Held(self.product(0, quarter, (self.other.value, 0)))
            return self.close_by
        self.close_by = self.far
        return self.close_by

    def three(self):
        if self.pairs:
            eighth = self.rows // 8
            self.part = Held(add_rows(eighth, (self.close_by.value, eighth), (self.far.value, eighth)))
        else:
            self.part = self.far
        return self.part

    def send_three(self):
        if self.pairs:
            self.side = Held(self.plan.exchange(self.part.value, self.name_b))
        else:
            whole = self.part.value.reshape(self.size_b, self.part.value.shape[0] // self.size_b, -1)
            self.side = Held(lax.psum_scatter(whole, self.name_b, scatter_dimension=0, tiled=False))

    def close(self):
        nz = self.plan.nz
        if self.pairs:
            eighth = self.rows // 8
            total = add_rows(eighth, (self.close_by.value, 0), (self.far.value, 0), (self.side.value, 0))
        else:
            total = self.side.value
        self.piece = Held(total.reshape(nz, total.shape[0] // nz, -1))
        return self.piece


def grad_kernel(lefts, starts, with_add, table_ref, *refs):
    j = pl.program_id(1)
    out = refs[-1]
    at = 0
    for (start, count), number in zip(starts, lefts):
        left_refs, right = refs[at:at + number], refs[at + number]
        at += number + 1

        @pl.when(jnp.logical_and(j >= start, j < start + count))
        def _(left_refs=left_refs, right=right):
            left = left_refs[0][...] if len(left_refs) == 1 else jnp.concatenate([r[...] for r in left_refs], axis=1)
            total = dot_tn(left, right[...])
            if with_add:
                total = total + refs[-2][...].astype(jnp.float32)
            out[...] = total.astype(out.dtype)


def grad_rows(pairs, start, stop, add=None, table=None):
    depth = pairs[0][0].shape[0]
    tile_n = 1024
    count = stop - start
    tile_m = min(512, count)
    specs, operands, lefts, starts, at = [], [], [], [], 0

    def column_map(first, begin, n):
        return lambda i, j, t: (0, first + jnp.clip(j - begin, 0, n - 1))

    for left, right, first, n in pairs:
        if table is None:
            block = start // tile_m
            specs.append(pl.BlockSpec((depth, tile_m), lambda i, j, t, block=block: (0, block + i)))
            operands.append(left)
            lefts.append(1)
        else:
            per = tile_m // TILE
            for k in range(per):
                specs.append(pl.BlockSpec((depth, TILE), lambda i, j, t, k=k, per=per: (0, t[start // TILE + i * per + k])))
                operands.append(left)
            lefts.append(per)
        specs.append(pl.BlockSpec((depth, tile_n), column_map(first, at, n)))
        operands.append(right)
        starts.append((at, n))
        at += n
    if add is not None:
        base = add[1] // tile_m
        specs.append(pl.BlockSpec((tile_m, tile_n), lambda i, j, t: (base + i, j)))
        operands.append(add[0])
    width = at * tile_n
    return pl.pallas_call(
        functools.partial(grad_kernel, lefts, starts, add is not None),
        grid_spec=pltpu.PrefetchScalarGridSpec(
            num_scalar_prefetch=1,
            grid=(count // tile_m, at),
            in_specs=specs,
            out_specs=pl.BlockSpec((tile_m, tile_n), lambda i, j, t: (i, j)),
        ),
        out_shape=jax.ShapeDtypeStruct((count, width), jnp.bfloat16),
        compiler_params=pltpu.CompilerParams(vmem_limit_bytes=32 << 20),
        cost_estimate=BRIEF,
        name="grad_rows",
    )(jnp.zeros((1,), jnp.int32) if table is None else table, *operands)


def project(x, gain, w_qkv):
    normed = (x * inv_rms(x) * gain).astype(jnp.bfloat16)
    return normed, matmul_rows(normed, w_qkv).astype(jnp.bfloat16)


def widen(attended, gain, w_inner):
    normed_mlp = (attended * inv_rms(attended) * gain).astype(jnp.bfloat16)
    return (normed_mlp,) + gelu_pair(matmul_rows(normed_mlp, w_inner))


def backward(plan, grad_out, layers, pos, bias, blk, perms, table, output_half):
    low, f32 = jnp.bfloat16, jnp.float32
    previous = None
    results, diags = [], []
    for weights, saved, orders in layers:
        attn_gain, w_qkv, w_output, mlp_gain, w_inner, w_outer = weights
        x, normed, queries, keys, values, context, log_total, attended, normed_mlp, hidden, slope = saved
        width = x.shape[1]
        grad_low = grad_out.astype(low)
        wide = hidden.shape[1]
        blocks = table[orders[1]]

        def outer_rows(a, b, add, hidden=hidden, grad_low=grad_low, blocks=blocks, wide=wide):
            if wide // blocks.shape[0] == TILE:
                return grad_rows([(hidden, grad_low, 0, 1)], a, b, add, blocks)
            rows = plan.take_blocks(matmul_left(hidden, grad_low).astype(low), blocks)[a:b]
            return rows if add is None else add_low(rows, add[0][add[1]:add[1] + b - a])

        def rows_of(*pairs):
            return lambda a, b, add: grad_rows(pairs, a, b, add)

        outer = Chain(plan, outer_rows, orders[1], wide)
        leaving = Held(output_half)
        late = [previous.outer.side, previous.inner.side] if previous else [leaving]
        grad_out = tie(grad_out, outer.one(), *late)
        outer.send_one()
        if not previous:
            arrived = Held(plan.exchange(leaving.value, "s"))
        grad_pre, grad_attended, attn_low, grad_mlp_gain = mlp_back(grad_out, attended, mlp_gain, w_outer, w_inner, slope)
        late = [previous.qk.far, previous.ov.far] if previous else [arrived]
        grad_pre = tie(grad_pre, outer.other, *late)
        left_m = matmul_rows(normed_mlp, perms[orders[0]]).astype(low)
        inner = Chain(plan, rows_of((left_m, grad_pre, 0, wide // 1024)), orders[0], width)
        late = []
        if previous:
            late = [part for c in (previous.qk, previous.ov) for part in (c.near(), c.three())]
            late += [previous.outer.close(), previous.inner.close()]
        grad_pre = tie(grad_pre, outer.two(), inner.one(), *late)
        outer.send_two()
        inner.send_one()
        if previous:
            previous.qk.send_three()
            previous.ov.send_three()
            previous.sum_mlp(plan)
        late = [previous.qk.side, previous.ov.side] if previous else []
        attn_low = tie(attn_low, inner.other, *late)
        late = [previous.qk.close(), previous.ov.close()] if previous else []
        attn_low = tie(attn_low, inner.two(), *late)
        inner.send_two()
        if previous:
            previous.sum_attn(plan)
        grad_context = matmul_back(attn_low, w_output).astype(low)
        ready = [outer.near(), inner.near()]
        left_c = matmul_rows(context, perms[orders[3]]).astype(low)
        left_n = {o: matmul_rows(normed, perms[o]).astype(low) for o in orders[2:]}
        left_c, n_q, n_v = Held(left_c), Held(left_n[orders[2]]), Held(left_n[orders[3]])
        grad_context = tie(grad_context, *ready, left_c, n_q, n_v)
        left_c, left_n = left_c.value, {orders[2]: n_q.value, orders[3]: n_v.value}
        grad_query, dk, dv, diag = attn_bwd(pos, queries, grad_context, context, log_total, keys, values, bias, blk, 0, 1)
        late = [previous.mlp_sum] if previous else []
        last = tie(dv[-1], outer.far, inner.far, *late)
        grad_k = plan.reduce_keys(dk).astype(low)
        grad_v = plan.reduce_keys(list(dv[:-1]) + [last]).astype(low)
        k_held = Held(grad_k)
        grad_v = tie(grad_v, k_held, outer.three(), inner.three())
        grad_k = k_held.value
        outer.send_three()
        inner.send_three()
        tiles = width // 1024
        qk = Chain(plan, rows_of((left_n[orders[2]], grad_query, 0, tiles), (left_n[orders[2]], grad_k, 0, tiles)), orders[2], width)
        ov = Chain(plan, rows_of((left_c, attn_low, 0, tiles), (left_n[orders[3]], grad_v, 0, tiles)), orders[3], width)
        grad_v = tie(grad_v, qk.one(), ov.one())
        qk.send_one()
        ov.send_one()
        grad_out, grad_attn_gain = project_back(grad_attended, x, attn_gain, grad_query, grad_k, grad_v, w_qkv)
        grad_out = tie(grad_out, qk.other, ov.other)
        grad_out = tie(grad_out, qk.two(), ov.two(), outer.close_by, inner.close_by)
        qk.send_two()
        ov.send_two()
        previous = LayerSums(outer, inner, qk, ov, grad_attn_gain, grad_mlp_gain, width)
        results.append(previous)
        diags.append(diag)
    outer.close()
    inner.close()
    previous.sum_mlp(plan)
    grad_out = tie(grad_out, qk.far, ov.far, qk.near(), ov.near())
    grad_out = tie(grad_out, qk.three(), ov.three())
    qk.send_three()
    ov.send_three()
    qk.close()
    qk.piece.value = tie(qk.piece.value, ov.close(), previous.mlp_sum, results[0].attn_sum)
    previous.sum_attn(plan)
    return grad_out, results, diags, arrived.value


class LayerSums:
    def __init__(self, outer, inner, qk, ov, grad_attn_gain, grad_mlp_gain, width):
        self.outer, self.inner, self.qk, self.ov = outer, inner, qk, ov
        self.attn_gain, self.mlp_gain, self.width = grad_attn_gain, grad_mlp_gain, width

    def sum_mlp(self, plan):
        w = self.width
        inner, outer = self.inner.piece.value, self.outer.piece.value
        self.runs, self.depth = inner.shape[2] // w, inner.shape[1]
        stacked = [inner[:, :, i * w:(i + 1) * w] for i in range(self.runs)]
        self.mlp_sum = Held(plan.sum_z(jnp.concatenate(stacked + [outer], axis=1)))

    def sum_attn(self, plan):
        self.attn_sum = Held(plan.sum_z(jnp.concatenate([c.piece.value for c in (self.qk, self.ov)], axis=2)))

    def grads(self):
        w = self.width
        f32 = jnp.float32
        query, key, output, value = [self.attn_sum.value[:, i * w:(i + 1) * w].astype(f32) for i in range(4)]
        both = self.mlp_sum.value.astype(f32)
        d = self.depth
        inner = jnp.concatenate([both[i * d:(i + 1) * d] for i in range(self.runs)], axis=1)
        return [self.attn_gain, query, key, value, output, self.mlp_gain, inner, both[self.runs * d:]]


def body(sizes, inputs, cotangent, lengths, bucket_ids, *params):
    plan = Plan(sizes)
    one, bias_table, two = params[:8], params[8], params[9:]
    blk, width = inputs.shape[1], inputs.shape[2]
    f32, low = jnp.float32, jnp.bfloat16
    gains = jnp.stack([one[0], one[5], two[0], two[5]], axis=1)
    rows = gains.shape[0]
    table_column = jnp.pad(bias_table, (0, rows - bias_table.shape[0]))[:, None] if bias_table.shape[0] < rows else bias_table[:rows, None]
    small = jnp.pad(jnp.concatenate([gains, table_column], axis=1), ((0, 0), (0, TILE - 5)))
    everywhere = plan.everywhere

    length = lax.dynamic_index_in_dim(lengths, plan.s, 0, keepdims=False)
    pos = plan.positions(length, blk)
    row = jnp.arange(blk, dtype=jnp.int32)
    row_pos = jnp.concatenate([row + pos[1] * TILE, row + pos[2] * TILE])
    row_valid = (row_pos < length).astype(f32)[:, None]

    shards = (
        jnp.concatenate([one[1], one[2], one[3], one[4], small], axis=1),
        one[6],
        one[7],
        jnp.concatenate([two[1], two[2], two[3], two[4]], axis=1),
        two[6],
        two[7],
    )
    attn_1, inner_1, outer_1, attn_2, inner_2, outer_2 = [Fetch(plan, piece) for piece in shards]
    attn_1.start()
    x = plan.to_sequences(inputs)
    cotangent = plan.to_sequences(cotangent)
    x = tie(x, inner_1.shard)
    inner_1.start()
    held = Held(cotangent)
    x = tie(x, held)
    cotangent = held.value
    x = attn_1.a(x, outer_1)
    x = attn_1.b(x)
    x = inner_1.a(x, attn_2)
    x, first = attn_1.c(x)
    picks = jnp.eye(8, TILE, dtype=low)
    smalls = matmul_back(picks, first[:, 4 * width:])
    gain = smalls[:4]
    whole_table = smalls[4].reshape(-1, rows)[:, :bias_table.shape[0]].reshape(-1)
    heads = width // DK
    buckets = whole_table.shape[0] // heads
    reversed_ids = jnp.concatenate([jnp.full((1,), -1, jnp.int32), bucket_ids[::-1]])
    indicator = (reversed_ids[None, :] == jnp.arange(buckets, dtype=jnp.int32)[:, None]).astype(low)
    vector = Held(matmul_rows(whole_table.reshape(heads, buckets).astype(low), indicator))
    x_one = x.astype(f32)
    normed_one, qkv = project(x_one, gain[0:1], first[:, :3 * width])
    qkv = inner_1.b(qkv)
    qkv = outer_1.a(qkv, inner_2)
    kv = plan.gather_keys(qkv[:, width:])
    qkv = tie(qkv, vector)
    bias = Held(toeplitz_tiles(vector.value))
    qkv = tie(qkv, bias)
    bias = bias.value
    queries_one = qkv[:, :width]
    keys_one, values_one = [p[:, :width] for p in kv], [p[:, width:] for p in kv]
    context_one, log_one = attn_fwd(pos, queries_one, keys_one, values_one, bias, blk)
    context_one, w_inner_one = inner_1.c(context_one, lambda main: attn_2.a(outer_1.b(main), outer_2))
    attended_one = x_one + matmul_rows(context_one, first[:, 3 * width:4 * width])
    normed_mlp_one, hidden_one, slope_one = widen(attended_one, gain[1:2], w_inner_one)
    slope_one = Held(slope_one)
    hidden_one = tie(hidden_one, slope_one)
    slope_one = slope_one.value
    hidden_one, w_outer_one = outer_1.c(hidden_one)
    hidden_one = attn_2.b(hidden_one)
    hidden_one = inner_2.a(hidden_one)
    x_two = attended_one + matmul_rows(hidden_one, w_outer_one)
    x_two, third = attn_2.c(x_two)
    normed_two, qkv = project(x_two, gain[2:3], third[:, :3 * width])
    qkv = inner_2.b(qkv)
    qkv = outer_2.a(qkv)
    kv = plan.gather_keys(qkv[:, width:])
    queries_two = qkv[:, :width]
    keys_two, values_two = [p[:, :width] for p in kv], [p[:, width:] for p in kv]
    context_two, log_two = attn_fwd(pos, queries_two, keys_two, values_two, bias, blk)
    context_two, w_inner_two = inner_2.c(context_two)
    context_two = outer_2.b(context_two)
    attended_two = x_two + matmul_rows(context_two, third[:, 3 * width:])
    normed_mlp_two, hidden_two, slope_two = widen(attended_two, gain[3:4], w_inner_two)
    slope_two = Held(slope_two)
    hidden_two = tie(hidden_two, slope_two)
    slope_two = slope_two.value
    hidden_two, w_outer_two = outer_2.c(hidden_two)
    final = attended_two + matmul_rows(hidden_two, w_outer_two)
    output_rows = (final * row_valid).astype(low)
    grad_out = cotangent.astype(f32) * row_valid

    weights_one = (gain[0:1], first, first[:, 3 * width:4 * width], gain[1:2], w_inner_one, w_outer_one)
    weights_two = (gain[2:3], third, third[:, 3 * width:], gain[3:4], w_inner_two, w_outer_two)
    saved_one = (x, normed_one, queries_one, keys_one, values_one, context_one, log_one, attended_one, normed_mlp_one, hidden_one, slope_one)
    saved_two = (x_two, normed_two, queries_two, keys_two, values_two, context_two, log_two, attended_two, normed_mlp_two, hidden_two, slope_two)

    xy, yx = ("x", "y"), ("y", "x")
    perms = {o: plan.permutation(o, width) for o in (xy, yx)}
    depth = one[7].shape[0]
    step = TILE if depth % TILE == 0 else depth
    blocks = jnp.arange(saved_one[9].shape[1] // step, dtype=jnp.int32)
    per = depth // step
    table = {o: plan.block_of(o, blocks // per) * per + blocks % per for o in (xy, yx)}
    layers = [(weights_two, saved_two, (xy, yx, yx, xy)), (weights_one, saved_one, (xy, yx, yx, xy))]
    grad_state, sums, diags, arrived = backward(plan, grad_out, layers, pos, bias, blk, perms, table, output_rows[blk:])
    output = plan.in_order(output_rows[:blk], arrived)
    grads_two, grads_one = sums[0].grads(), sums[1].grads()
    input_grad = plan.from_sequences(grad_state.astype(low))

    grad_table = lax.dot_general(diags[0] + diags[1], indicator.astype(f32), (((1,), (1,)), ((), ())), precision=HIGH_PRECISION)
    vectors = jnp.concatenate([grads_one[0][0], grads_one[5][0], grads_two[0][0], grads_two[5][0], grad_table.reshape(-1)])
    held = Held(vectors)
    grad_state = tie(grad_state, held)
    vectors = plan.sum_vector(held.value)
    device = ((plan.z * plan.ny + plan.y) * plan.nx + plan.x) * 2 + plan.core

    def share(start, count):
        return lax.dynamic_slice_in_dim(vectors, start + device * count, count, 0)

    gain_grads = [share(i * width, rows) for i in range(4)]
    table_grad = share(4 * width, bias_table.shape[0])
    return (
        output,
        input_grad,
        gain_grads[0],
        *grads_one[1:5],
        gain_grads[1],
        *grads_one[6:],
        table_grad,
        gain_grads[2],
        *grads_two[1:5],
        gain_grads[3],
        *grads_two[6:],
    )


def solution(mesh):
    dp, cp = mesh.shape["dp"], mesh.shape["cp"]
    nx = cp // 2
    ny = nx if dp % nx == 0 else 1

    def run(inputs, *rest):
        ns = inputs.shape[0] // dp
        assert ns == 2 and nx % ns == 0
        sizes = (dp // ny, ny, ns, nx // ns)
        finer = Mesh(mesh.devices.reshape(*sizes, 2), ("z", "y", "s", "q", "core"))
        dpn, cpn = ("z", "y"), ("s", "q", "core")
        tokens = P(dpn, cpn, None)
        vector, matrix = P(dpn + cpn), P(dpn + cpn, None)
        layer = (vector, matrix, matrix, matrix, matrix, vector, matrix, matrix)
        return jax.shard_map(
            functools.partial(body, sizes),
            mesh=finer,
            in_specs=(tokens, tokens, P(dpn), P()) + layer + (vector,) + layer,
            out_specs=(tokens, tokens) + layer + (vector,) + layer,
            check_vma=False,
        )(inputs, *rest)

    return run
```

```python
import functools

import jax
import jax.numpy as jnp
import numpy as np
from jax import lax
from jax.experimental import pallas as pl
from jax.experimental.pallas import tpu as pltpu
from jax.sharding import Mesh
from jax.sharding import PartitionSpec as P

DK = 64
TILE = 128
EPS = 1e-06
NEGATIVE = -1e30
HIGH_PRECISION = lax.Precision.HIGHEST
BRIEF = pl.CostEstimate(flops=1024, bytes_accessed=1024, transcendentals=0)


def toeplitz_kernel(span, u_ref, t_ref):
    rolled = jnp.broadcast_to(u_ref[0], (TILE, u_ref.shape[2]))
    rolled = pltpu.roll(rolled, 0, 1, stride=1, stride_axis=0)
    for e in range(span):
        base = TILE * (span - e)
        t_ref[0, e] = rolled[:, base:base + TILE].astype(t_ref.dtype)

def toeplitz_tiles(u):
    heads, width = u.shape
    span = width // TILE - 1
    return pl.pallas_call(
        functools.partial(toeplitz_kernel, span),
        grid=(heads,),
        in_specs=[pl.BlockSpec((1, 1, width), lambda h: (h, 0, 0))],
        out_specs=pl.BlockSpec((1, span, TILE, TILE), lambda h: (h, 0, 0, 0)),
        out_shape=jax.ShapeDtypeStruct((heads, span, TILE, TILE), jnp.bfloat16),
        cost_estimate=BRIEF,
        name="toeplitz",
    )(u.reshape(heads, 1, width))

def head_lanes(h, x):
    lane = lax.broadcasted_iota(jnp.int32, x.shape, 1)
    return jnp.where((lane // DK) == h, x, jnp.zeros_like(x))

def dot_nt(a, b):
    return lax.dot_general(a, b, (((1,), (1,)), ((), ())), preferred_element_type=jnp.float32)

def dot_tn(a, b):
    return lax.dot_general(a, b, (((0,), (0,)), ((), ())), preferred_element_type=jnp.float32)

def dot_nn(a, b):
    return lax.dot_general(a, b, (((1,), (0,)), ((), ())), preferred_element_type=jnp.float32)

def key_chunks(parts, rows, chunk):
    return [(i, s) for i in range(parts) for s in range(0, rows, chunk)]

def chunk_scores(pos_ref, k_chunk, q_head, bias_ref, h, c, chunk, blk, q_rows):
    n = chunk // blk
    sub = blk // TILE
    nq = q_rows // blk
    s = dot_nt(k_chunk, q_head)
    half = bias_ref.shape[1] // 2
    rows = []
    for kb in range(n):
        kpos = pos_ref[1 + nq + c * n + kb]
        for kk in range(sub):
            cols = []
            for qb in range(nq):
                e0 = (kpos - pos_ref[1 + qb]) + half + kk
                for qq in range(sub):
                    cols.append(bias_ref[h, e0 - qq])
            rows.append(jnp.concatenate(cols, axis=1))
    bias = jnp.concatenate(rows, axis=0).astype(jnp.float32)
    s = s + bias
    valid = []
    for kb in range(n):
        limit = pos_ref[0] - pos_ref[1 + nq + c * n + kb] * TILE
        valid.append(lax.broadcasted_iota(jnp.int32, (blk, 1), 0) < limit)
    ok = valid[0] if n == 1 else jnp.concatenate([v.astype(jnp.int32) for v in valid], axis=0) > 0
    return s, ok

def attn_fwd_kernel(parts, chunk, blk, pos_ref, q_ref, *refs):
    k_refs, v_refs = refs[:parts], refs[parts:2 * parts]
    bias_ref, o_ref, lse_ref, s_ref = refs[2 * parts:]
    q_rows = q_ref.shape[0]
    rows = k_refs[0].shape[0]
    chunks = key_chunks(parts, rows, chunk)
    outs = []
    for h in range(2):
        qh = head_lanes(h, q_ref[...])
        top = None
        for c, (i, s0) in enumerate(chunks):
            s, ok = chunk_scores(pos_ref, k_refs[i][s0:s0 + chunk, :], qh, bias_ref, h, c, chunk, blk, q_rows)
            s = jnp.where(ok, s, NEGATIVE)
            s_ref[c * chunk:(c + 1) * chunk, :] = s
            m = jnp.max(s, axis=0, keepdims=True)
            top = m if top is None else jnp.maximum(top, m)
        total = jnp.zeros((1, q_rows), jnp.float32)
        acc = jnp.zeros((2 * DK, q_rows), jnp.float32)
        for c, (i, s0) in enumerate(chunks):
            p = jnp.exp(s_ref[c * chunk:(c + 1) * chunk, :] - top)
            total = total + jnp.sum(p, axis=0, keepdims=True)
            acc = acc + dot_tn(v_refs[i][s0:s0 + chunk, :], p.astype(jnp.bfloat16))
        outs.append((acc / total)[h * DK:(h + 1) * DK])
        lse_ref[0, h:h + 1, :] = top + jnp.log(total)
    o_ref[...] = jnp.concatenate(outs, axis=0).T.astype(o_ref.dtype)

def attn_fwd(pos, q, ks, vs, bias, blk):
    q_rows, width = q.shape
    parts, rows = len(ks), ks[0].shape[0]
    keys = parts * rows
    heads = width // DK
    span = bias.shape[1]
    chunk = min(256, rows)
    spec_q = pl.BlockSpec((q_rows, 2 * DK), lambda p, s: (0, p))
    spec_k = pl.BlockSpec((rows, 2 * DK), lambda p, s: (0, p))
    o, lse = pl.pallas_call(
        functools.partial(attn_fwd_kernel, parts, chunk, blk),
        grid_spec=pltpu.PrefetchScalarGridSpec(
            num_scalar_prefetch=1,
            grid=(heads // 2,),
            in_specs=[spec_q] + [spec_k] * (2 * parts) + [pl.BlockSpec((2, span, TILE, TILE), lambda p, s: (p, 0, 0, 0))],
            out_specs=[spec_q, pl.BlockSpec((1, 2, q_rows), lambda p, s: (p, 0, 0))],
            scratch_shapes=[pltpu.VMEM((keys, q_rows), jnp.float32)],
        ),
        out_shape=[jax.ShapeDtypeStruct((q_rows, width), jnp.bfloat16), jax.ShapeDtypeStruct((heads // 2, 2, q_rows), jnp.float32)],
        compiler_params=pltpu.CompilerParams(vmem_limit_bytes=48 << 20),
        cost_estimate=BRIEF,
        name="attn_fwd",
    )(pos, q, *ks, *vs, bias)
    return o, lse

def skew_rows(x):
    width = 2 * x.shape[1]
    x = jnp.concatenate([jnp.zeros_like(x), x], axis=1)
    rows = x.shape[0]
    while rows > 8:
        rows //= 2
        x = x[:rows] + pltpu.roll(x[rows:], width - rows, 1)
    row = lax.broadcasted_iota(jnp.int32, x.shape, 0)
    for bit in (1, 2, 4):
        x = jnp.where((row & bit) != 0, pltpu.roll(x, width - bit, 1), x)
    return x

def attn_bwd_kernel(parts, chunk, blk, pos_ref, q_ref, do_ref, o_ref, lse_ref, *refs):
    k_refs, v_refs = refs[:parts], refs[parts:2 * parts]
    bias_ref, dq_ref = refs[2 * parts:2 * parts + 2]
    dk_refs, dv_refs = refs[2 * parts + 2:3 * parts + 2], refs[3 * parts + 2:4 * parts + 2]
    d_ref, e_ref = refs[4 * parts + 2:]
    q_rows = q_ref.shape[0]
    rows = k_refs[0].shape[0]
    chunks = key_chunks(parts, rows, chunk)
    span = bias_ref.shape[1]
    half = span // 2
    n, sub, nq = chunk // blk, blk // TILE, q_rows // blk
    prod = (do_ref[...].astype(jnp.float32) * o_ref[...].astype(jnp.float32)).T
    outs = []
    for h in range(2):
        qh = head_lanes(h, q_ref[...])
        doh = head_lanes(h, do_ref[...])
        inner = jnp.sum(prod[h * DK:(h + 1) * DK], axis=0, keepdims=True)
        lse = lse_ref[0, h:h + 1, :]
        acc = jnp.zeros((2 * DK, q_rows), jnp.float32)
        e_ref[...] = jnp.zeros_like(e_ref)
        for c, (i, s0) in enumerate(chunks):
            k_chunk = k_refs[i][s0:s0 + chunk, :]
            s, ok = chunk_scores(pos_ref, k_chunk, qh, bias_ref, h, c, chunk, blk, q_rows)
            p = jnp.where(ok, jnp.exp(s - lse), 0.0)
            dp = dot_nt(v_refs[i][s0:s0 + chunk, :], doh)
            ds = p * (dp - inner)
            dsb = ds.astype(jnp.bfloat16)
            dv = dot_nn(p.astype(jnp.bfloat16), doh)
            dk = dot_nn(dsb, qh)
            at = pl.ds(s0, chunk)
            if h == 0:
                dk_refs[i][at, :] = dk.astype(jnp.bfloat16)
                dv_refs[i][at, :] = dv.astype(jnp.bfloat16)
            else:
                dk_refs[i][at, :] = (dk_refs[i][at, :].astype(jnp.float32) + dk).astype(jnp.bfloat16)
                dv_refs[i][at, :] = (dv_refs[i][at, :].astype(jnp.float32) + dv).astype(jnp.bfloat16)
            acc = acc + dot_tn(k_chunk, dsb)
            for kb in range(n):
                kpos = pos_ref[1 + nq + c * n + kb]
                for qb in range(nq):
                    e0 = (kpos - pos_ref[1 + qb]) + half
                    for d in range(1 - sub, sub):
                        tot = None
                        for kk in range(sub):
                            qq = kk - d
                            if 0 <= qq < sub:
                                r0, c0 = kb * blk + kk * TILE, qb * blk + qq * TILE
                                t = ds[r0:r0 + TILE, c0:c0 + TILE]
                                tot = t if tot is None else tot + t
                        e_ref[e0 + d] += tot
        outs.append(acc[h * DK:(h + 1) * DK])
        pieces = [jnp.zeros((1, TILE), jnp.float32) for _ in range(span + 1)]
        for e in range(span):
            r = jnp.sum(skew_rows(e_ref[e]), axis=0, keepdims=True)
            b = span - 1 - e
            pieces[b] = pieces[b] + r[:, :TILE]
            pieces[b + 1] = pieces[b + 1] + r[:, TILE:]
        d_ref[0, h:h + 1, :] = jnp.concatenate(pieces, axis=1)
    dq_ref[...] = jnp.concatenate(outs, axis=0).T.astype(dq_ref.dtype)

def attn_bwd(pos, q, do, o, lse, ks, vs, bias, blk, share, shares):
    q_rows, width = q.shape
    parts, rows = len(ks), ks[0].shape[0]
    keys = parts * rows
    heads = width // DK // shares
    width = width // shares
    span = bias.shape[1]
    chunk = min(256, rows)
    first = share * (heads // 2)
    spec_q = pl.BlockSpec((q_rows, 2 * DK), lambda p, s: (0, first + p))
    spec_k = pl.BlockSpec((rows, 2 * DK), lambda p, s: (0, first + p))
    spec_l = pl.BlockSpec((1, 2, q_rows), lambda p, s: (first + p, 0, 0))
    spec_b = pl.BlockSpec((2, span, TILE, TILE), lambda p, s: (first + p, 0, 0, 0))
    out_q = pl.BlockSpec((q_rows, 2 * DK), lambda p, s: (0, p))
    out_k = pl.BlockSpec((rows, 2 * DK), lambda p, s: (0, p))
    out = pl.pallas_call(
        functools.partial(attn_bwd_kernel, parts, chunk, blk),
        grid_spec=pltpu.PrefetchScalarGridSpec(
            num_scalar_prefetch=1,
            grid=(heads // 2,),
            in_specs=[spec_q, spec_q, spec_q, spec_l] + [spec_k] * (2 * parts) + [spec_b],
            out_specs=[out_q] + [out_k] * (2 * parts) + [pl.BlockSpec((1, 2, (span + 1) * TILE), lambda p, s: (p, 0, 0))],
            scratch_shapes=[pltpu.VMEM((span, TILE, TILE), jnp.float32)],
        ),
        out_shape=[jax.ShapeDtypeStruct((q_rows, width), jnp.bfloat16)]
        + [jax.ShapeDtypeStruct((rows, width), jnp.bfloat16)] * (2 * parts)
        + [jax.ShapeDtypeStruct((heads // 2, 2, (span + 1) * TILE), jnp.float32)],
        compiler_params=pltpu.CompilerParams(vmem_limit_bytes=48 << 20),
        cost_estimate=pl.CostEstimate(flops=40 * q_rows * keys * width, bytes_accessed=8 * keys * width + 8 * q_rows * width, transcendentals=heads * q_rows * keys),
        name="attn_bwd",
    )(pos, q, do, o, lse, *ks, *vs, bias)
    dq, dks, dvs, d = out[0], out[1:1 + parts], out[1 + parts:1 + 2 * parts], out[-1]
    return dq, dks, dvs, d.reshape(heads, (span + 1) * TILE)


def matmul_rows(left, right):
    return jnp.dot(left, right, preferred_element_type=jnp.float32)


def matmul_left(left, right):
    return lax.dot_general(left, right, (((0,), (0,)), ((), ())), preferred_element_type=jnp.float32)


def matmul_back(left, right):
    return lax.dot_general(left, right, (((1,), (1,)), ((), ())), preferred_element_type=jnp.float32)


def inv_rms(values):
    return lax.rsqrt(jnp.mean(values * values, axis=-1, keepdims=True) + EPS)


def norm_back(grad, values, gain):
    scale = inv_rms(values)
    weighted = gain * grad
    mean = jnp.mean(weighted * values, axis=-1, keepdims=True)
    grad_in = scale * weighted - values * (scale * scale * scale) * mean
    return grad_in, jnp.sum(grad * values * scale, axis=0, keepdims=True)


def mlp_back_kernel(grad_ref, value_ref, gain_ref, outer_ref, inner_ref, slope_ref, pre_ref, out_ref, low_ref, gain_grad_ref, acc_ref, left_ref):
    i = pl.program_id(0)

    @pl.when(i == 0)
    def _():
        left_ref[...] = grad_ref[...].astype(jnp.bfloat16)
        acc_ref[...] = jnp.zeros_like(acc_ref)

    grad_pre = (dot_nt(left_ref[...], outer_ref[...]) * slope_ref[...].astype(jnp.float32)).astype(jnp.bfloat16)
    pre_ref[...] = grad_pre
    acc_ref[...] += dot_nt(grad_pre, inner_ref[...])

    @pl.when(i == pl.num_programs(0) - 1)
    def _():
        grad_in, grad_gain = norm_back(acc_ref[...], value_ref[...], gain_ref[...])
        total = grad_ref[...] + grad_in
        out_ref[...] = total
        low_ref[...] = total.astype(jnp.bfloat16)
        gain_grad_ref[...] = grad_gain


def mlp_back(grad_out, attended, gain, w_outer, w_inner, slope):
    rows, width = grad_out.shape
    wide = w_outer.shape[0]
    tile = min(1024, wide)
    whole = pl.BlockSpec((rows, width), lambda i: (0, 0))
    line = pl.BlockSpec((1, width), lambda i: (0, 0))
    return pl.pallas_call(
        mlp_back_kernel,
        grid=(wide // tile,),
        in_specs=[
            whole,
            whole,
            line,
            pl.BlockSpec((tile, width), lambda i: (i, 0)),
            pl.BlockSpec((width, tile), lambda i: (0, i)),
            pl.BlockSpec((rows, tile), lambda i: (0, i)),
        ],
        out_specs=[pl.BlockSpec((rows, tile), lambda i: (0, i)), whole, whole, line],
        out_shape=[
            jax.ShapeDtypeStruct((rows, wide), jnp.bfloat16),
            jax.ShapeDtypeStruct((rows, width), jnp.float32),
            jax.ShapeDtypeStruct((rows, width), jnp.bfloat16),
            jax.ShapeDtypeStruct((1, width), jnp.float32),
        ],
        scratch_shapes=[pltpu.VMEM((rows, width), jnp.float32), pltpu.VMEM((rows, width), jnp.bfloat16)],
        compiler_params=pltpu.CompilerParams(vmem_limit_bytes=48 << 20),
        cost_estimate=BRIEF,
        name="mlp_back",
    )(grad_out, attended, gain, w_outer, w_inner, slope)


def project_back_kernel(add_ref, value_ref, gain_ref, q_ref, k_ref, v_ref, w_ref, out_ref, gain_grad_ref, acc_ref):
    i = pl.program_id(0)
    for j, r in enumerate((q_ref, k_ref, v_ref)):

        @pl.when(i == j)
        def _(j=j, r=r):
            part = dot_nt(r[...], w_ref[...])
            acc_ref[...] = part if j == 0 else acc_ref[...] + part

    @pl.when(i == 2)
    def _():
        grad_in, grad_gain = norm_back(acc_ref[...], value_ref[...].astype(jnp.float32), gain_ref[...])
        out_ref[...] = add_ref[...] + grad_in
        gain_grad_ref[...] = grad_gain


def project_back(grad_attended, x, gain, grad_query, grad_k, grad_v, w):
    rows, width = x.shape
    whole = pl.BlockSpec((rows, width), lambda i: (0, 0))
    line = pl.BlockSpec((1, width), lambda i: (0, 0))
    return pl.pallas_call(
        project_back_kernel,
        grid=(3,),
        in_specs=[whole, whole, line, whole, whole, whole, pl.BlockSpec((width, width), lambda i: (0, i))],
        out_specs=[whole, line],
        out_shape=[jax.ShapeDtypeStruct((rows, width), jnp.float32), jax.ShapeDtypeStruct((1, width), jnp.float32)],
        scratch_shapes=[pltpu.VMEM((rows, width), jnp.float32)],
        compiler_params=pltpu.CompilerParams(vmem_limit_bytes=48 << 20),
        cost_estimate=BRIEF,
        name="project_back",
    )(grad_attended, x, gain, grad_query, grad_k, grad_v, w)


def gelu_pair(pre):
    c = np.float32(np.sqrt(2.0 / np.pi))
    sq = pre * pre
    t = jnp.tanh(c * (pre + 0.044715 * (sq * pre)))
    half = 0.5 * (1.0 + t)
    slope = half + (0.5 * c) * pre * (1.0 - t * t) * (1.0 + 0.134145 * sq)
    return (pre * half).astype(jnp.bfloat16), slope.astype(jnp.bfloat16)


SWAP = [(0, 1), (1, 0)]


class Plan:
    def __init__(self, sizes):
        self.nz, self.ny, self.ns, self.m = sizes
        self.nx = self.ns * self.m
        self.z = lax.axis_index("z")
        self.y = lax.axis_index("y")
        self.s = lax.axis_index("s")
        self.q = lax.axis_index("q")
        self.core = lax.axis_index("core")
        self.x = self.s * self.m + self.q
        self.everywhere = ("z", "y", "s", "q", "core")
        self.axes = {"x": (("s", "q") if self.m > 1 else "s", self.nx, self.x), "y": ("y", self.ny, self.y)}

    def block_of(self, order, n):
        n_z = n % self.nz
        n = n // self.nz
        place = {}
        for name in reversed(order):
            _, size, mine = self.axes[name]
            part = n % size
            n = n // size
            place[name] = part ^ mine if size == 2 else part
        core = n ^ self.core
        return ((n_z * self.ny + place["y"]) * self.nx + place["x"]) * 2 + core

    def permutation(self, order, width):
        depth = width // (self.nz * self.ny * self.nx * 2)
        n = lax.broadcasted_iota(jnp.int32, (width, width), 1)
        i = lax.broadcasted_iota(jnp.int32, (width, width), 0)
        source = self.block_of(order, n // depth) * depth + n % depth
        return (i == source).astype(jnp.bfloat16)

    def take_blocks(self, rows, table):
        return jnp.take(rows.reshape(table.shape[0], -1, rows.shape[1]), table, axis=0).reshape(rows.shape)

    def exchange(self, piece, name):
        return lax.ppermute(piece, name, SWAP)

    def sum_z(self, piece):
        if self.nz == 1:
            return piece[0]
        return lax.psum_scatter(piece, "z", scatter_dimension=0, tiled=False)

    def sum_vector(self, vector):
        for name, size in (("core", 2), ("z", self.nz), ("y", self.ny), ("q", self.m), ("s", self.ns)):
            if size & (size - 1):
                vector = lax.psum(vector, name)
                continue
            step = 1
            while step < size:
                vector = vector + lax.ppermute(vector, name, [(i, i ^ step) for i in range(size)])
                step *= 2
        return vector

    def to_sequences(self, local):
        own = lax.dynamic_index_in_dim(local, self.s, 0, keepdims=False)
        other = lax.dynamic_index_in_dim(local, 1 - self.s, 0, keepdims=False)
        return jnp.concatenate([own, self.exchange(other, "s")], axis=0)

    def from_sequences(self, rows):
        blk = rows.shape[0] // 2
        return self.in_order(rows[:blk], self.exchange(rows[blk:], "s"))

    def in_order(self, own, other):
        first = self.s == 0
        return jnp.stack([jnp.where(first, own, other), jnp.where(first, other, own)], axis=0)

    def gather_keys(self, rows):
        if self.m == 1:
            return [rows, self.exchange(rows, "core")]
        return [lax.all_gather(rows, ("q", "core"), axis=0, tiled=True)]

    def reduce_keys(self, parts):
        if self.m == 1:
            return add_rows(parts[0].shape[0], (parts[0], 0), (self.exchange(parts[1], "core"), 0))
        return lax.psum_scatter(parts[0], ("q", "core"), scatter_dimension=0, tiled=True).astype(jnp.float32)

    def positions(self, length, blk):
        unit = blk // TILE
        mine = [(((self.s ^ j) * self.m + self.q) * 2 + self.core) * unit for j in range(2)]
        if self.m == 1:
            keys = [(((self.s ^ j) * self.m + self.q) * 2 + (self.core ^ c)) * unit for c in range(2) for j in range(2)]
        else:
            keys = [(((self.s ^ j) * self.m + q) * 2 + c) * unit for q in range(self.m) for c in range(2) for j in range(2)]
        return jnp.stack([length] + mine + keys).astype(jnp.int32)


def assemble_kernel(steps, depth, table_ref, *refs):
    i = pl.program_id(0)
    out = refs[-1]
    core, x = table_ref[0], table_ref[1]
    quads = [refs[j:j + 4] for j in range(0, len(refs) - 1, 4)]
    for quad, (start, count) in zip(quads, steps):

        @pl.when(jnp.logical_and(i >= start, i < start + count))
        def _(quad=quad):
            for j, r in enumerate(quad):
                place = (x ^ (j // 2)) * 2 + (core ^ (j % 2))
                out[pl.ds(pl.multiple_of(place * depth, depth), depth), :] = r[...]


def assemble(table, quads, depth):
    width = quads[0][0].shape[1]
    steps, at = [], 0
    for q in quads:
        steps.append((at, q[0].shape[0] // depth))
        at += q[0].shape[0] // depth

    def source_map(start, count):
        return lambda i, t: (jnp.clip(i - start, 0, count - 1), 0)

    return pl.pallas_call(
        functools.partial(assemble_kernel, steps, depth),
        grid_spec=pltpu.PrefetchScalarGridSpec(
            num_scalar_prefetch=1,
            grid=(at,),
            in_specs=[pl.BlockSpec((depth, width), source_map(*s)) for s in steps for _ in range(4)],
            out_specs=pl.BlockSpec((4 * depth, width), lambda i, t: (t[2 + i], 0)),
        ),
        out_shape=jax.ShapeDtypeStruct((at * 4 * depth, width), quads[0][0].dtype),
        compiler_params=pltpu.CompilerParams(vmem_limit_bytes=48 << 20),
        cost_estimate=BRIEF,
        name="assemble",
    )(table, *[r for q in quads for r in q])


class Held:
    def __init__(self, value):
        self.value = value


def tie(main, *held):
    got = lax.optimization_barrier((main,) + tuple(h.value for h in held))
    for h, v in zip(held, got[1:]):
        h.value = v
    return got[0]


class Fetch:
    def __init__(self, plan, shard):
        self.plan, self.shard = plan, Held(shard)
        self.pairs = plan.nx == 2 and plan.ny == 2 and plan.nz % 2 == 0
        self.depth = shard.shape[0]

    def start(self):
        axes = "z" if self.pairs else self.plan.everywhere
        self.near = Held(lax.all_gather(self.shard.value, axes, axis=0, tiled=True))

    def send(self, piece, name):
        return Held(self.plan.exchange(piece.value, name))

    def send_in_plane(self):
        if self.pairs:
            self.by_x, self.by_y, self.near_twin = [self.send(self.near, n) for n in ("s", "y", "core")]

    def a(self, main, following=None):
        main = tie(main, self.near, *([following.shard] if following else []))
        if following:
            following.start()
        self.send_in_plane()
        return main

    def b(self, main, *fill):
        if not self.pairs:
            return main
        main = tie(main, self.by_x, self.by_y, self.near_twin)
        half = self.by_x.value.shape[0] // 2
        self.low = Held(self.plan.exchange(self.by_y.value[:half], "s"))
        self.high = Held(self.plan.exchange(self.by_x.value[half:], "y"))
        self.x_twin, self.y_twin = self.send(self.by_x, "core"), self.send(self.by_y, "core")
        return tie(main, self.x_twin, self.y_twin, *fill)

    def c(self, main, between=None, fill=()):
        if not self.pairs:
            return (between(main) if between else main), self.near.value
        plan = self.plan
        main = tie(main, self.low, self.high)
        twins = [self.send(p, "core") for p in (self.low, self.high)]
        main = tie(main, *twins, *fill)
        main = between(main) if between else main
        low_twin, high_twin = [t.value for t in twins]
        half = self.low.value.shape[0]
        by_y, y_twin = self.by_y.value, self.y_twin.value
        quads = [
            (self.near.value, self.near_twin.value, self.by_x.value, self.x_twin.value),
            (by_y[:half], y_twin[:half], self.low.value, low_twin),
            (by_y[half:], y_twin[half:], self.high.value, high_twin),
        ]
        z = jnp.arange(plan.nz, dtype=jnp.int32)
        order = jnp.concatenate([z * 2 + plan.y, z * 2 + (1 - plan.y)])
        table = jnp.concatenate([jnp.stack([plan.core, plan.x]).astype(jnp.int32), order.astype(jnp.int32)])
        whole = Held(assemble(table, quads, self.depth))
        main = tie(main, whole)
        return main, whole.value


def add_kernel(*refs):
    total = refs[0][...].astype(jnp.float32)
    for r in refs[1:-1]:
        total = total + r[...].astype(jnp.float32)
    refs[-1][...] = total.astype(refs[-1].dtype)


def add_rows(count, *terms):
    width = terms[0][0].shape[1]
    tile = count // 2
    return pl.pallas_call(
        add_kernel,
        grid=(2,),
        in_specs=[pl.BlockSpec((tile, width), lambda i, base=first // tile: (base + i, 0)) for _, first in terms],
        out_specs=pl.BlockSpec((tile, width), lambda i: (i, 0)),
        out_shape=jax.ShapeDtypeStruct((count, width), jnp.bfloat16),
        compiler_params=pltpu.CompilerParams(vmem_limit_bytes=32 << 20),
        cost_estimate=BRIEF,
        name="add_rows",
    )(*[array for array, _ in terms])


def add_low(*terms):
    total = terms[0].astype(jnp.float32)
    for t in terms[1:]:
        total = total + t.astype(jnp.float32)
    return total.astype(jnp.bfloat16)


class Chain:
    def __init__(self, plan, product, order, rows):
        self.plan, self.product, self.rows = plan, product, rows
        self.name_a, self.size_a, _ = plan.axes[order[0]]
        self.name_b, self.size_b, _ = plan.axes[order[1]]
        self.pairs = self.size_a == 2 and self.size_b == 2
        self.part = None

    def one(self):
        self.part = Held(self.product(self.rows // 2, self.rows, None))
        return self.part

    def send_one(self):
        self.other = Held(self.plan.exchange(self.part.value, "core"))

    def two(self):
        half = self.rows // 2
        if self.pairs:
            quarter = half // 2
            self.part = Held(self.product(quarter, half, (self.other.value, quarter)))
        else:
            self.part = Held(self.product(0, half, (self.other.value, 0)))
        return self.part

    def send_two(self):
        if self.pairs:
            self.far = Held(self.plan.exchange(self.part.value, self.name_a))
        else:
            whole = self.part.value.reshape(self.size_a, self.rows // (2 * self.size_a), -1)
            self.far = Held(lax.psum_scatter(whole, self.name_a, scatter_dimension=0, tiled=False))

    def near(self):
        if self.pairs:
            quarter = self.rows // 4
            self.close_by = Held(self.product(0, quarter, (self.other.value, 0)))
            return self.close_by
        self.close_by = self.far
        return self.close_by

    def three(self):
        if self.pairs:
            eighth = self.rows // 8
            self.part = Held(add_rows(eighth, (self.close_by.value, eighth), (self.far.value, eighth)))
        else:
            self.part = self.far
        return self.part

    def send_three(self):
        if self.pairs:
            self.side = Held(self.plan.exchange(self.part.value, self.name_b))
        else:
            whole = self.part.value.reshape(self.size_b, self.part.value.shape[0] // self.size_b, -1)
            self.side = Held(lax.psum_scatter(whole, self.name_b, scatter_dimension=0, tiled=False))

    def close(self):
        nz = self.plan.nz
        if self.pairs:
            eighth = self.rows // 8
            total = add_rows(eighth, (self.close_by.value, 0), (self.far.value, 0), (self.side.value, 0))
        else:
            total = self.side.value
        self.piece = Held(total.reshape(nz, total.shape[0] // nz, -1))
        return self.piece


def grad_kernel(lefts, starts, with_add, table_ref, *refs):
    j = pl.program_id(1)
    out = refs[-1]
    at = 0
    for (start, count), number in zip(starts, lefts):
        left_refs, right = refs[at:at + number], refs[at + number]
        at += number + 1

        @pl.when(jnp.logical_and(j >= start, j < start + count))
        def _(left_refs=left_refs, right=right):
            left = left_refs[0][...] if len(left_refs) == 1 else jnp.concatenate([r[...] for r in left_refs], axis=1)
            total = dot_tn(left, right[...])
            if with_add:
                total = total + refs[-2][...].astype(jnp.float32)
            out[...] = total.astype(out.dtype)


def grad_rows(pairs, start, stop, add=None, table=None):
    depth = pairs[0][0].shape[0]
    tile_n = 1024
    count = stop - start
    tile_m = min(512, count)
    specs, operands, lefts, starts, at = [], [], [], [], 0

    def column_map(first, begin, n):
        return lambda i, j, t: (0, first + jnp.clip(j - begin, 0, n - 1))

    for left, right, first, n in pairs:
        if table is None:
            block = start // tile_m
            specs.append(pl.BlockSpec((depth, tile_m), lambda i, j, t, block=block: (0, block + i)))
            operands.append(left)
            lefts.append(1)
        else:
            per = tile_m // TILE
            for k in range(per):
                specs.append(pl.BlockSpec((depth, TILE), lambda i, j, t, k=k, per=per: (0, t[start // TILE + i * per + k])))
                operands.append(left)
            lefts.append(per)
        specs.append(pl.BlockSpec((depth, tile_n), column_map(first, at, n)))
        operands.append(right)
        starts.append((at, n))
        at += n
    if add is not None:
        base = add[1] // tile_m
        specs.append(pl.BlockSpec((tile_m, tile_n), lambda i, j, t: (base + i, j)))
        operands.append(add[0])
    width = at * tile_n
    return pl.pallas_call(
        functools.partial(grad_kernel, lefts, starts, add is not None),
        grid_spec=pltpu.PrefetchScalarGridSpec(
            num_scalar_prefetch=1,
            grid=(count // tile_m, at),
            in_specs=specs,
            out_specs=pl.BlockSpec((tile_m, tile_n), lambda i, j, t: (i, j)),
        ),
        out_shape=jax.ShapeDtypeStruct((count, width), jnp.bfloat16),
        compiler_params=pltpu.CompilerParams(vmem_limit_bytes=32 << 20),
        cost_estimate=BRIEF,
        name="grad_rows",
    )(jnp.zeros((1,), jnp.int32) if table is None else table, *operands)


def project(x, gain, w_qkv):
    normed = (x * inv_rms(x) * gain).astype(jnp.bfloat16)
    return normed, matmul_rows(normed, w_qkv).astype(jnp.bfloat16)


def widen(attended, gain, w_inner):
    normed_mlp = (attended * inv_rms(attended) * gain).astype(jnp.bfloat16)
    return (normed_mlp,) + gelu_pair(matmul_rows(normed_mlp, w_inner))


def backward(plan, grad_out, layers, pos, bias, blk, table, output_half):
    low, f32 = jnp.bfloat16, jnp.float32
    previous = None
    results, diags = [], []
    for weights, saved, orders in layers:
        attn_gain, w_qkv, w_output, mlp_gain, w_inner, w_outer = weights
        x, queries, keys, values, context, log_total, attended, hidden, slope, left_m, left_c, n_qk, n_v = saved
        width = x.shape[1]
        grad_low = grad_out.astype(low)
        wide = hidden.shape[1]
        blocks = table[orders[1]]

        def outer_rows(a, b, add, hidden=hidden, grad_low=grad_low, blocks=blocks, wide=wide):
            if wide // blocks.shape[0] == TILE:
                return grad_rows([(hidden, grad_low, 0, 1)], a, b, add, blocks)
            rows = plan.take_blocks(matmul_left(hidden, grad_low).astype(low), blocks)[a:b]
            return rows if add is None else add_low(rows, add[0][add[1]:add[1] + b - a])

        def rows_of(*pairs):
            return lambda a, b, add: grad_rows(pairs, a, b, add)

        outer = Chain(plan, outer_rows, orders[1], wide)
        leaving = Held(output_half)
        late = [previous.outer.side, previous.inner.side] if previous else [leaving]
        grad_out = tie(grad_out, outer.one(), *late)
        outer.send_one()
        if not previous:
            arrived = Held(plan.exchange(leaving.value, "s"))
        grad_pre, grad_attended, attn_low, grad_mlp_gain = mlp_back(grad_out, attended, mlp_gain, w_outer, w_inner, slope)
        late = [previous.qk.far, previous.ov.far] if previous else [arrived]
        grad_pre = tie(grad_pre, outer.other, *late)
        inner = Chain(plan, rows_of((left_m, grad_pre, 0, wide // 1024)), orders[0], width)
        late = []
        if previous:
            late = [part for c in (previous.qk, previous.ov) for part in (c.near(), c.three())]
            late += [previous.outer.close(), previous.inner.close()]
        grad_pre = tie(grad_pre, outer.two(), inner.one(), *late)
        outer.send_two()
        inner.send_one()
        if previous:
            previous.qk.send_three()
            previous.ov.send_three()
            previous.sum_mlp(plan)
        attn_low = tie(attn_low, inner.other)
        attn_low = tie(attn_low, inner.two())
        inner.send_two()
        grad_context = matmul_back(attn_low, w_output).astype(low)
        ready = [outer.near(), inner.near()]
        late = [previous.qk.side, previous.ov.side] if previous else []
        grad_context = tie(grad_context, *ready, *late)
        if previous:
            grad_context = tie(grad_context, previous.qk.close(), previous.ov.close())
            previous.sum_attn(plan)
        grad_query, dk, dv, diag = attn_bwd(pos, queries, grad_context, context, log_total, keys, values, bias, blk, 0, 1)
        late = [previous.mlp_sum] if previous else []
        last = tie(dv[-1], outer.far, inner.far, *late)
        grad_k = plan.reduce_keys(dk).astype(low)
        grad_v = plan.reduce_keys(list(dv[:-1]) + [last]).astype(low)
        k_held = Held(grad_k)
        grad_v = tie(grad_v, k_held, outer.three(), inner.three())
        grad_k = k_held.value
        outer.send_three()
        inner.send_three()
        tiles = width // 1024
        qk = Chain(plan, rows_of((n_qk, grad_query, 0, tiles), (n_qk, grad_k, 0, tiles)), orders[2], width)
        ov = Chain(plan, rows_of((left_c, attn_low, 0, tiles), (n_v, grad_v, 0, tiles)), orders[3], width)
        grad_v = tie(grad_v, qk.one(), ov.one())
        qk.send_one()
        ov.send_one()
        grad_out, grad_attn_gain = project_back(grad_attended, x, attn_gain, grad_query, grad_k, grad_v, w_qkv)
        grad_out = tie(grad_out, qk.other, ov.other)
        grad_out = tie(grad_out, qk.two(), ov.two(), outer.close_by, inner.close_by)
        qk.send_two()
        ov.send_two()
        previous = LayerSums(outer, inner, qk, ov, grad_attn_gain, grad_mlp_gain, width)
        results.append(previous)
        diags.append(diag)
    outer.close()
    inner.close()
    previous.sum_mlp(plan)
    grad_out = tie(grad_out, qk.far, ov.far, qk.near(), ov.near())
    grad_out = tie(grad_out, qk.three(), ov.three())
    qk.send_three()
    ov.send_three()
    qk.close()
    qk.piece.value = tie(qk.piece.value, ov.close(), previous.mlp_sum, results[0].attn_sum)
    previous.sum_attn(plan)
    return grad_out, results, diags, arrived.value


class LayerSums:
    def __init__(self, outer, inner, qk, ov, grad_attn_gain, grad_mlp_gain, width):
        self.outer, self.inner, self.qk, self.ov = outer, inner, qk, ov
        self.attn_gain, self.mlp_gain, self.width = grad_attn_gain, grad_mlp_gain, width

    def sum_mlp(self, plan):
        w = self.width
        inner, outer = self.inner.piece.value, self.outer.piece.value
        self.runs, self.depth = inner.shape[2] // w, inner.shape[1]
        stacked = [inner[:, :, i * w:(i + 1) * w] for i in range(self.runs)]
        self.mlp_sum = Held(plan.sum_z(jnp.concatenate(stacked + [outer], axis=1)))

    def sum_attn(self, plan):
        self.attn_sum = Held(plan.sum_z(jnp.concatenate([c.piece.value for c in (self.qk, self.ov)], axis=2)))

    def grads(self):
        w = self.width
        f32 = jnp.float32
        query, key, output, value = [self.attn_sum.value[:, i * w:(i + 1) * w].astype(f32) for i in range(4)]
        both = self.mlp_sum.value.astype(f32)
        d = self.depth
        inner = jnp.concatenate([both[i * d:(i + 1) * d] for i in range(self.runs)], axis=1)
        return [self.attn_gain, query, key, value, output, self.mlp_gain, inner, both[self.runs * d:]]


def body(sizes, inputs, cotangent, lengths, bucket_ids, *params):
    plan = Plan(sizes)
    one, bias_table, two = params[:8], params[8], params[9:]
    blk, width = inputs.shape[1], inputs.shape[2]
    f32, low = jnp.float32, jnp.bfloat16
    gains = jnp.stack([one[0], one[5], two[0], two[5]], axis=1)
    rows = gains.shape[0]
    table_column = jnp.pad(bias_table, (0, rows - bias_table.shape[0]))[:, None] if bias_table.shape[0] < rows else bias_table[:rows, None]
    small = jnp.pad(jnp.concatenate([gains, table_column], axis=1), ((0, 0), (0, TILE - 5)))
    everywhere = plan.everywhere

    length = lax.dynamic_index_in_dim(lengths, plan.s, 0, keepdims=False)
    pos = plan.positions(length, blk)
    row = jnp.arange(blk, dtype=jnp.int32)
    row_pos = jnp.concatenate([row + pos[1] * TILE, row + pos[2] * TILE])
    row_valid = (row_pos < length).astype(f32)[:, None]

    xy, yx = ("x", "y"), ("y", "x")
    perms = {o: plan.permutation(o, width) for o in (xy, yx)}

    def permuted(rows_low, order):
        return Held(matmul_rows(rows_low, perms[order]).astype(low))

    shards = (
        jnp.concatenate([one[1], one[2], one[3], one[4], small], axis=1),
        one[6],
        one[7],
        jnp.concatenate([two[1], two[2], two[3], two[4]], axis=1),
        two[6],
        two[7],
    )
    attn_1, inner_1, outer_1, attn_2, inner_2, outer_2 = [Fetch(plan, piece) for piece in shards]
    attn_1.start()
    x = plan.to_sequences(inputs)
    cotangent = plan.to_sequences(cotangent)
    x = tie(x, inner_1.shard)
    inner_1.start()
    held = Held(cotangent)
    x = tie(x, held)
    cotangent = held.value
    x = attn_1.a(x, outer_1)
    x = attn_1.b(x)
    x = inner_1.a(x, attn_2)
    x, first = attn_1.c(x)
    picks = jnp.eye(8, TILE, dtype=low)
    smalls = matmul_back(picks, first[:, 4 * width:])
    gain = smalls[:4]
    whole_table = smalls[4].reshape(-1, rows)[:, :bias_table.shape[0]].reshape(-1)
    heads = width // DK
    buckets = whole_table.shape[0] // heads
    reversed_ids = jnp.concatenate([jnp.full((1,), -1, jnp.int32), bucket_ids[::-1]])
    indicator = (reversed_ids[None, :] == jnp.arange(buckets, dtype=jnp.int32)[:, None]).astype(low)
    vector = Held(matmul_rows(whole_table.reshape(heads, buckets).astype(low), indicator))
    x_one = x.astype(f32)
    normed_one, qkv = project(x_one, gain[0:1], first[:, :3 * width])
    qkv = inner_1.b(qkv)
    qkv = outer_1.a(qkv, inner_2)
    kv = plan.gather_keys(qkv[:, width:])
    qkv = tie(qkv, vector)
    bias = Held(toeplitz_tiles(vector.value))
    qkv = tie(qkv, bias)
    bias = bias.value
    queries_one = qkv[:, :width]
    keys_one, values_one = [p[:, :width] for p in kv], [p[:, width:] for p in kv]
    context_one, log_one = attn_fwd(pos, queries_one, keys_one, values_one, bias, blk)
    n_yx_one, n_xy_one = permuted(normed_one, yx), permuted(normed_one, xy)
    context_one, w_inner_one = inner_1.c(context_one, lambda main: attn_2.a(outer_1.b(main, n_xy_one), outer_2), [n_yx_one])
    c_one = permuted(context_one, xy)
    attended_one = x_one + matmul_rows(context_one, first[:, 3 * width:4 * width])
    normed_mlp_one, hidden_one, slope_one = widen(attended_one, gain[1:2], w_inner_one)
    slope_one = Held(slope_one)
    hidden_one = tie(hidden_one, slope_one)
    slope_one = slope_one.value
    m_one = permuted(normed_mlp_one, xy)
    hidden_one, w_outer_one = outer_1.c(hidden_one, None, [c_one])
    hidden_one = attn_2.b(hidden_one, m_one)
    hidden_one = inner_2.a(hidden_one)
    x_two = attended_one + matmul_rows(hidden_one, w_outer_one)
    x_two, third = attn_2.c(x_two)
    normed_two, qkv = project(x_two, gain[2:3], third[:, :3 * width])
    qkv = inner_2.b(qkv)
    qkv = outer_2.a(qkv)
    kv = plan.gather_keys(qkv[:, width:])
    queries_two = qkv[:, :width]
    keys_two, values_two = [p[:, :width] for p in kv], [p[:, width:] for p in kv]
    context_two, log_two = attn_fwd(pos, queries_two, keys_two, values_two, bias, blk)
    n_yx_two, n_xy_two = permuted(normed_two, yx), permuted(normed_two, xy)
    context_two, w_inner_two = inner_2.c(context_two, None, [n_yx_two])
    context_two = outer_2.b(context_two, n_xy_two)
    c_two = permuted(context_two, xy)
    attended_two = x_two + matmul_rows(context_two, third[:, 3 * width:])
    normed_mlp_two, hidden_two, slope_two = widen(attended_two, gain[3:4], w_inner_two)
    slope_two = Held(slope_two)
    hidden_two = tie(hidden_two, slope_two)
    slope_two = slope_two.value
    hidden_two, w_outer_two = outer_2.c(hidden_two, None, [c_two])
    m_two = permuted(normed_mlp_two, xy)
    final = attended_two + matmul_rows(hidden_two, w_outer_two)
    output_rows = (final * row_valid).astype(low)
    grad_out = cotangent.astype(f32) * row_valid

    weights_one = (gain[0:1], first, first[:, 3 * width:4 * width], gain[1:2], w_inner_one, w_outer_one)
    weights_two = (gain[2:3], third, third[:, 3 * width:], gain[3:4], w_inner_two, w_outer_two)
    saved_one = (x, queries_one, keys_one, values_one, context_one, log_one, attended_one, hidden_one, slope_one, m_one.value, c_one.value, n_yx_one.value, n_xy_one.value)
    saved_two = (x_two, queries_two, keys_two, values_two, context_two, log_two, attended_two, hidden_two, slope_two, m_two.value, c_two.value, n_yx_two.value, n_xy_two.value)

    depth = one[7].shape[0]
    step = TILE if depth % TILE == 0 else depth
    blocks = jnp.arange(hidden_one.shape[1] // step, dtype=jnp.int32)
    per = depth // step
    table = {o: plan.block_of(o, blocks // per) * per + blocks % per for o in (xy, yx)}
    layers = [(weights_two, saved_two, (xy, yx, yx, xy)), (weights_one, saved_one, (xy, yx, yx, xy))]
    grad_state, sums, diags, arrived = backward(plan, grad_out, layers, pos, bias, blk, table, output_rows[blk:])
    output = plan.in_order(output_rows[:blk], arrived)
    grads_two, grads_one = sums[0].grads(), sums[1].grads()
    input_grad = plan.from_sequences(grad_state.astype(low))

    grad_table = lax.dot_general(diags[0] + diags[1], indicator.astype(f32), (((1,), (1,)), ((), ())), precision=HIGH_PRECISION)
    vectors = jnp.concatenate([grads_one[0][0], grads_one[5][0], grads_two[0][0], grads_two[5][0], grad_table.reshape(-1)])
    held = Held(vectors)
    grad_state = tie(grad_state, held)
    vectors = plan.sum_vector(held.value)
    device = ((plan.z * plan.ny + plan.y) * plan.nx + plan.x) * 2 + plan.core

    def share(start, count):
        return lax.dynamic_slice_in_dim(vectors, start + device * count, count, 0)

    gain_grads = [share(i * width, rows) for i in range(4)]
    table_grad = share(4 * width, bias_table.shape[0])
    return (
        output,
        input_grad,
        gain_grads[0],
        *grads_one[1:5],
        gain_grads[1],
        *grads_one[6:],
        table_grad,
        gain_grads[2],
        *grads_two[1:5],
        gain_grads[3],
        *grads_two[6:],
    )


def solution(mesh):
    dp, cp = mesh.shape["dp"], mesh.shape["cp"]
    nx = cp // 2
    ny = nx if dp % nx == 0 else 1

    def run(inputs, *rest):
        ns = inputs.shape[0] // dp
        assert ns == 2 and nx % ns == 0
        sizes = (dp // ny, ny, ns, nx // ns)
        finer = Mesh(mesh.devices.reshape(*sizes, 2), ("z", "y", "s", "q", "core"))
        dpn, cpn = ("z", "y"), ("s", "q", "core")
        tokens = P(dpn, cpn, None)
        vector, matrix = P(dpn + cpn), P(dpn + cpn, None)
        layer = (vector, matrix, matrix, matrix, matrix, vector, matrix, matrix)
        return jax.shard_map(
            functools.partial(body, sizes),
            mesh=finer,
            in_specs=(tokens, tokens, P(dpn), P()) + layer + (vector,) + layer,
            out_specs=(tokens, tokens) + layer + (vector,) + layer,
            check_vma=False,
        )(inputs, *rest)

    return run
```

```python
import functools

import jax
import jax.numpy as jnp
import numpy as np
from jax import lax
from jax.experimental import pallas as pl
from jax.experimental.pallas import tpu as pltpu
from jax.sharding import Mesh
from jax.sharding import PartitionSpec as P

DK = 64
TILE = 128
EPS = 1e-06
NEGATIVE = -1e30
HIGH_PRECISION = lax.Precision.HIGHEST
BRIEF = pl.CostEstimate(flops=1024, bytes_accessed=1024, transcendentals=0)


def toeplitz_kernel(span, u_ref, t_ref):
    rolled = jnp.broadcast_to(u_ref[0], (TILE, u_ref.shape[2]))
    rolled = pltpu.roll(rolled, 0, 1, stride=1, stride_axis=0)
    for e in range(span):
        base = TILE * (span - e)
        t_ref[0, e] = rolled[:, base:base + TILE].astype(t_ref.dtype)

def toeplitz_tiles(u):
    heads, width = u.shape
    span = width // TILE - 1
    return pl.pallas_call(
        functools.partial(toeplitz_kernel, span),
        grid=(heads,),
        in_specs=[pl.BlockSpec((1, 1, width), lambda h: (h, 0, 0))],
        out_specs=pl.BlockSpec((1, span, TILE, TILE), lambda h: (h, 0, 0, 0)),
        out_shape=jax.ShapeDtypeStruct((heads, span, TILE, TILE), jnp.bfloat16),
        cost_estimate=BRIEF,
        name="toeplitz",
    )(u.reshape(heads, 1, width))

def head_lanes(h, x):
    lane = lax.broadcasted_iota(jnp.int32, x.shape, 1)
    return jnp.where((lane // DK) == h, x, jnp.zeros_like(x))

def dot_nt(a, b):
    return lax.dot_general(a, b, (((1,), (1,)), ((), ())), preferred_element_type=jnp.float32)

def dot_tn(a, b):
    return lax.dot_general(a, b, (((0,), (0,)), ((), ())), preferred_element_type=jnp.float32)

def dot_nn(a, b):
    return lax.dot_general(a, b, (((1,), (0,)), ((), ())), preferred_element_type=jnp.float32)

def key_chunks(parts, rows, chunk):
    return [(i, s) for i in range(parts) for s in range(0, rows, chunk)]

def chunk_scores(pos_ref, k_chunk, q_head, bias_ref, h, c, chunk, blk, q_rows):
    n = chunk // blk
    sub = blk // TILE
    nq = q_rows // blk
    s = dot_nt(k_chunk, q_head)
    half = bias_ref.shape[1] // 2
    rows = []
    for kb in range(n):
        kpos = pos_ref[1 + nq + c * n + kb]
        for kk in range(sub):
            cols = []
            for qb in range(nq):
                e0 = (kpos - pos_ref[1 + qb]) + half + kk
                for qq in range(sub):
                    cols.append(bias_ref[h, e0 - qq])
            rows.append(jnp.concatenate(cols, axis=1))
    bias = jnp.concatenate(rows, axis=0).astype(jnp.float32)
    s = s + bias
    valid = []
    for kb in range(n):
        limit = pos_ref[0] - pos_ref[1 + nq + c * n + kb] * TILE
        valid.append(lax.broadcasted_iota(jnp.int32, (blk, 1), 0) < limit)
    ok = valid[0] if n == 1 else jnp.concatenate([v.astype(jnp.int32) for v in valid], axis=0) > 0
    return s, ok

def attn_fwd_kernel(parts, chunk, blk, pos_ref, q_ref, *refs):
    k_refs, v_refs = refs[:parts], refs[parts:2 * parts]
    bias_ref, o_ref, lse_ref, s_ref = refs[2 * parts:]
    q_rows = q_ref.shape[0]
    rows = k_refs[0].shape[0]
    chunks = key_chunks(parts, rows, chunk)
    outs = []
    for h in range(2):
        qh = head_lanes(h, q_ref[...])
        top = None
        for c, (i, s0) in enumerate(chunks):
            s, ok = chunk_scores(pos_ref, k_refs[i][s0:s0 + chunk, :], qh, bias_ref, h, c, chunk, blk, q_rows)
            s = jnp.where(ok, s, NEGATIVE)
            s_ref[c * chunk:(c + 1) * chunk, :] = s
            m = jnp.max(s, axis=0, keepdims=True)
            top = m if top is None else jnp.maximum(top, m)
        total = jnp.zeros((1, q_rows), jnp.float32)
        acc = jnp.zeros((2 * DK, q_rows), jnp.float32)
        for c, (i, s0) in enumerate(chunks):
            p = jnp.exp(s_ref[c * chunk:(c + 1) * chunk, :] - top)
            total = total + jnp.sum(p, axis=0, keepdims=True)
            acc = acc + dot_tn(v_refs[i][s0:s0 + chunk, :], p.astype(jnp.bfloat16))
        outs.append((acc / total)[h * DK:(h + 1) * DK])
        lse_ref[0, h:h + 1, :] = top + jnp.log(total)
    o_ref[...] = jnp.concatenate(outs, axis=0).T.astype(o_ref.dtype)

def attn_fwd(pos, q, ks, vs, bias, blk):
    q_rows, width = q.shape
    parts, rows = len(ks), ks[0].shape[0]
    keys = parts * rows
    heads = width // DK
    span = bias.shape[1]
    chunk = min(256, rows)
    spec_q = pl.BlockSpec((q_rows, 2 * DK), lambda p, s: (0, p))
    spec_k = pl.BlockSpec((rows, 2 * DK), lambda p, s: (0, p))
    o, lse = pl.pallas_call(
        functools.partial(attn_fwd_kernel, parts, chunk, blk),
        grid_spec=pltpu.PrefetchScalarGridSpec(
            num_scalar_prefetch=1,
            grid=(heads // 2,),
            in_specs=[spec_q] + [spec_k] * (2 * parts) + [pl.BlockSpec((2, span, TILE, TILE), lambda p, s: (p, 0, 0, 0))],
            out_specs=[spec_q, pl.BlockSpec((1, 2, q_rows), lambda p, s: (p, 0, 0))],
            scratch_shapes=[pltpu.VMEM((keys, q_rows), jnp.float32)],
        ),
        out_shape=[jax.ShapeDtypeStruct((q_rows, width), jnp.bfloat16), jax.ShapeDtypeStruct((heads // 2, 2, q_rows), jnp.float32)],
        compiler_params=pltpu.CompilerParams(vmem_limit_bytes=60 << 20),
        cost_estimate=BRIEF,
        name="attn_fwd",
    )(pos, q, *ks, *vs, bias)
    return o, lse

def skew_rows(x):
    width = 2 * x.shape[1]
    x = jnp.concatenate([jnp.zeros_like(x), x], axis=1)
    rows = x.shape[0]
    while rows > 8:
        rows //= 2
        x = x[:rows] + pltpu.roll(x[rows:], width - rows, 1)
    row = lax.broadcasted_iota(jnp.int32, x.shape, 0)
    for bit in (1, 2, 4):
        x = jnp.where((row & bit) != 0, pltpu.roll(x, width - bit, 1), x)
    return x

def attn_bwd_kernel(parts, chunk, blk, pos_ref, q_ref, do_ref, o_ref, lse_ref, *refs):
    k_refs, v_refs = refs[:parts], refs[parts:2 * parts]
    bias_ref, dq_ref = refs[2 * parts:2 * parts + 2]
    dk_refs, dv_refs = refs[2 * parts + 2:3 * parts + 2], refs[3 * parts + 2:4 * parts + 2]
    d_ref, e_ref = refs[4 * parts + 2:]
    q_rows = q_ref.shape[0]
    rows = k_refs[0].shape[0]
    chunks = key_chunks(parts, rows, chunk)
    span = bias_ref.shape[1]
    half = span // 2
    n, sub, nq = chunk // blk, blk // TILE, q_rows // blk
    prod = (do_ref[...].astype(jnp.float32) * o_ref[...].astype(jnp.float32)).T
    outs = []
    for h in range(2):
        qh = head_lanes(h, q_ref[...])
        doh = head_lanes(h, do_ref[...])
        inner = jnp.sum(prod[h * DK:(h + 1) * DK], axis=0, keepdims=True)
        lse = lse_ref[0, h:h + 1, :]
        acc = jnp.zeros((2 * DK, q_rows), jnp.float32)
        e_ref[...] = jnp.zeros_like(e_ref)
        for c, (i, s0) in enumerate(chunks):
            k_chunk = k_refs[i][s0:s0 + chunk, :]
            s, ok = chunk_scores(pos_ref, k_chunk, qh, bias_ref, h, c, chunk, blk, q_rows)
            p = jnp.where(ok, jnp.exp(s - lse), 0.0)
            dp = dot_nt(v_refs[i][s0:s0 + chunk, :], doh)
            ds = p * (dp - inner)
            dsb = ds.astype(jnp.bfloat16)
            dv = dot_nn(p.astype(jnp.bfloat16), doh)
            dk = dot_nn(dsb, qh)
            at = pl.ds(s0, chunk)
            if h == 0:
                dk_refs[i][at, :] = dk.astype(jnp.bfloat16)
                dv_refs[i][at, :] = dv.astype(jnp.bfloat16)
            else:
                dk_refs[i][at, :] = (dk_refs[i][at, :].astype(jnp.float32) + dk).astype(jnp.bfloat16)
                dv_refs[i][at, :] = (dv_refs[i][at, :].astype(jnp.float32) + dv).astype(jnp.bfloat16)
            acc = acc + dot_tn(k_chunk, dsb)
            for kb in range(n):
                kpos = pos_ref[1 + nq + c * n + kb]
                for qb in range(nq):
                    e0 = (kpos - pos_ref[1 + qb]) + half
                    for d in range(1 - sub, sub):
                        tot = None
                        for kk in range(sub):
                            qq = kk - d
                            if 0 <= qq < sub:
                                r0, c0 = kb * blk + kk * TILE, qb * blk + qq * TILE
                                t = ds[r0:r0 + TILE, c0:c0 + TILE]
                                tot = t if tot is None else tot + t
                        e_ref[e0 + d] += tot
        outs.append(acc[h * DK:(h + 1) * DK])
        pieces = [jnp.zeros((1, TILE), jnp.float32) for _ in range(span + 1)]
        for e in range(span):
            r = jnp.sum(skew_rows(e_ref[e]), axis=0, keepdims=True)
            b = span - 1 - e
            pieces[b] = pieces[b] + r[:, :TILE]
            pieces[b + 1] = pieces[b + 1] + r[:, TILE:]
        d_ref[0, h:h + 1, :] = jnp.concatenate(pieces, axis=1)
    dq_ref[...] = jnp.concatenate(outs, axis=0).T.astype(dq_ref.dtype)

def attn_bwd(pos, q, do, o, lse, ks, vs, bias, blk, share, shares):
    q_rows, width = q.shape
    parts, rows = len(ks), ks[0].shape[0]
    keys = parts * rows
    heads = width // DK // shares
    width = width // shares
    span = bias.shape[1]
    chunk = min(256, rows)
    first = share * (heads // 2)
    spec_q = pl.BlockSpec((q_rows, 2 * DK), lambda p, s: (0, first + p))
    spec_k = pl.BlockSpec((rows, 2 * DK), lambda p, s: (0, first + p))
    spec_l = pl.BlockSpec((1, 2, q_rows), lambda p, s: (first + p, 0, 0))
    spec_b = pl.BlockSpec((2, span, TILE, TILE), lambda p, s: (first + p, 0, 0, 0))
    out_q = pl.BlockSpec((q_rows, 2 * DK), lambda p, s: (0, p))
    out_k = pl.BlockSpec((rows, 2 * DK), lambda p, s: (0, p))
    out = pl.pallas_call(
        functools.partial(attn_bwd_kernel, parts, chunk, blk),
        grid_spec=pltpu.PrefetchScalarGridSpec(
            num_scalar_prefetch=1,
            grid=(heads // 2,),
            in_specs=[spec_q, spec_q, spec_q, spec_l] + [spec_k] * (2 * parts) + [spec_b],
            out_specs=[out_q] + [out_k] * (2 * parts) + [pl.BlockSpec((1, 2, (span + 1) * TILE), lambda p, s: (p, 0, 0))],
            scratch_shapes=[pltpu.VMEM((span, TILE, TILE), jnp.float32)],
        ),
        out_shape=[jax.ShapeDtypeStruct((q_rows, width), jnp.bfloat16)]
        + [jax.ShapeDtypeStruct((rows, width), jnp.bfloat16)] * (2 * parts)
        + [jax.ShapeDtypeStruct((heads // 2, 2, (span + 1) * TILE), jnp.float32)],
        compiler_params=pltpu.CompilerParams(vmem_limit_bytes=60 << 20),
        cost_estimate=pl.CostEstimate(flops=40 * q_rows * keys * width, bytes_accessed=8 * keys * width + 8 * q_rows * width, transcendentals=heads * q_rows * keys),
        name="attn_bwd",
    )(pos, q, do, o, lse, *ks, *vs, bias)
    dq, dks, dvs, d = out[0], out[1:1 + parts], out[1 + parts:1 + 2 * parts], out[-1]
    return dq, dks, dvs, d.reshape(heads, (span + 1) * TILE)


def matmul_rows(left, right):
    return jnp.dot(left, right, preferred_element_type=jnp.float32)


def matmul_left(left, right):
    return lax.dot_general(left, right, (((0,), (0,)), ((), ())), preferred_element_type=jnp.float32)


def matmul_back(left, right):
    return lax.dot_general(left, right, (((1,), (1,)), ((), ())), preferred_element_type=jnp.float32)


def inv_rms(values):
    return lax.rsqrt(jnp.mean(values * values, axis=-1, keepdims=True) + EPS)


def norm_back(grad, values, gain):
    scale = inv_rms(values)
    weighted = gain * grad
    mean = jnp.mean(weighted * values, axis=-1, keepdims=True)
    grad_in = scale * weighted - values * (scale * scale * scale) * mean
    return grad_in, jnp.sum(grad * values * scale, axis=0, keepdims=True)


def mlp_back_kernel(grad_ref, value_ref, gain_ref, outer_ref, inner_ref, slope_ref, pre_ref, out_ref, low_ref, gain_grad_ref, acc_ref, left_ref):
    i = pl.program_id(0)

    @pl.when(i == 0)
    def _():
        left_ref[...] = grad_ref[...].astype(jnp.bfloat16)
        acc_ref[...] = jnp.zeros_like(acc_ref)

    grad_pre = (dot_nt(left_ref[...], outer_ref[...]) * slope_ref[...].astype(jnp.float32)).astype(jnp.bfloat16)
    pre_ref[...] = grad_pre
    acc_ref[...] += dot_nt(grad_pre, inner_ref[...])

    @pl.when(i == pl.num_programs(0) - 1)
    def _():
        grad_in, grad_gain = norm_back(acc_ref[...], value_ref[...], gain_ref[...])
        total = grad_ref[...] + grad_in
        out_ref[...] = total
        low_ref[...] = total.astype(jnp.bfloat16)
        gain_grad_ref[...] = grad_gain


def mlp_back(grad_out, attended, gain, w_outer, w_inner, slope):
    rows, width = grad_out.shape
    wide = w_outer.shape[0]
    tile = min(1024, wide)
    whole = pl.BlockSpec((rows, width), lambda i: (0, 0))
    line = pl.BlockSpec((1, width), lambda i: (0, 0))
    return pl.pallas_call(
        mlp_back_kernel,
        grid=(wide // tile,),
        in_specs=[
            whole,
            whole,
            line,
            pl.BlockSpec((tile, width), lambda i: (i, 0)),
            pl.BlockSpec((width, tile), lambda i: (0, i)),
            pl.BlockSpec((rows, tile), lambda i: (0, i)),
        ],
        out_specs=[pl.BlockSpec((rows, tile), lambda i: (0, i)), whole, whole, line],
        out_shape=[
            jax.ShapeDtypeStruct((rows, wide), jnp.bfloat16),
            jax.ShapeDtypeStruct((rows, width), jnp.float32),
            jax.ShapeDtypeStruct((rows, width), jnp.bfloat16),
            jax.ShapeDtypeStruct((1, width), jnp.float32),
        ],
        scratch_shapes=[pltpu.VMEM((rows, width), jnp.float32), pltpu.VMEM((rows, width), jnp.bfloat16)],
        compiler_params=pltpu.CompilerParams(vmem_limit_bytes=60 << 20),
        cost_estimate=BRIEF,
        name="mlp_back",
    )(grad_out, attended, gain, w_outer, w_inner, slope)


def project_back_kernel(add_ref, value_ref, gain_ref, q_ref, k_ref, v_ref, w_ref, out_ref, gain_grad_ref, acc_ref):
    i = pl.program_id(0)
    for j, r in enumerate((q_ref, k_ref, v_ref)):

        @pl.when(i == j)
        def _(j=j, r=r):
            part = dot_nt(r[...], w_ref[...])
            acc_ref[...] = part if j == 0 else acc_ref[...] + part

    @pl.when(i == 2)
    def _():
        grad_in, grad_gain = norm_back(acc_ref[...], value_ref[...].astype(jnp.float32), gain_ref[...])
        out_ref[...] = add_ref[...] + grad_in
        gain_grad_ref[...] = grad_gain


def project_back(grad_attended, x, gain, grad_query, grad_k, grad_v, w):
    rows, width = x.shape
    whole = pl.BlockSpec((rows, width), lambda i: (0, 0))
    line = pl.BlockSpec((1, width), lambda i: (0, 0))
    return pl.pallas_call(
        project_back_kernel,
        grid=(3,),
        in_specs=[whole, whole, line, whole, whole, whole, pl.BlockSpec((width, width), lambda i: (0, i))],
        out_specs=[whole, line],
        out_shape=[jax.ShapeDtypeStruct((rows, width), jnp.float32), jax.ShapeDtypeStruct((1, width), jnp.float32)],
        scratch_shapes=[pltpu.VMEM((rows, width), jnp.float32)],
        compiler_params=pltpu.CompilerParams(vmem_limit_bytes=60 << 20),
        cost_estimate=BRIEF,
        name="project_back",
    )(grad_attended, x, gain, grad_query, grad_k, grad_v, w)


def gelu_pair(pre):
    c = np.float32(np.sqrt(2.0 / np.pi))
    sq = pre * pre
    t = jnp.tanh(c * (pre + 0.044715 * (sq * pre)))
    half = 0.5 * (1.0 + t)
    slope = half + (0.5 * c) * pre * (1.0 - t * t) * (1.0 + 0.134145 * sq)
    return (pre * half).astype(jnp.bfloat16), slope.astype(jnp.bfloat16)


SWAP = [(0, 1), (1, 0)]


class Plan:
    def __init__(self, sizes):
        self.nz, self.ny, self.ns, self.m = sizes
        self.nx = self.ns * self.m
        self.z = lax.axis_index("z")
        self.y = lax.axis_index("y")
        self.s = lax.axis_index("s")
        self.q = lax.axis_index("q")
        self.core = lax.axis_index("core")
        self.x = self.s * self.m + self.q
        self.everywhere = ("z", "y", "s", "q", "core")
        self.axes = {"x": (("s", "q") if self.m > 1 else "s", self.nx, self.x), "y": ("y", self.ny, self.y)}

    def block_of(self, order, n):
        n_z = n % self.nz
        n = n // self.nz
        place = {}
        for name in reversed(order):
            _, size, mine = self.axes[name]
            part = n % size
            n = n // size
            place[name] = part ^ mine if size == 2 else part
        core = n ^ self.core
        return ((n_z * self.ny + place["y"]) * self.nx + place["x"]) * 2 + core

    def permutation(self, order, width):
        depth = width // (self.nz * self.ny * self.nx * 2)
        n = lax.broadcasted_iota(jnp.int32, (width, width), 1)
        i = lax.broadcasted_iota(jnp.int32, (width, width), 0)
        source = self.block_of(order, n // depth) * depth + n % depth
        return (i == source).astype(jnp.bfloat16)

    def take_blocks(self, rows, table):
        return jnp.take(rows.reshape(table.shape[0], -1, rows.shape[1]), table, axis=0).reshape(rows.shape)

    def exchange(self, piece, name):
        return lax.ppermute(piece, name, SWAP)

    def sum_z(self, piece):
        if self.nz == 1:
            return piece[0]
        return lax.psum_scatter(piece, "z", scatter_dimension=0, tiled=False)

    def sum_vector(self, vector):
        for name, size in (("core", 2), ("z", self.nz), ("y", self.ny), ("q", self.m), ("s", self.ns)):
            if size & (size - 1):
                vector = lax.psum(vector, name)
                continue
            step = 1
            while step < size:
                vector = vector + lax.ppermute(vector, name, [(i, i ^ step) for i in range(size)])
                step *= 2
        return vector

    def to_sequences(self, local):
        own = lax.dynamic_index_in_dim(local, self.s, 0, keepdims=False)
        other = lax.dynamic_index_in_dim(local, 1 - self.s, 0, keepdims=False)
        return jnp.concatenate([own, self.exchange(other, "s")], axis=0)

    def from_sequences(self, rows):
        blk = rows.shape[0] // 2
        return self.in_order(rows[:blk], self.exchange(rows[blk:], "s"))

    def in_order(self, own, other):
        first = self.s == 0
        return jnp.stack([jnp.where(first, own, other), jnp.where(first, other, own)], axis=0)

    def gather_keys(self, rows):
        if self.m == 1:
            return [rows, self.exchange(rows, "core")]
        return [lax.all_gather(rows, ("q", "core"), axis=0, tiled=True)]

    def reduce_keys(self, parts):
        if self.m == 1:
            return add_rows(parts[0].shape[0], (parts[0], 0), (self.exchange(parts[1], "core"), 0))
        return lax.psum_scatter(parts[0], ("q", "core"), scatter_dimension=0, tiled=True).astype(jnp.float32)

    def positions(self, length, blk):
        unit = blk // TILE
        mine = [(((self.s ^ j) * self.m + self.q) * 2 + self.core) * unit for j in range(2)]
        if self.m == 1:
            keys = [(((self.s ^ j) * self.m + self.q) * 2 + (self.core ^ c)) * unit for c in range(2) for j in range(2)]
        else:
            keys = [(((self.s ^ j) * self.m + q) * 2 + c) * unit for q in range(self.m) for c in range(2) for j in range(2)]
        return jnp.stack([length] + mine + keys).astype(jnp.int32)


def assemble_kernel(steps, depth, table_ref, *refs):
    i = pl.program_id(0)
    out = refs[-1]
    core, x = table_ref[0], table_ref[1]
    quads = [refs[j:j + 4] for j in range(0, len(refs) - 1, 4)]
    for quad, (start, count) in zip(quads, steps):

        @pl.when(jnp.logical_and(i >= start, i < start + count))
        def _(quad=quad):
            for j, r in enumerate(quad):
                place = (x ^ (j // 2)) * 2 + (core ^ (j % 2))
                out[pl.ds(pl.multiple_of(place * depth, depth), depth), :] = r[...]


def assemble(table, quads, depth):
    width = quads[0][0].shape[1]
    steps, at = [], 0
    for q in quads:
        steps.append((at, q[0].shape[0] // depth))
        at += q[0].shape[0] // depth

    def source_map(start, count):
        return lambda i, t: (jnp.clip(i - start, 0, count - 1), 0)

    return pl.pallas_call(
        functools.partial(assemble_kernel, steps, depth),
        grid_spec=pltpu.PrefetchScalarGridSpec(
            num_scalar_prefetch=1,
            grid=(at,),
            in_specs=[pl.BlockSpec((depth, width), source_map(*s)) for s in steps for _ in range(4)],
            out_specs=pl.BlockSpec((4 * depth, width), lambda i, t: (t[2 + i], 0)),
        ),
        out_shape=jax.ShapeDtypeStruct((at * 4 * depth, width), quads[0][0].dtype),
        compiler_params=pltpu.CompilerParams(vmem_limit_bytes=60 << 20),
        cost_estimate=BRIEF,
        name="assemble",
    )(table, *[r for q in quads for r in q])


class Held:
    def __init__(self, value):
        self.value = value


def tie(main, *held):
    got = lax.optimization_barrier((main,) + tuple(h.value for h in held))
    for h, v in zip(held, got[1:]):
        h.value = v
    return got[0]


class Fetch:
    def __init__(self, plan, shard):
        self.plan, self.shard = plan, Held(shard)
        self.pairs = plan.nx == 2 and plan.ny == 2 and plan.nz % 2 == 0
        self.depth = shard.shape[0]

    def start(self):
        axes = "z" if self.pairs else self.plan.everywhere
        self.near = Held(lax.all_gather(self.shard.value, axes, axis=0, tiled=True))

    def send(self, piece, name):
        return Held(self.plan.exchange(piece.value, name))

    def send_in_plane(self):
        if self.pairs:
            self.by_x, self.by_y, self.near_twin = [self.send(self.near, n) for n in ("s", "y", "core")]

    def a(self, main, following=None):
        main = tie(main, self.near, *([following.shard] if following else []))
        if following:
            following.start()
        self.send_in_plane()
        return main

    def b(self, main, *fill):
        if not self.pairs:
            return main
        main = tie(main, self.by_x, self.by_y, self.near_twin)
        half = self.by_x.value.shape[0] // 2
        self.low = Held(self.plan.exchange(self.by_y.value[:half], "s"))
        self.high = Held(self.plan.exchange(self.by_x.value[half:], "y"))
        self.x_twin, self.y_twin = self.send(self.by_x, "core"), self.send(self.by_y, "core")
        return tie(main, self.x_twin, self.y_twin, *fill)

    def c(self, main, between=None, fill=()):
        if not self.pairs:
            return (between(main) if between else main), self.near.value
        plan = self.plan
        main = tie(main, self.low, self.high)
        twins = [self.send(p, "core") for p in (self.low, self.high)]
        main = tie(main, *twins, *fill)
        main = between(main) if between else main
        low_twin, high_twin = [t.value for t in twins]
        half = self.low.value.shape[0]
        by_y, y_twin = self.by_y.value, self.y_twin.value
        quads = [
            (self.near.value, self.near_twin.value, self.by_x.value, self.x_twin.value),
            (by_y[:half], y_twin[:half], self.low.value, low_twin),
            (by_y[half:], y_twin[half:], self.high.value, high_twin),
        ]
        z = jnp.arange(plan.nz, dtype=jnp.int32)
        order = jnp.concatenate([z * 2 + plan.y, z * 2 + (1 - plan.y)])
        table = jnp.concatenate([jnp.stack([plan.core, plan.x]).astype(jnp.int32), order.astype(jnp.int32)])
        whole = Held(assemble(table, quads, self.depth))
        main = tie(main, whole)
        return main, whole.value


def add_kernel(*refs):
    total = refs[0][...].astype(jnp.float32)
    for r in refs[1:-1]:
        total = total + r[...].astype(jnp.float32)
    refs[-1][...] = total.astype(refs[-1].dtype)


def add_rows(count, *terms):
    width = terms[0][0].shape[1]
    tile = count // 2
    return pl.pallas_call(
        add_kernel,
        grid=(2,),
        in_specs=[pl.BlockSpec((tile, width), lambda i, base=first // tile: (base + i, 0)) for _, first in terms],
        out_specs=pl.BlockSpec((tile, width), lambda i: (i, 0)),
        out_shape=jax.ShapeDtypeStruct((count, width), jnp.bfloat16),
        compiler_params=pltpu.CompilerParams(vmem_limit_bytes=60 << 20),
        cost_estimate=BRIEF,
        name="add_rows",
    )(*[array for array, _ in terms])


def add_low(*terms):
    total = terms[0].astype(jnp.float32)
    for t in terms[1:]:
        total = total + t.astype(jnp.float32)
    return total.astype(jnp.bfloat16)


class Chain:
    def __init__(self, plan, product, order, rows):
        self.plan, self.product, self.rows = plan, product, rows
        self.name_a, self.size_a, _ = plan.axes[order[0]]
        self.name_b, self.size_b, _ = plan.axes[order[1]]
        self.pairs = self.size_a == 2 and self.size_b == 2
        self.part = None

    def one(self):
        self.part = Held(self.product(self.rows // 2, self.rows, None))
        return self.part

    def send_one(self):
        self.other = Held(self.plan.exchange(self.part.value, "core"))

    def two(self):
        half = self.rows // 2
        if self.pairs:
            quarter = half // 2
            self.part = Held(self.product(quarter, half, (self.other.value, quarter)))
        else:
            self.part = Held(self.product(0, half, (self.other.value, 0)))
        return self.part

    def send_two(self):
        if self.pairs:
            self.far = Held(self.plan.exchange(self.part.value, self.name_a))
        else:
            whole = self.part.value.reshape(self.size_a, self.rows // (2 * self.size_a), -1)
            self.far = Held(lax.psum_scatter(whole, self.name_a, scatter_dimension=0, tiled=False))

    def near(self):
        if self.pairs:
            quarter = self.rows // 4
            self.close_by = Held(self.product(0, quarter, (self.other.value, 0)))
            return self.close_by
        self.close_by = self.far
        return self.close_by

    def three(self):
        if self.pairs:
            eighth = self.rows // 8
            self.part = Held(add_rows(eighth, (self.close_by.value, eighth), (self.far.value, eighth)))
        else:
            self.part = self.far
        return self.part

    def send_three(self):
        if self.pairs:
            self.side = Held(self.plan.exchange(self.part.value, self.name_b))
        else:
            whole = self.part.value.reshape(self.size_b, self.part.value.shape[0] // self.size_b, -1)
            self.side = Held(lax.psum_scatter(whole, self.name_b, scatter_dimension=0, tiled=False))

    def close(self):
        nz = self.plan.nz
        if self.pairs:
            eighth = self.rows // 8
            total = add_rows(eighth, (self.close_by.value, 0), (self.far.value, 0), (self.side.value, 0))
        else:
            total = self.side.value
        self.piece = Held(total.reshape(nz, total.shape[0] // nz, -1))
        return self.piece


def grad_kernel(lefts, starts, with_add, table_ref, *refs):
    j = pl.program_id(1)
    out = refs[-1]
    at = 0
    for (start, count), number in zip(starts, lefts):
        left_refs, right = refs[at:at + number], refs[at + number]
        at += number + 1

        @pl.when(jnp.logical_and(j >= start, j < start + count))
        def _(left_refs=left_refs, right=right):
            left = left_refs[0][...] if len(left_refs) == 1 else jnp.concatenate([r[...] for r in left_refs], axis=1)
            total = dot_tn(left, right[...])
            if with_add:
                total = total + refs[-2][...].astype(jnp.float32)
            out[...] = total.astype(out.dtype)


def grad_rows(pairs, start, stop, add=None, table=None):
    depth = pairs[0][0].shape[0]
    tile_n = 1024
    count = stop - start
    tile_m = min(512, count)
    specs, operands, lefts, starts, at = [], [], [], [], 0

    def column_map(first, begin, n):
        return lambda i, j, t: (0, first + jnp.clip(j - begin, 0, n - 1))

    for left, right, first, n in pairs:
        if table is None:
            block = start // tile_m
            specs.append(pl.BlockSpec((depth, tile_m), lambda i, j, t, block=block: (0, block + i)))
            operands.append(left)
            lefts.append(1)
        else:
            per = tile_m // TILE
            for k in range(per):
                specs.append(pl.BlockSpec((depth, TILE), lambda i, j, t, k=k, per=per: (0, t[start // TILE + i * per + k])))
                operands.append(left)
            lefts.append(per)
        specs.append(pl.BlockSpec((depth, tile_n), column_map(first, at, n)))
        operands.append(right)
        starts.append((at, n))
        at += n
    if add is not None:
        base = add[1] // tile_m
        specs.append(pl.BlockSpec((tile_m, tile_n), lambda i, j, t: (base + i, j)))
        operands.append(add[0])
    width = at * tile_n
    return pl.pallas_call(
        functools.partial(grad_kernel, lefts, starts, add is not None),
        grid_spec=pltpu.PrefetchScalarGridSpec(
            num_scalar_prefetch=1,
            grid=(count // tile_m, at),
            in_specs=specs,
            out_specs=pl.BlockSpec((tile_m, tile_n), lambda i, j, t: (i, j)),
        ),
        out_shape=jax.ShapeDtypeStruct((count, width), jnp.bfloat16),
        compiler_params=pltpu.CompilerParams(vmem_limit_bytes=60 << 20),
        cost_estimate=BRIEF,
        name="grad_rows",
    )(jnp.zeros((1,), jnp.int32) if table is None else table, *operands)


def project(x, gain, w_qkv):
    normed = (x * inv_rms(x) * gain).astype(jnp.bfloat16)
    return normed, matmul_rows(normed, w_qkv).astype(jnp.bfloat16)


def widen(attended, gain, w_inner):
    normed_mlp = (attended * inv_rms(attended) * gain).astype(jnp.bfloat16)
    return (normed_mlp,) + gelu_pair(matmul_rows(normed_mlp, w_inner))


def backward(plan, grad_out, layers, pos, bias, blk, table, output_half):
    low, f32 = jnp.bfloat16, jnp.float32
    previous = None
    results, diags = [], []
    for weights, saved, orders in layers:
        attn_gain, w_qkv, w_output, mlp_gain, w_inner, w_outer = weights
        x, queries, keys, values, context, log_total, attended, hidden, slope, left_m, left_c, n_qk, n_v = saved
        width = x.shape[1]
        grad_low = grad_out.astype(low)
        wide = hidden.shape[1]
        blocks = table[orders[1]]

        def outer_rows(a, b, add, hidden=hidden, grad_low=grad_low, blocks=blocks, wide=wide):
            if wide // blocks.shape[0] == TILE:
                return grad_rows([(hidden, grad_low, 0, 1)], a, b, add, blocks)
            rows = plan.take_blocks(matmul_left(hidden, grad_low).astype(low), blocks)[a:b]
            return rows if add is None else add_low(rows, add[0][add[1]:add[1] + b - a])

        def rows_of(*pairs):
            return lambda a, b, add: grad_rows(pairs, a, b, add)

        outer = Chain(plan, outer_rows, orders[1], wide)
        leaving = Held(output_half)
        late = [previous.outer.side, previous.inner.side] if previous else [leaving]
        grad_out = tie(grad_out, outer.one(), *late)
        outer.send_one()
        if not previous:
            arrived = Held(plan.exchange(leaving.value, "s"))
        grad_pre, grad_attended, attn_low, grad_mlp_gain = mlp_back(grad_out, attended, mlp_gain, w_outer, w_inner, slope)
        late = [previous.qk.far, previous.ov.far] if previous else [arrived]
        grad_pre = tie(grad_pre, outer.other, *late)
        inner = Chain(plan, rows_of((left_m, grad_pre, 0, wide // 1024)), orders[0], width)
        late = []
        if previous:
            late = [part for c in (previous.qk, previous.ov) for part in (c.near(), c.three())]
            late += [previous.outer.close(), previous.inner.close()]
        grad_pre = tie(grad_pre, outer.two(), inner.one(), *late)
        outer.send_two()
        inner.send_one()
        if previous:
            previous.qk.send_three()
            previous.ov.send_three()
            previous.sum_mlp(plan)
        attn_low = tie(attn_low, inner.other)
        attn_low = tie(attn_low, inner.two())
        inner.send_two()
        grad_context = matmul_back(attn_low, w_output).astype(low)
        ready = [outer.near(), inner.near()]
        late = [previous.qk.side, previous.ov.side] if previous else []
        grad_context = tie(grad_context, *ready, *late)
        if previous:
            grad_context = tie(grad_context, previous.qk.close(), previous.ov.close())
            previous.sum_attn(plan)
        grad_query, dk, dv, diag = attn_bwd(pos, queries, grad_context, context, log_total, keys, values, bias, blk, 0, 1)
        late = [previous.mlp_sum] if previous else []
        last = tie(dv[-1], outer.far, inner.far, *late)
        grad_k = plan.reduce_keys(dk).astype(low)
        grad_v = plan.reduce_keys(list(dv[:-1]) + [last]).astype(low)
        k_held = Held(grad_k)
        grad_v = tie(grad_v, k_held, outer.three(), inner.three())
        grad_k = k_held.value
        outer.send_three()
        inner.send_three()
        tiles = width // 1024
        qk = Chain(plan, rows_of((n_qk, grad_query, 0, tiles), (n_qk, grad_k, 0, tiles)), orders[2], width)
        ov = Chain(plan, rows_of((left_c, attn_low, 0, tiles), (n_v, grad_v, 0, tiles)), orders[3], width)
        grad_v = tie(grad_v, qk.one(), ov.one())
        qk.send_one()
        ov.send_one()
        grad_out, grad_attn_gain = project_back(grad_attended, x, attn_gain, grad_query, grad_k, grad_v, w_qkv)
        grad_out = tie(grad_out, qk.other, ov.other)
        grad_out = tie(grad_out, qk.two(), ov.two(), outer.close_by, inner.close_by)
        qk.send_two()
        ov.send_two()
        previous = LayerSums(outer, inner, qk, ov, grad_attn_gain, grad_mlp_gain, width)
        results.append(previous)
        diags.append(diag)
    outer.close()
    inner.close()
    previous.sum_mlp(plan)
    grad_out = tie(grad_out, qk.far, ov.far, qk.near(), ov.near())
    grad_out = tie(grad_out, qk.three(), ov.three())
    qk.send_three()
    ov.send_three()
    qk.close()
    qk.piece.value = tie(qk.piece.value, ov.close(), previous.mlp_sum, results[0].attn_sum)
    previous.sum_attn(plan)
    return grad_out, results, diags, arrived.value


class LayerSums:
    def __init__(self, outer, inner, qk, ov, grad_attn_gain, grad_mlp_gain, width):
        self.outer, self.inner, self.qk, self.ov = outer, inner, qk, ov
        self.attn_gain, self.mlp_gain, self.width = grad_attn_gain, grad_mlp_gain, width

    def sum_mlp(self, plan):
        w = self.width
        inner, outer = self.inner.piece.value, self.outer.piece.value
        self.runs, self.depth = inner.shape[2] // w, inner.shape[1]
        stacked = [inner[:, :, i * w:(i + 1) * w] for i in range(self.runs)]
        self.mlp_sum = Held(plan.sum_z(jnp.concatenate(stacked + [outer], axis=1)))

    def sum_attn(self, plan):
        self.attn_sum = Held(plan.sum_z(jnp.concatenate([c.piece.value for c in (self.qk, self.ov)], axis=2)))

    def grads(self):
        w = self.width
        f32 = jnp.float32
        query, key, output, value = [self.attn_sum.value[:, i * w:(i + 1) * w].astype(f32) for i in range(4)]
        both = self.mlp_sum.value.astype(f32)
        d = self.depth
        inner = jnp.concatenate([both[i * d:(i + 1) * d] for i in range(self.runs)], axis=1)
        return [self.attn_gain, query, key, value, output, self.mlp_gain, inner, both[self.runs * d:]]


def body(sizes, inputs, cotangent, lengths, bucket_ids, *params):
    plan = Plan(sizes)
    one, bias_table, two = params[:8], params[8], params[9:]
    blk, width = inputs.shape[1], inputs.shape[2]
    f32, low = jnp.float32, jnp.bfloat16
    gains = jnp.stack([one[0], one[5], two[0], two[5]], axis=1)
    rows = gains.shape[0]
    table_column = jnp.pad(bias_table, (0, rows - bias_table.shape[0]))[:, None] if bias_table.shape[0] < rows else bias_table[:rows, None]
    small = jnp.pad(jnp.concatenate([gains, table_column], axis=1), ((0, 0), (0, TILE - 5)))
    everywhere = plan.everywhere

    length = lax.dynamic_index_in_dim(lengths, plan.s, 0, keepdims=False)
    pos = plan.positions(length, blk)
    row = jnp.arange(blk, dtype=jnp.int32)
    row_pos = jnp.concatenate([row + pos[1] * TILE, row + pos[2] * TILE])
    row_valid = (row_pos < length).astype(f32)[:, None]

    xy, yx = ("x", "y"), ("y", "x")
    perms = {o: plan.permutation(o, width) for o in (xy, yx)}

    def permuted(rows_low, order):
        return Held(matmul_rows(rows_low, perms[order]).astype(low))

    shards = (
        jnp.concatenate([one[1], one[2], one[3], one[4], small], axis=1),
        one[6],
        one[7],
        jnp.concatenate([two[1], two[2], two[3], two[4]], axis=1),
        two[6],
        two[7],
    )
    attn_1, inner_1, outer_1, attn_2, inner_2, outer_2 = [Fetch(plan, piece) for piece in shards]
    attn_1.start()
    x = plan.to_sequences(inputs)
    cotangent = plan.to_sequences(cotangent)
    x = tie(x, inner_1.shard)
    inner_1.start()
    held = Held(cotangent)
    x = tie(x, held)
    cotangent = held.value
    x = attn_1.a(x, outer_1)
    x = attn_1.b(x)
    x = inner_1.a(x, attn_2)
    x, first = attn_1.c(x)
    picks = jnp.eye(8, TILE, dtype=low)
    smalls = matmul_back(picks, first[:, 4 * width:])
    gain = smalls[:4]
    whole_table = smalls[4].reshape(-1, rows)[:, :bias_table.shape[0]].reshape(-1)
    heads = width // DK
    buckets = whole_table.shape[0] // heads
    reversed_ids = jnp.concatenate([jnp.full((1,), -1, jnp.int32), bucket_ids[::-1]])
    indicator = (reversed_ids[None, :] == jnp.arange(buckets, dtype=jnp.int32)[:, None]).astype(low)
    vector = Held(matmul_rows(whole_table.reshape(heads, buckets).astype(low), indicator))
    x_one = x.astype(f32)
    normed_one, qkv = project(x_one, gain[0:1], first[:, :3 * width])
    qkv = inner_1.b(qkv)
    qkv = outer_1.a(qkv, inner_2)
    kv = plan.gather_keys(qkv[:, width:])
    qkv = tie(qkv, vector)
    bias = Held(toeplitz_tiles(vector.value))
    qkv = tie(qkv, bias)
    bias = bias.value
    queries_one = qkv[:, :width]
    keys_one, values_one = [p[:, :width] for p in kv], [p[:, width:] for p in kv]
    context_one, log_one = attn_fwd(pos, queries_one, keys_one, values_one, bias, blk)
    n_yx_one, n_xy_one = permuted(normed_one, yx), permuted(normed_one, xy)
    context_one, w_inner_one = inner_1.c(context_one, lambda main: attn_2.a(outer_1.b(main, n_xy_one), outer_2), [n_yx_one])
    c_one = permuted(context_one, xy)
    attended_one = x_one + matmul_rows(context_one, first[:, 3 * width:4 * width])
    normed_mlp_one, hidden_one, slope_one = widen(attended_one, gain[1:2], w_inner_one)
    slope_one = Held(slope_one)
    hidden_one = tie(hidden_one, slope_one)
    slope_one = slope_one.value
    m_one = permuted(normed_mlp_one, xy)
    hidden_one, w_outer_one = outer_1.c(hidden_one, None, [c_one])
    hidden_one = attn_2.b(hidden_one, m_one)
    hidden_one = inner_2.a(hidden_one)
    x_two = attended_one + matmul_rows(hidden_one, w_outer_one)
    x_two, third = attn_2.c(x_two)
    normed_two, qkv = project(x_two, gain[2:3], third[:, :3 * width])
    qkv = inner_2.b(qkv)
    qkv = outer_2.a(qkv)
    kv = plan.gather_keys(qkv[:, width:])
    queries_two = qkv[:, :width]
    keys_two, values_two = [p[:, :width] for p in kv], [p[:, width:] for p in kv]
    context_two, log_two = attn_fwd(pos, queries_two, keys_two, values_two, bias, blk)
    n_yx_two, n_xy_two = permuted(normed_two, yx), permuted(normed_two, xy)
    context_two, w_inner_two = inner_2.c(context_two, None, [n_yx_two])
    context_two = outer_2.b(context_two, n_xy_two)
    c_two = permuted(context_two, xy)
    attended_two = x_two + matmul_rows(context_two, third[:, 3 * width:])
    normed_mlp_two, hidden_two, slope_two = widen(attended_two, gain[3:4], w_inner_two)
    slope_two = Held(slope_two)
    hidden_two = tie(hidden_two, slope_two)
    slope_two = slope_two.value
    hidden_two, w_outer_two = outer_2.c(hidden_two, None, [c_two])
    m_two = permuted(normed_mlp_two, xy)
    final = attended_two + matmul_rows(hidden_two, w_outer_two)
    output_rows = (final * row_valid).astype(low)
    grad_out = cotangent.astype(f32) * row_valid

    weights_one = (gain[0:1], first, first[:, 3 * width:4 * width], gain[1:2], w_inner_one, w_outer_one)
    weights_two = (gain[2:3], third, third[:, 3 * width:], gain[3:4], w_inner_two, w_outer_two)
    saved_one = (x, queries_one, keys_one, values_one, context_one, log_one, attended_one, hidden_one, slope_one, m_one.value, c_one.value, n_yx_one.value, n_xy_one.value)
    saved_two = (x_two, queries_two, keys_two, values_two, context_two, log_two, attended_two, hidden_two, slope_two, m_two.value, c_two.value, n_yx_two.value, n_xy_two.value)

    depth = one[7].shape[0]
    step = TILE if depth % TILE == 0 else depth
    blocks = jnp.arange(hidden_one.shape[1] // step, dtype=jnp.int32)
    per = depth // step
    table = {o: plan.block_of(o, blocks // per) * per + blocks % per for o in (xy, yx)}
    layers = [(weights_two, saved_two, (xy, yx, yx, xy)), (weights_one, saved_one, (xy, yx, yx, xy))]
    grad_state, sums, diags, arrived = backward(plan, grad_out, layers, pos, bias, blk, table, output_rows[blk:])
    output = plan.in_order(output_rows[:blk], arrived)
    grads_two, grads_one = sums[0].grads(), sums[1].grads()
    input_grad = plan.from_sequences(grad_state.astype(low))

    grad_table = lax.dot_general(diags[0] + diags[1], indicator.astype(f32), (((1,), (1,)), ((), ())), precision=HIGH_PRECISION)
    vectors = jnp.concatenate([grads_one[0][0], grads_one[5][0], grads_two[0][0], grads_two[5][0], grad_table.reshape(-1)])
    held = Held(vectors)
    grad_state = tie(grad_state, held)
    vectors = plan.sum_vector(held.value)
    device = ((plan.z * plan.ny + plan.y) * plan.nx + plan.x) * 2 + plan.core

    def share(start, count):
        return lax.dynamic_slice_in_dim(vectors, start + device * count, count, 0)

    gain_grads = [share(i * width, rows) for i in range(4)]
    table_grad = share(4 * width, bias_table.shape[0])
    return (
        output,
        input_grad,
        gain_grads[0],
        *grads_one[1:5],
        gain_grads[1],
        *grads_one[6:],
        table_grad,
        gain_grads[2],
        *grads_two[1:5],
        gain_grads[3],
        *grads_two[6:],
    )


def solution(mesh):
    dp, cp = mesh.shape["dp"], mesh.shape["cp"]
    nx = cp // 2
    ny = nx if dp % nx == 0 else 1

    def run(inputs, *rest):
        ns = inputs.shape[0] // dp
        assert ns == 2 and nx % ns == 0
        sizes = (dp // ny, ny, ns, nx // ns)
        finer = Mesh(mesh.devices.reshape(*sizes, 2), ("z", "y", "s", "q", "core"))
        dpn, cpn = ("z", "y"), ("s", "q", "core")
        tokens = P(dpn, cpn, None)
        vector, matrix = P(dpn + cpn), P(dpn + cpn, None)
        layer = (vector, matrix, matrix, matrix, matrix, vector, matrix, matrix)
        return jax.shard_map(
            functools.partial(body, sizes),
            mesh=finer,
            in_specs=(tokens, tokens, P(dpn), P()) + layer + (vector,) + layer,
            out_specs=(tokens, tokens) + layer + (vector,) + layer,
            check_vma=False,
        )(inputs, *rest)

    return run
```
